32 devices in a mesh: seq: 8 (over z, y), tensor: 4 (over x, core).
Axes of the slice: x: 2, y: 2, z: 4, core: 2. Of those that a mesh axis runs over, the one named last changes fastest.
Arguments:
- stream: bfloat16 [8192, 768], P('seq'), may hold values from -6 to 6
- cotangent: bfloat16 [8192, 768], P('seq'), may hold values from -6 to 6
- boundary: int32 [8192], P('seq'), may hold values from 0 to 1, as said below
- counts: int32 [2, 4], replicated, may hold values from 0 to 256, as said below
- attend_gain: float32 [768], replicated, may hold values from 0.25 to 1.75
- attend_input: bfloat16 [768, 3, 768], P(None, None, 'tensor'), may hold values from -0.21875 to 0.21875
- attend_output: bfloat16 [768, 768], P('tensor'), may hold values from -3.5 to 3.5
- byte_gain: float32 [768], replicated, may hold values from 0.25 to 1.75
- byte_up: bfloat16 [768, 3072], P(None, 'tensor'), may hold values from -0.21875 to 0.21875
- byte_down: bfloat16 [3072, 768], P('tensor'), may hold values from -0.109375 to 0.109375
- patch_gain: float32 [1536], replicated, may hold values from 0.25 to 1.75
- patch_input: bfloat16 [1536, 3, 1536], P(None, None, 'tensor'), may hold values from -0.15625 to 0.15625
- patch_output: bfloat16 [1536, 1536], P('tensor'), may hold values from -1.75 to 1.75
- dense_gain: float32 [1536], replicated, may hold values from 0.25 to 1.75
- dense_up: bfloat16 [1536, 6144], P(None, 'tensor'), may hold values from -0.15625 to 0.15625
- dense_down: bfloat16 [6144, 768], P('tensor'), may hold values from -0.078125 to 0.078125
Outputs:
- result: bfloat16 [8192, 768], P('seq')
- inflow: bfloat16 [8192, 768], P('seq')
- attendgain_grad: float32 [768], replicated
- attendinput_grad: float32 [768, 3, 768], P(None, None, 'tensor')
- attendoutput_grad: float32 [768, 768], P('tensor')
- bytegain_grad: float32 [768], replicated
- byteup_grad: float32 [768, 3072], P(None, 'tensor')
- bytedown_grad: float32 [3072, 768], P('tensor')
- patchgain_grad: float32 [1536], replicated
- patchinput_grad: float32 [1536, 3, 1536], P(None, None, 'tensor')
- patchoutput_grad: float32 [1536, 1536], P('tensor')
- densegain_grad: float32 [1536], replicated
- denseup_grad: float32 [1536, 6144], P(None, 'tensor')
- densedown_grad: float32 [6144, 768], P('tensor')
The draws below stay inside these ranges and needn't reach their ends.
Inputs may be any that keep to these rules, and one draw needn't show every extreme that they name: `boundary`: the ones on the 1024 bytes of one device number at most 256, a number reached on some device in every draw. counts[i, j] is the number of ones of boundary on bytes (i * 4 + j) * 1024 to (i * 4 + j + 1) * 1024 - 1; all counts together sum to exactly 1024.
All inputs are finite; a program needn't handle non-finite values.
Results may differ from the reference program's by a relative error of at most 0.024.
Values may be sent and summed in bfloat16 or wider, within the bound.
A program may use at most 320 MiB of HBM per device.

```python
import jax
import jax.numpy as jnp
from jax import lax

D = 768
HL = 12
HD = 64
FL = 3072
G = 1536
HG = 24
FG = 6144
WIN = 1536
DEV_ITEM = 4
TOK_DEV = 1024
TOKENS = 8192
ITEMS = 2
ITEM_LEN = 4096
ITEM_CAP = 1024


def boundary_layout(key):
    half_items = ITEMS // 2
    capacity = TOK_DEV // 4
    order_items = jax.random.permutation(jax.random.fold_in(key, 11), ITEMS)
    spread_draw = jax.random.randint(jax.random.fold_in(key, 12), (half_items * DEV_ITEM,), 0, capacity // 4)
    zero_index = jax.random.randint(jax.random.fold_in(key, 13), (), 0, half_items * DEV_ITEM)
    spread_flat = jnp.where(jnp.arange(half_items * DEV_ITEM) == zero_index, 0, spread_draw)
    spread_pairs = spread_flat.reshape(half_items, DEV_ITEM)
    prose_item = order_items >= half_items
    pair_index = jnp.where(prose_item, order_items - half_items, order_items)
    chosen = jnp.take(spread_pairs, pair_index, axis=0)
    layout = jnp.where(prose_item[:, None], capacity - chosen, chosen)
    return layout.astype(jnp.int32)


def shuffle_positions(device_key):
    return jax.random.permutation(device_key, TOK_DEV)


def draw_boundary(key, part):
    layout = boundary_layout(key)
    device_keys = jax.random.split(jax.random.fold_in(key, 14), ITEMS * DEV_ITEM)
    orders = jax.vmap(shuffle_positions)(device_keys)
    marks = (orders < layout.reshape(-1)[:, None]).astype(jnp.int32)
    return marks.reshape(-1)


def draw_counts(key, part):
    return boundary_layout(key)


def shard_levels(rng, dims, cuts, low, high):
    factor_of = 1.0
    for position, blocks in cuts:
        steps = jax.random.uniform(jax.random.fold_in(jax.random.fold_in(rng, 6), position), (blocks,), jnp.float32, low / len(cuts), high / len(cuts))
        factor_of = factor_of * jnp.repeat(jnp.exp(steps), dims[position] // blocks).reshape((-1,) + (1,) * (len(dims) - 1 - position))
    return factor_of


def scatter_about(key, dims, spread, most, cuts=(), kind=jnp.bfloat16):
    entries = jax.random.normal(key, dims, jnp.float32) * spread
    if len(cuts) > 0:
        entries = shard_levels(key, dims, cuts, -0.22, 0.18) * entries
    return jnp.clip(entries, min=-most, max=most).astype(kind)


def setup_inputs(seed: int = 0) -> dict:
    splits = jax.random.split(jax.random.key(seed), 17)
    stream = scatter_about(splits[0], (TOKENS, D), 1.0, 6.0, ((0, 8),))
    cotangent = scatter_about(splits[1], (TOKENS, D), 1.0, 6.0, ((0, 8),))
    boundary = draw_boundary(jax.random.fold_in(splits[16], 71), 0)
    counts = draw_counts(jax.random.fold_in(splits[16], 71), 0)
    attend_gain = jnp.clip(1.0 + 0.15 * jax.random.normal(splits[4], (D,), jnp.float32), 0.25, 1.75)
    attend_input = scatter_about(splits[5], (D, 3, HL * HD), D ** -0.5, 0.21875, ((2, 4),))
    attend_output = scatter_about(splits[6], (HL * HD, D), (HL * HD // 256) ** -0.5, 3.5, ((0, 4),))
    byte_gain = jnp.clip(1.0 + 0.15 * jax.random.normal(splits[7], (D,), jnp.float32), 0.25, 1.75)
    byte_up = scatter_about(splits[8], (D, FL), D ** -0.5, 0.21875, ((1, 4),))
    byte_down = scatter_about(splits[9], (FL, D), FL ** -0.5, 0.109375, ((0, 4),))
    patch_gain = jnp.clip(1.0 + 0.15 * jax.random.normal(splits[10], (G,), jnp.float32), 0.25, 1.75)
    patch_input = scatter_about(splits[11], (G, 3, HG * HD), G ** -0.5, 0.15625, ((2, 4),))
    patch_output = scatter_about(splits[12], (HG * HD, G), (HG * HD // 128) ** -0.5, 1.75, ((0, 4),))
    dense_gain = jnp.clip(1.0 + 0.15 * jax.random.normal(splits[13], (G,), jnp.float32), 0.25, 1.75)
    dense_up = scatter_about(splits[14], (G, FG), G ** -0.5, 0.15625, ((1, 4),))
    dense_down = scatter_about(splits[15], (FG, D), FG ** -0.5, 0.078125, ((0, 4),))
    return dict(stream=stream, cotangent=cotangent, boundary=boundary, counts=counts, attend_gain=attend_gain, attend_input=attend_input, attend_output=attend_output, byte_gain=byte_gain, byte_up=byte_up, byte_down=byte_down, patch_gain=patch_gain, patch_input=patch_input, patch_output=patch_output, dense_gain=dense_gain, dense_up=dense_up, dense_down=dense_down)


@jax.custom_vjp
def low(v):
    return lax.optimization_barrier(v.astype(jnp.bfloat16)).astype(jnp.float32)

@jax.custom_vjp
def low_back(v):
    return v

def low_keep(v):
    return (low(v), None)

def low_pass(kept, grad):
    return (grad,)

def back_keep(v):
    return (v, None)

def back_low(kept, grad):
    return (low(grad),)
low.defvjp(low_keep, low_pass)
low_back.defvjp(back_keep, back_low)
EPSILON = 1e-06
NEGATIVE = -1e+30
HIGHEST = lax.Precision.HIGHEST

def matmul(left_side, right_side):
    return jnp.dot(left_side, right_side, precision=HIGHEST, preferred_element_type=jnp.float32)

def rms_scale(values, scaling):
    return values * lax.rsqrt(lax.optimization_barrier(jnp.mean(values * values, axis=-1, keepdims=True)) + EPSILON) * scaling

def gelu_tanh(values):
    return jax.nn.gelu(values, approximate=True)

def masked_softmax(scores, allowed):
    return jax.nn.softmax(jnp.where(allowed, scores, NEGATIVE), axis=-1)

def window_attention(queries, keys_all, values_all):
    block_rows = min(512, TOK_DEV)
    margin = WIN - 1
    score_scale = HD ** (-0.5)
    keys_pad = jnp.concatenate([jnp.zeros((margin, HL, HD), jnp.float32), keys_all], axis=0)
    values_pad = jnp.concatenate([jnp.zeros((margin, HL, HD), jnp.float32), values_all], axis=0)

    def one_block(block_start):
        query_rows = lax.dynamic_slice_in_dim(queries, block_start, block_rows, 0)
        key_rows = lax.dynamic_slice_in_dim(keys_pad, block_start, block_rows + margin, 0)
        value_rows = lax.dynamic_slice_in_dim(values_pad, block_start, block_rows + margin, 0)
        query_pos = block_start + jnp.arange(block_rows, dtype=jnp.int32)
        key_pos = block_start - margin + jnp.arange(block_rows + margin, dtype=jnp.int32)
        distance = query_pos[:, None] - key_pos[None, :]
        allowed = (distance >= 0) & (distance < WIN) & (key_pos[None, :] >= 0)
        scores = low_back(score_scale * jnp.einsum('qhe,khe->hqk', query_rows, key_rows, precision=HIGHEST))
        soft_weights = masked_softmax(scores, allowed[None])
        return jnp.einsum('hqk,khe->qhe', low(soft_weights), value_rows, precision=HIGHEST)
    starts = (jnp.arange(TOKENS // block_rows) * block_rows).astype(jnp.int32)
    outputs = lax.map(jax.checkpoint(one_block), starts)
    return outputs.reshape(TOKENS, HL * HD)

def patch_attention(queries, keys_all, values_all, valid_rows):
    score_scale = HD ** (-0.5)
    rank_index = jnp.arange(ITEM_CAP)
    allowed = valid_rows[None, :] & (rank_index[None, :] <= rank_index[:, None])
    scores = low_back(score_scale * jnp.einsum('qhe,khe->hqk', queries, keys_all, precision=HIGHEST))
    soft_weights = masked_softmax(scores, allowed[None])
    mixed_rows = jnp.einsum('hqk,khe->qhe', low(soft_weights), values_all, precision=HIGHEST)
    return mixed_rows.reshape(ITEM_CAP, HG * HD)

def byte_forward(stream_all, weights):
    attend_gain, attend_input, attend_output, byte_gain, byte_up, byte_down = weights[:6]
    normed = low(rms_scale(stream_all, attend_gain))
    projected = low(low_back(matmul(normed, attend_input.reshape(D, 3 * HL * HD))))
    queries = projected[:, :HL * HD].reshape(TOKENS, HL, HD)
    keys_all = projected[:, HL * HD:2 * HL * HD].reshape(TOKENS, HL, HD)
    values_all = projected[:, 2 * HL * HD:].reshape(TOKENS, HL, HD)
    mixed_heads = low(low_back(window_attention(queries, keys_all, values_all)))
    after_attend = stream_all + low_back(matmul(mixed_heads, attend_output))
    normed_two = low(rms_scale(after_attend, byte_gain))
    gate_pre = low_back(matmul(normed_two, byte_up))
    activated = low(gelu_tanh(gate_pre))
    return after_attend + low_back(matmul(activated, byte_down))

def patch_delta(after_feed, boundary_item, count_item, weights):
    patch_gain, patch_input, patch_output, dense_gain, dense_up, dense_down = weights[6:]
    rank_index = (jnp.cumsum(boundary_item) - 1).astype(jnp.int32)
    target = jnp.where(boundary_item == 1, rank_index, ITEM_CAP).astype(jnp.int32)
    gathered = jnp.zeros((ITEM_CAP + 1, D), jnp.float32).at[target].set(after_feed)[:ITEM_CAP]
    byte_rows = low(low_back(gathered))
    patch_rows = jnp.concatenate([byte_rows, jnp.zeros((ITEM_CAP, G - D), jnp.float32)], axis=1)
    valid_rows = jnp.arange(ITEM_CAP) < count_item
    normed_three = low(rms_scale(patch_rows, patch_gain))
    patch_projected = low(low_back(matmul(normed_three, patch_input.reshape(G, 3 * HG * HD))))
    patch_queries = patch_projected[:, :HG * HD].reshape(ITEM_CAP, HG, HD)
    patch_keys = patch_projected[:, HG * HD:2 * HG * HD].reshape(ITEM_CAP, HG, HD)
    patch_values = patch_projected[:, 2 * HG * HD:].reshape(ITEM_CAP, HG, HD)
    mixed_patch = low(low_back(patch_attention(patch_queries, patch_keys, patch_values, valid_rows)))
    patch_branch = low_back(matmul(mixed_patch, patch_output))
    after_patch = patch_rows + patch_branch
    normed_four = low(rms_scale(after_patch, dense_gain))
    dense_pre = low_back(matmul(normed_four, dense_up))
    dense_act = low(gelu_tanh(dense_pre))
    dense_out = low_back(matmul(dense_act, dense_down))
    delta_rows = low(patch_branch[:, :D] + dense_out)
    padded_delta = jnp.concatenate([delta_rows, jnp.zeros((1, D), jnp.float32)], axis=0)
    return padded_delta[target]

def reference(stream, cotangent, boundary, counts, attend_gain, attend_input, attend_output, byte_gain, byte_up, byte_down, patch_gain, patch_input, patch_output, dense_gain, dense_up, dense_down):
    weights = tuple((member.astype(jnp.float32) for member in (attend_gain, attend_input, attend_output, byte_gain, byte_up, byte_down, patch_gain, patch_input, patch_output, dense_gain, dense_up, dense_down)))
    boundary_items = boundary.reshape(ITEMS, ITEM_LEN).astype(jnp.int32)
    item_counts = lax.optimization_barrier(jnp.sum(counts, axis=1)).astype(jnp.int32)

    def forward(stream_value, weight_values):
        after_feed = byte_forward(stream_value, weight_values)
        feed_items = after_feed.reshape(ITEMS, ITEM_LEN, D)

        def one_item(inputs):
            feed_item, boundary_item, count_item = inputs
            return patch_delta(feed_item, boundary_item, count_item, weight_values)
        deltas = lax.map(jax.checkpoint(one_item), (feed_items, boundary_items, item_counts))
        return after_feed + deltas.reshape(TOKENS, D)
    output, pullback = jax.vjp(forward, stream.astype(jnp.float32), weights)
    stream_grad, totals = pullback(cotangent.astype(jnp.float32))
    return (output.astype(jnp.bfloat16), stream_grad.astype(jnp.bfloat16), totals[0], totals[1], totals[2], totals[3], totals[4], totals[5], totals[6], totals[7], totals[8], totals[9], totals[10], totals[11])
```

```python
import functools

import jax
import jax.numpy as jnp
from jax import lax
from jax.experimental import pallas as pl
from jax.experimental.pallas import tpu as pltpu
from jax.sharding import PartitionSpec as P

HD = 64
WIN = 1536
DEV_ITEM = 4

EPSILON = 1e-06
NEGATIVE = -1e30
SCORE_SCALE = HD ** (-0.5)
WIDE_TYPE = jnp.float32
NARROW_TYPE = jnp.bfloat16
VMEM_BYTES = 48 << 20


def from_behind(value, axis, steps):
    count = lax.axis_size(axis)
    initial, last = (max(0, -steps), min(count, count - steps))
    return lax.ppermute(value, axis, [(source, source + steps) for source in range(initial, last)])


def rms_scale(values, scaling):
    return values * lax.rsqrt(jnp.mean(values * values, axis=-1, keepdims=True) + EPSILON) * scaling


def gelu_tanh(values):
    return jax.nn.gelu(values, approximate=True)


def norm_back(values, scaling, upstream):
    unused, pullback = jax.vjp(rms_scale, values, scaling)
    return pullback(upstream)


def gelu_back(values, upstream):
    unused, pullback = jax.vjp(gelu_tanh, values)
    return pullback(upstream)[0]


def contract(left_side, right_side, left_axis, right_axis):
    return lax.dot_general(
        left_side,
        right_side,
        (((left_axis,), (right_axis,)), ((), ())),
        preferred_element_type=WIDE_TYPE,
    )


def product(left_side, right_side):
    return contract(left_side, right_side, 1, 0)


def times_transposed(left_side, right_side):
    return contract(left_side, right_side, 1, 1)


def transposed_times(left_side, right_side):
    return contract(left_side, right_side, 0, 0)


def wide(values):
    return values.astype(WIDE_TYPE)


def narrow(values):
    return values.astype(NARROW_TYPE)


def tensor_sum(pieces):
    return lax.psum(narrow(pieces), "tensor")


def seq_gather(block):
    gathered = lax.all_gather(block, "seq", axis=0, tiled=True)
    return gathered


def allowed_pairs(low_row, first_key, span, first_query, query_rows):
    key_pos = first_key + lax.broadcasted_iota(jnp.int32, (span, query_rows), 0)
    query_pos = first_query + lax.broadcasted_iota(jnp.int32, (span, query_rows), 1)
    return (key_pos >= low_row) & (key_pos <= query_pos)


def forward_body(heads, query_rows, span, offset, low, queries, keys, values, mixed, log_total):
    block = pl.program_id(1)
    start = jnp.maximum(block * query_rows + query_rows + offset - span, 0)
    start = pl.multiple_of(start, 128)
    allowed = allowed_pairs(low[...], start, span, block * query_rows + offset, query_rows)
    rows = pl.ds(start, span)
    for head in range(heads):
        cols = slice(head * HD, (head + 1) * HD)
        scores = contract(keys[rows, cols], queries[:, cols] * SCORE_SCALE, 1, 1)
        scores = jnp.where(allowed, scores, NEGATIVE)
        top = jnp.max(scores, axis=0, keepdims=True)
        raised = jnp.exp(scores - top)
        total = jnp.sum(raised, axis=0, keepdims=True)
        weights = narrow(raised * (1.0 / total))
        mixed[:, cols] = narrow(contract(values[rows, cols], weights, 0, 0).T)
        log_total[0, head : head + 1, :] = top + jnp.log(total)


def backward_body(
    heads,
    query_rows,
    span,
    offset,
    low,
    log_total,
    queries,
    out_grads,
    keys,
    values,
    query_grads,
    key_grads,
    value_grads,
    key_sum,
    value_sum,
):
    block = pl.program_id(1)

    @pl.when(block == 0)
    def clear():
        key_sum[...] = jnp.zeros_like(key_sum)
        value_sum[...] = jnp.zeros_like(value_sum)

    start = jnp.maximum(block * query_rows + query_rows + offset - span, 0)
    start = pl.multiple_of(start, 128)
    allowed = allowed_pairs(low[...], start, span, block * query_rows + offset, query_rows)
    rows = pl.ds(start, span)
    for head in range(heads):
        cols = slice(head * HD, (head + 1) * HD)
        query = queries[:, cols] * SCORE_SCALE
        out_grad = out_grads[:, cols]
        key = keys[rows, cols]
        scores = contract(key, query, 1, 1)
        weights = jnp.where(allowed, jnp.exp(scores - log_total[0, head : head + 1, :]), 0.0)
        weight_grad = contract(values[rows, cols], out_grad, 1, 1)
        inner = jnp.sum(weights * weight_grad, axis=0, keepdims=True)
        score_grad = narrow(weights * (weight_grad - inner))
        query_grads[:, cols] = narrow(contract(key, score_grad, 0, 0).T * SCORE_SCALE)
        key_sum[rows, cols] += contract(score_grad, query, 1, 0)
        value_sum[rows, cols] += contract(narrow(weights), out_grad, 1, 0)

    @pl.when(block == pl.num_programs(1) - 1)
    def finish():
        key_grads[...] = narrow(key_sum[...])
        value_grads[...] = narrow(value_sum[...])


def attend_sizes(queries, keys, span, query_rows):
    rows, cols = queries.shape
    extent = keys.shape[0]
    group_cols = 128 if cols % 128 == 0 else cols
    groups = cols // group_cols
    heads = group_cols // HD
    low_spec = pl.BlockSpec((1, query_rows), lambda g, b: (0, b))
    row_spec = pl.BlockSpec((query_rows, group_cols), lambda g, b: (b, g))
    all_spec = pl.BlockSpec((extent, group_cols), lambda g, b: (0, g))
    log_spec = pl.BlockSpec((1, heads, query_rows), lambda g, b: (g, 0, b))
    args = (heads, query_rows, span, extent - rows)
    log_shape = jax.ShapeDtypeStruct((groups, heads, rows), WIDE_TYPE)
    grid = (groups, rows // query_rows)
    flops = 2 * rows * span * cols
    return args, grid, low_spec, row_spec, all_spec, log_spec, log_shape, group_cols, flops


def attend_forward(low, queries, keys, values, span, query_rows):
    args, grid, low_spec, row_spec, all_spec, log_spec, log_shape, unused, flops = attend_sizes(
        queries, keys, span, query_rows
    )
    return pl.pallas_call(
        functools.partial(forward_body, *args),
        grid=grid,
        in_specs=[low_spec, row_spec, all_spec, all_spec],
        out_specs=[row_spec, log_spec],
        out_shape=[jax.ShapeDtypeStruct(queries.shape, NARROW_TYPE), log_shape],
        compiler_params=pltpu.CompilerParams(vmem_limit_bytes=VMEM_BYTES),
        cost_estimate=pl.CostEstimate(
            flops=16 * flops, transcendentals=flops // 128, bytes_accessed=1 << 20
        ),
        name="attend_forward",
    )(low, queries, keys, values)


def attend_backward(low, log_total, queries, out_grads, keys, values, span, query_rows):
    args, grid, low_spec, row_spec, all_spec, log_spec, unused, group_cols, flops = attend_sizes(
        queries, keys, span, query_rows
    )
    key_shape = jax.ShapeDtypeStruct(keys.shape, NARROW_TYPE)
    return pl.pallas_call(
        functools.partial(backward_body, *args),
        grid=grid,
        in_specs=[low_spec, log_spec, row_spec, row_spec, all_spec, all_spec],
        out_specs=[row_spec, all_spec, all_spec],
        out_shape=[jax.ShapeDtypeStruct(queries.shape, NARROW_TYPE), key_shape, key_shape],
        scratch_shapes=[pltpu.VMEM((keys.shape[0], group_cols), WIDE_TYPE)] * 2,
        compiler_params=pltpu.CompilerParams(vmem_limit_bytes=VMEM_BYTES),
        cost_estimate=pl.CostEstimate(
            flops=20 * flops, transcendentals=flops // 128, bytes_accessed=1 << 20
        ),
        name="attend_backward",
    )(low, log_total, queries, out_grads, keys, values)


def in_blocks(function, rows, block_rows):
    if rows <= block_rows:
        return function(0)
    starts = jnp.arange(rows // block_rows, dtype=jnp.int32) * block_rows
    return lax.map(function, starts).reshape(rows, -1)


def on_device(
    stream,
    cotangent,
    boundary,
    counts,
    attend_gain,
    attend_input,
    attend_output,
    byte_gain,
    byte_up,
    byte_down,
    patch_gain,
    patch_input,
    patch_output,
    dense_gain,
    dense_up,
    dense_down,
):
    tok_rows, width = stream.shape
    head_cols = attend_input.shape[2]
    big_width = patch_input.shape[0]
    patch_cols = patch_input.shape[2]
    item_count = counts.shape[0]
    seq_devices = lax.axis_size("seq")
    device = lax.axis_index("seq")
    capacity = tok_rows // 4
    total_rows = seq_devices * capacity // 2
    owned_rows = total_rows // seq_devices
    item_cap = DEV_ITEM * capacity
    query_rows = min(256, tok_rows)

    per_device = counts.reshape(-1)
    ends = jnp.cumsum(per_device)
    offsets = ends - per_device
    item_begin = offsets.reshape(item_count, DEV_ITEM)[:, 0]
    my_first = offsets[device]
    rank_local = jnp.cumsum(boundary) - 1
    target = jnp.where(boundary == 1, rank_local, -1)
    send_map = narrow(jnp.arange(capacity)[:, None] == target[None, :])
    rank = jnp.arange(total_rows, dtype=jnp.int32)
    rank_device = jnp.sum(rank[:, None] >= ends[None, :], axis=1)
    rank_start = jnp.sum(
        jnp.where(rank_device[:, None] == jnp.arange(seq_devices)[None, :], offsets[None, :], 0),
        axis=1,
    )
    rank_slot = rank_device * capacity + rank - rank_start
    rank_low = jnp.max(
        jnp.where(rank[:, None] >= item_begin[None, :], item_begin[None, :], 0), axis=1
    )
    rank_low = rank_low[None, :].astype(jnp.int32)
    slot_rows = seq_devices * capacity

    def compact(slots):
        block_rows = min(1024, total_rows)

        def one_block(first_row):
            places = lax.dynamic_slice_in_dim(rank_slot, first_row, block_rows, 0)
            take_map = narrow(places[:, None] == jnp.arange(slot_rows)[None, :])
            return narrow(product(take_map, slots))

        return in_blocks(one_block, total_rows, block_rows)

    def my_slots(table):
        padded = jnp.pad(table, ((0, capacity), (0, 0)))
        return lax.dynamic_slice_in_dim(padded, my_first, capacity, 0)

    def my_block(table):
        return lax.dynamic_slice_in_dim(table, device * owned_rows, owned_rows, 0)

    with jax.named_scope("cotangent_rows"):
        delta_grad = compact(seq_gather(narrow(product(send_map, cotangent))))
        delta_own = my_block(delta_grad)

    with jax.named_scope("byte_attend"):
        stream_value = wide(stream)
        normed = narrow(rms_scale(stream_value, attend_gain))
        in_matrix = attend_input.reshape(width, 3 * head_cols)
        projected = narrow(product(normed, in_matrix))
        queries = projected[:, :head_cols]
        key_value = projected[:, head_cols:]
        need_list = []
        while sum(need_list) < WIN:
            need_list.append(min(tok_rows, WIN - sum(need_list)))
        arrived_list = []
        for step, need_rows in enumerate(need_list):
            arrived_list.append(from_behind(key_value[tok_rows - need_rows :], "seq", step + 1))
        extended = jnp.concatenate(arrived_list[::-1] + [key_value], axis=0)
        keys = extended[:, :head_cols]
        values = extended[:, head_cols:]
        window_low = jnp.maximum(
            jnp.arange(tok_rows, dtype=jnp.int32) + 1, WIN - device * tok_rows
        )[None, :]
        window_span = WIN + query_rows
        mixed_heads, window_log = attend_forward(
            window_low, queries, keys, values, window_span, query_rows
        )
        all_mixed = lax.all_gather(mixed_heads, "tensor", axis=1, tiled=True)
        all_output = lax.all_gather(attend_output, "tensor", axis=0, tiled=True)
        after_attend = stream_value + product(all_mixed, all_output)

    with jax.named_scope("byte_feed"):
        normed_two = narrow(rms_scale(after_attend, byte_gain))
        gate_pre = product(normed_two, byte_up)
        activated = narrow(gelu_tanh(gate_pre))
        feed_part = narrow(product(activated, byte_down))

    with jax.named_scope("patch_rows"):
        attend_high = narrow(after_attend)
        attend_rest = narrow(after_attend - wide(attend_high))
        rows_sum = wide(tensor_sum(product(send_map, feed_part)))
        rows_here = narrow(
            product(send_map, attend_high) + product(send_map, attend_rest) + rows_sum
        )
        byte_rows = compact(seq_gather(rows_here))

    wide_pad = ((0, 0), (0, big_width - width))
    with jax.named_scope("patch_attend"):
        normed_three = narrow(rms_scale(wide(jnp.pad(byte_rows, wide_pad)), patch_gain))
        patch_matrix = patch_input.reshape(big_width, 3 * patch_cols)
        patch_projected = narrow(product(normed_three, patch_matrix))
        patch_queries = patch_projected[:, :patch_cols]
        patch_keys = patch_projected[:, patch_cols : 2 * patch_cols]
        patch_values = patch_projected[:, 2 * patch_cols :]
        patch_query_rows = min(256, total_rows)
        patch_span = min(total_rows, item_cap + patch_query_rows)
        mixed_patch, patch_log = attend_forward(
            rank_low, patch_queries, patch_keys, patch_values, patch_span, patch_query_rows
        )
        branch_own = wide(tensor_sum(product(my_block(mixed_patch), patch_output)))

    with jax.named_scope("patch_dense"):
        own_rows = wide(jnp.pad(my_block(byte_rows), wide_pad))
        after_patch = own_rows + branch_own
        normed_four = narrow(rms_scale(after_patch, dense_gain))
        all_normed = seq_gather(normed_four)
        dense_pre = product(normed_four, dense_up)
        dense_pre_grad = narrow(gelu_back(dense_pre, times_transposed(delta_own, dense_down)))
        normed_four_grad = wide(tensor_sum(times_transposed(dense_pre_grad, dense_up)))
        after_patch_grad, densegain_grad = norm_back(after_patch, dense_gain, normed_four_grad)
        branch_grad_own = narrow(after_patch_grad + wide(jnp.pad(delta_own, wide_pad)))
        branch_grad = seq_gather(branch_grad_own)

    with jax.named_scope("dense_weights"):
        block_rows = min(1024, total_rows)

        def dense_block(first_row):
            some_normed = lax.dynamic_slice_in_dim(all_normed, first_row, block_rows, 0)
            some_delta = lax.dynamic_slice_in_dim(delta_grad, first_row, block_rows, 0)
            some_pre = product(some_normed, dense_up)
            some_act = narrow(gelu_tanh(some_pre))
            some_grad = narrow(gelu_back(some_pre, times_transposed(some_delta, dense_down)))
            return (
                some_act,
                transposed_times(some_act, some_delta),
                transposed_times(some_normed, some_grad),
            )

        if total_rows == block_rows:
            dense_act, densedown_grad, denseup_grad = dense_block(0)
        else:

            def dense_step(sums, first_row):
                some_act, down_part, up_part = dense_block(first_row)
                return (sums[0] + down_part, sums[1] + up_part), some_act

            starts = jnp.arange(total_rows // block_rows, dtype=jnp.int32) * block_rows
            initial = (jnp.zeros(dense_down.shape), jnp.zeros(dense_up.shape))
            (densedown_grad, denseup_grad), dense_act = lax.scan(dense_step, initial, starts)
            dense_act = dense_act.reshape(total_rows, -1)

    with jax.named_scope("result"):
        delta_part = product(my_slots(mixed_patch), patch_output[:, :width])
        delta_part = narrow(delta_part + product(my_slots(dense_act), dense_down))
        result_part = wide(feed_part) + transposed_times(send_map, delta_part)
        result = narrow(after_attend + wide(tensor_sum(result_part)))

    with jax.named_scope("patch_attend_back"):
        patchoutput_grad = transposed_times(mixed_patch, branch_grad)
        mixed_patch_grad = narrow(times_transposed(branch_grad, patch_output))
        patch_projected_grad = jnp.concatenate(
            attend_backward(
                rank_low,
                patch_log,
                patch_queries,
                mixed_patch_grad,
                patch_keys,
                patch_values,
                patch_span,
                patch_query_rows,
            ),
            axis=1,
        )
        patchinput_grad = transposed_times(normed_three, patch_projected_grad)
        patchinput_grad = patchinput_grad.reshape(big_width, 3, patch_cols)
        normed_three_grad = wide(
            tensor_sum(times_transposed(my_slots(patch_projected_grad), patch_matrix))
        )
        patch_norm_grad, patchgain_grad = norm_back(
            wide(jnp.pad(rows_here, wide_pad)), patch_gain, normed_three_grad
        )
        rows_grad = narrow(wide(my_slots(branch_grad[:, :width])) + patch_norm_grad[:, :width])

    with jax.named_scope("byte_feed_back"):
        feed_grad = narrow(
            jnp.where(
                boundary[:, None] == 1,
                transposed_times(send_map, rows_grad),
                wide(cotangent),
            )
        )
        activated_grad = times_transposed(feed_grad, byte_down)
        gate_grad = narrow(gelu_back(gate_pre, activated_grad))
        bytedown_grad = transposed_times(activated, feed_grad)
        byteup_grad = transposed_times(normed_two, gate_grad)
        normed_two_grad = wide(tensor_sum(times_transposed(gate_grad, byte_up)))
        feed_norm_grad, bytegain_grad = norm_back(after_attend, byte_gain, normed_two_grad)
        after_attend_grad = wide(feed_grad) + feed_norm_grad

    with jax.named_scope("byte_attend_back"):
        attend_branch_grad = narrow(after_attend_grad)
        attendoutput_grad = transposed_times(mixed_heads, attend_branch_grad)
        mixed_heads_grad = narrow(times_transposed(attend_branch_grad, attend_output))
        query_grad, key_grad, value_grad = attend_backward(
            window_low, window_log, queries, mixed_heads_grad, keys, values, window_span, query_rows
        )
        pair_grad = jnp.concatenate([key_grad, value_grad], axis=1)
        own_grad = wide(pair_grad[WIN:])
        begin_row = WIN
        for step, need_rows in enumerate(need_list):
            begin_row = begin_row - need_rows
            returned = from_behind(pair_grad[begin_row : begin_row + need_rows], "seq", -step - 1)
            own_grad = own_grad.at[tok_rows - need_rows :].add(wide(returned))
        projected_grad = jnp.concatenate([query_grad, narrow(own_grad)], axis=1)
        attendinput_grad = transposed_times(normed, projected_grad)
        normed_grad = wide(tensor_sum(times_transposed(projected_grad, in_matrix)))
        stream_norm_grad, attendgain_grad = norm_back(stream_value, attend_gain, normed_grad)
        inflow = narrow(after_attend_grad + stream_norm_grad)

    with jax.named_scope("weight_sums"):

        def seq_sum(pieces):
            part = lax.psum_scatter(narrow(pieces), "seq", scatter_dimension=0, tiled=True)
            return wide(lax.all_gather(part, "seq", axis=0, tiled=True))

        feed_sum = seq_sum(jnp.concatenate([byteup_grad, bytedown_grad], axis=1))
        hidden = byte_up.shape[1]
        byteup_grad = feed_sum[:, :hidden]
        bytedown_grad = feed_sum[:, hidden:]
        attend_sum = seq_sum(
            jnp.concatenate([attendinput_grad, attendoutput_grad.reshape(width, -1)], axis=1)
        )
        attendinput_grad = attend_sum[:, : 3 * head_cols].reshape(width, 3, head_cols)
        attendoutput_grad = attend_sum[:, 3 * head_cols :].reshape(head_cols, width)
        gains = jnp.concatenate([attendgain_grad, bytegain_grad, patchgain_grad, densegain_grad])
        gains = lax.psum(gains, "seq")
        attendgain_grad = gains[:width]
        bytegain_grad = gains[width : 2 * width]
        patchgain_grad = gains[2 * width : 2 * width + big_width]
        densegain_grad = gains[2 * width + big_width :]

    return (
        result,
        inflow,
        attendgain_grad,
        attendinput_grad,
        attendoutput_grad,
        bytegain_grad,
        byteup_grad,
        bytedown_grad,
        patchgain_grad,
        patchinput_grad,
        patchoutput_grad,
        densegain_grad,
        denseup_grad,
        densedown_grad,
    )


def solution(mesh):
    in_specs = (
        P("seq", None),
        P("seq", None),
        P("seq"),
        P(),
        P(),
        P(None, None, "tensor"),
        P("tensor", None),
        P(),
        P(None, "tensor"),
        P("tensor", None),
        P(),
        P(None, None, "tensor"),
        P("tensor", None),
        P(),
        P(None, "tensor"),
        P("tensor", None),
    )
    out_specs = (
        P("seq", None),
        P("seq", None),
        P(),
        P(None, None, "tensor"),
        P("tensor", None),
        P(),
        P(None, "tensor"),
        P("tensor", None),
        P(),
        P(None, None, "tensor"),
        P("tensor", None),
        P(),
        P(None, "tensor"),
        P("tensor", None),
    )
    return jax.shard_map(
        on_device, mesh=mesh, in_specs=in_specs, out_specs=out_specs, check_vma=False
    )
```

```python
import functools

import jax
import jax.numpy as jnp
from jax import lax
from jax.experimental import pallas as pl
from jax.experimental.pallas import tpu as pltpu
from jax.sharding import PartitionSpec as P

HD = 64
WIN = 1536
DEV_ITEM = 4

EPSILON = 1e-06
NEGATIVE = -1e30
SCORE_SCALE = HD ** (-0.5)
WIDE_TYPE = jnp.float32
NARROW_TYPE = jnp.bfloat16
VMEM_BYTES = 48 << 20
MESH = pl.DeviceIdType.MESH


def from_behind(value, axis, steps):
    count = lax.axis_size(axis)
    initial, last = (max(0, -steps), min(count, count - steps))
    return lax.ppermute(value, axis, [(source, source + steps) for source in range(initial, last)])


def rms_scale(values, scaling):
    return values * lax.rsqrt(jnp.mean(values * values, axis=-1, keepdims=True) + EPSILON) * scaling


def gelu_tanh(values):
    return jax.nn.gelu(values, approximate=True)


def norm_back(values, scaling, upstream):
    unused, pullback = jax.vjp(rms_scale, values, scaling)
    return pullback(upstream)


def gelu_back(values, upstream):
    unused, pullback = jax.vjp(gelu_tanh, values)
    return pullback(upstream)[0]


def contract(left_side, right_side, left_axis, right_axis):
    return lax.dot_general(
        left_side,
        right_side,
        (((left_axis,), (right_axis,)), ((), ())),
        preferred_element_type=WIDE_TYPE,
    )


def product(left_side, right_side):
    return contract(left_side, right_side, 1, 0)


def times_transposed(left_side, right_side):
    return contract(left_side, right_side, 1, 1)


def transposed_times(left_side, right_side):
    return contract(left_side, right_side, 0, 0)


def wide(values):
    return values.astype(WIDE_TYPE)


def narrow(values):
    return values.astype(NARROW_TYPE)


def meet(peers):
    barrier = pltpu.get_barrier_semaphore()
    for peer in peers:
        pl.semaphore_signal(barrier, inc=1, device_id=peer, device_id_type=MESH)
    pl.semaphore_wait(barrier, len(peers))


def tensor_peers():
    place = lax.axis_index("tensor")
    pair = place + 1 - 2 * (place % 2)
    across = (place + 2) % 4
    return place, pair, across


def remote(source, target, send_sem, recv_sem, peer):
    return pltpu.make_async_remote_copy(
        src_ref=source,
        dst_ref=target,
        send_sem=send_sem,
        recv_sem=recv_sem,
        device_id=peer,
        device_id_type=MESH,
    )


def tensor_sum_body(
    chunks, part, total, pair_got, mine, across_got, pair_send, pair_recv, far_send, far_recv,
    out_send, out_recv,
):
    place, pair, across = tensor_peers()
    pair_id = {"tensor": pair}
    across_id = {"tensor": across}
    meet((pair_id, across_id))
    rows = part.shape[0] // 4
    step = rows // chunks
    pair_across = (pair + 2) % 4

    def piece(quarter, chunk):
        return pl.ds(pl.multiple_of(quarter * rows + chunk * step, 16), step)

    copies = []
    for slot, quarter in enumerate((pair_across, pair)):
        for chunk in range(chunks):
            copy = remote(
                part.at[piece(quarter, chunk)],
                pair_got.at[slot, pl.ds(chunk * step, step)],
                pair_send.at[slot, chunk],
                pair_recv.at[slot, chunk],
                pair_id,
            )
            copy.start()
            copies.append(copy)
    far = []
    for chunk in range(chunks):
        copies[chunk].wait_recv()
        here = pl.ds(chunk * step, step)
        mine[here] = (
            part[piece(across, chunk)].astype(WIDE_TYPE) + pair_got[0, here].astype(WIDE_TYPE)
        ).astype(NARROW_TYPE)
        copy = remote(
            mine.at[here],
            across_got.at[here],
            far_send.at[chunk],
            far_recv.at[chunk],
            across_id,
        )
        copy.start()
        far.append(copy)
    out_copies = []
    for chunk in range(chunks):
        copies[chunks + chunk].wait_recv()
        far[chunk].wait_recv()
        here = pl.ds(chunk * step, step)
        own = piece(place, chunk)
        total[own] = (
            part[own].astype(WIDE_TYPE)
            + pair_got[1, here].astype(WIDE_TYPE)
            + across_got[here].astype(WIDE_TYPE)
        ).astype(NARROW_TYPE)
        for kind, peer in ((0, across_id), (1, pair_id)):
            copy = remote(
                total.at[own],
                total.at[own],
                out_send.at[kind, chunk],
                out_recv.at[kind, chunk],
                peer,
            )
            copy.start()
            out_copies.append(copy)
    passed = []
    for chunk in range(chunks):
        out_copies[2 * chunk].wait_recv()
        theirs = piece(across, chunk)
        copy = remote(
            total.at[theirs],
            total.at[theirs],
            out_send.at[2, chunk],
            out_recv.at[2, chunk],
            pair_id,
        )
        copy.start()
        passed.append(copy)
    for chunk in range(chunks):
        out_copies[2 * chunk + 1].wait_recv()
        passed[chunk].wait_recv()
    for copy in copies + far + out_copies + passed:
        copy.wait_send()


def tensor_sum(part, collective_id, chunks):
    rows, cols = part.shape
    quarter = rows // 4
    dma = pltpu.SemaphoreType.DMA
    return pl.pallas_call(
        functools.partial(tensor_sum_body, chunks),
        in_specs=[pl.BlockSpec(memory_space=pltpu.VMEM)],
        out_specs=pl.BlockSpec(memory_space=pltpu.VMEM),
        out_shape=jax.ShapeDtypeStruct((rows, cols), NARROW_TYPE),
        scratch_shapes=[
            pltpu.VMEM((2, quarter, cols), NARROW_TYPE),
            pltpu.VMEM((quarter, cols), NARROW_TYPE),
            pltpu.VMEM((quarter, cols), NARROW_TYPE),
            dma((2, chunks)), dma((2, chunks)), dma((chunks,)), dma((chunks,)),
            dma((3, chunks)), dma((3, chunks)),
        ],
        compiler_params=pltpu.CompilerParams(
            collective_id=collective_id, has_side_effects=True, vmem_limit_bytes=VMEM_BYTES
        ),
        name="tensor_sum",
    )(part)


def tensor_gather_body(chunks, block, out, local_sem, send_sem, recv_sem):
    place, pair, across = tensor_peers()
    pair_id = {"tensor": pair}
    across_id = {"tensor": across}
    meet((pair_id, across_id))
    rows = block.shape[0]
    step = rows // chunks

    def piece(owner, chunk):
        return pl.ds(pl.multiple_of(owner * rows + chunk * step, 16), step)

    copies = []
    for kind, peer in ((0, across_id), (1, pair_id)):
        for chunk in range(chunks):
            copy = remote(
                block.at[pl.ds(chunk * step, step)],
                out.at[piece(place, chunk)],
                send_sem.at[kind, chunk],
                recv_sem.at[kind, chunk],
                peer,
            )
            copy.start()
            copies.append(copy)
    local = pltpu.make_async_copy(block, out.at[pl.ds(pl.multiple_of(place * rows, 16), rows)], local_sem)
    local.start()
    passed = []
    for chunk in range(chunks):
        copies[chunk].wait_recv()
        copy = remote(
            out.at[piece(across, chunk)],
            out.at[piece(across, chunk)],
            send_sem.at[2, chunk],
            recv_sem.at[2, chunk],
            pair_id,
        )
        copy.start()
        passed.append(copy)
    local.wait()
    for chunk in range(chunks):
        copies[chunks + chunk].wait_recv()
        passed[chunk].wait_recv()
    for copy in copies + passed:
        copy.wait_send()


def tensor_gather(block, collective_id, chunks):
    rows, cols = block.shape
    dma = pltpu.SemaphoreType.DMA
    return pl.pallas_call(
        functools.partial(tensor_gather_body, chunks),
        in_specs=[pl.BlockSpec(memory_space=pltpu.VMEM)],
        out_specs=pl.BlockSpec(memory_space=pltpu.VMEM),
        out_shape=jax.ShapeDtypeStruct((4*rows, cols), NARROW_TYPE),
        scratch_shapes=[dma(()), dma((3, chunks)), dma((3, chunks))],
        compiler_params=pltpu.CompilerParams(
            collective_id=collective_id, has_side_effects=True, vmem_limit_bytes=VMEM_BYTES
        ),
        name="tensor_gather",
    )(block)


def ring_at(spot, count):
    half = spot // (count // 2)
    return (1 - half) * 2 * spot + half * (2 * (count - 1 - spot) + 1)


def ring_spot(device, count):
    return device // 2 + (device % 2) * (count - 1 - 2 * (device // 2))


def seq_gather_body(count, block, out, local_sem, ring_send, ring_recv, pair_send, pair_recv):
    device = lax.axis_index("seq")
    place, pair, across = tensor_peers()
    spot = ring_spot(device, count)
    ahead = {"seq": ring_at((spot + 1) % count, count)}
    behind = {"seq": ring_at((spot + count - 1) % count, count)}
    pair_id = {"tensor": pair}
    meet((ahead, behind, pair_id))
    rows = block.shape[0]
    step = rows // 4
    core = place % 2

    def piece(owner, sub):
        return pl.ds(pl.multiple_of(owner * rows + core * 2 * step + sub * step, 16), step)

    hops = count // 2
    sends = []
    moves = {}

    def launch(way, hop, sub):
        distance = hop - 1
        if way == 0:
            owner = ring_at((spot + count - distance) % count, count)
        else:
            owner = ring_at((spot + distance) % count, count)
        if hop == 1:
            source = block.at[pl.ds(pl.multiple_of(core * 2 * step + sub * step, 16), step)]
        else:
            source = out.at[piece(owner, sub)]
        copy = remote(
            source,
            out.at[piece(owner, sub)],
            ring_send.at[way, hop - 1, sub],
            ring_recv.at[way, hop - 1, sub],
            (ahead, behind)[way],
        )
        copy.start()
        moves[way, hop, sub] = copy
        sends.append(copy)

    order = ((0, 0), (1, 1), (0, 1), (1, 0))
    for way, sub in order:
        launch(way, 1, sub)
    local = pltpu.make_async_copy(
        block, out.at[pl.ds(pl.multiple_of(device * rows, 16), rows)], local_sem
    )
    local.start()
    pairs = []
    for hop in range(1, hops + 1):
        for way, sub in order:
            if hop == hops and way != sub:
                continue
            moves[way, hop, sub].wait_recv()
            if hop + 1 < hops or (hop + 1 == hops and way == sub):
                launch(way, hop + 1, sub)
            if way == 0:
                owner = ring_at((spot + count - hop) % count, count)
            else:
                owner = ring_at((spot + hop) % count, count)
            copy = remote(
                out.at[piece(owner, sub)],
                out.at[piece(owner, sub)],
                pair_send.at[way, hop - 1, sub],
                pair_recv.at[way, hop - 1, sub],
                pair_id,
            )
            copy.start()
            pairs.append(copy)
    local.wait()
    for copy in pairs:
        copy.wait_recv()
    for copy in sends + pairs:
        copy.wait_send()


def seq_gather(block, collective_id):
    rows, cols = block.shape
    count = lax.axis_size("seq")
    dma = pltpu.SemaphoreType.DMA
    sems = dma((2, count // 2, 2))
    return pl.pallas_call(
        functools.partial(seq_gather_body, count),
        in_specs=[pl.BlockSpec(memory_space=pltpu.VMEM)],
        out_specs=pl.BlockSpec(memory_space=pltpu.VMEM),
        out_shape=jax.ShapeDtypeStruct((count*rows, cols), NARROW_TYPE),
        scratch_shapes=[dma(()), sems, sems, sems, sems],
        compiler_params=pltpu.CompilerParams(
            collective_id=collective_id, has_side_effects=True, vmem_limit_bytes=VMEM_BYTES
        ),
        name="seq_gather",
    )(block)


def allowed_pairs(low_row, first_key, span, first_query, query_rows):
    key_pos = first_key + lax.broadcasted_iota(jnp.int32, (span, query_rows), 0)
    query_pos = first_query + lax.broadcasted_iota(jnp.int32, (span, query_rows), 1)
    return (key_pos >= low_row) & (key_pos <= query_pos)


def forward_body(
    heads, query_rows, span, offset, upright, low, queries, keys, values, mixed, log_total
):
    block = pl.program_id(1)
    start = jnp.maximum(block * query_rows + query_rows + offset - span, 0)
    start = pl.multiple_of(start, 128)
    allowed = allowed_pairs(low[...], start, span, block * query_rows + offset, query_rows)
    rows = pl.ds(start, span)
    for head in range(heads):
        cols = slice(head * HD, (head + 1) * HD)
        scores = contract(keys[rows, cols], queries[:, cols] * SCORE_SCALE, 1, 1)
        scores = jnp.where(allowed, scores, NEGATIVE)
        top = jnp.max(scores, axis=0, keepdims=True)
        raised = jnp.exp(scores - top)
        total = jnp.sum(raised, axis=0, keepdims=True)
        weights = narrow(raised * (1.0 / total))
        mixed_head = contract(values[rows, cols], weights, 0, 0)
        if upright:
            mixed[cols, :] = narrow(mixed_head)
        else:
            mixed[:, cols] = narrow(mixed_head.T)
        log_total[0, head : head + 1, :] = top + jnp.log(total)


def backward_body(
    heads,
    query_rows,
    span,
    offset,
    low,
    log_total,
    queries,
    out_grads,
    keys,
    values,
    query_grads,
    key_grads,
    value_grads,
    key_sum,
    value_sum,
):
    block = pl.program_id(1)

    @pl.when(block == 0)
    def clear():
        key_sum[...] = jnp.zeros_like(key_sum)
        value_sum[...] = jnp.zeros_like(value_sum)

    start = jnp.maximum(block * query_rows + query_rows + offset - span, 0)
    start = pl.multiple_of(start, 128)
    allowed = allowed_pairs(low[...], start, span, block * query_rows + offset, query_rows)
    rows = pl.ds(start, span)
    for head in range(heads):
        cols = slice(head * HD, (head + 1) * HD)
        query = queries[:, cols] * SCORE_SCALE
        out_grad = out_grads[:, cols]
        key = keys[rows, cols]
        scores = contract(key, query, 1, 1)
        weights = jnp.where(allowed, jnp.exp(scores - log_total[0, head : head + 1, :]), 0.0)
        weight_grad = contract(values[rows, cols], out_grad, 1, 1)
        inner = jnp.sum(weights * weight_grad, axis=0, keepdims=True)
        score_grad = narrow(weights * (weight_grad - inner))
        query_grads[:, cols] = narrow(contract(key, score_grad, 0, 0).T * SCORE_SCALE)
        key_sum[rows, cols] += contract(score_grad, query, 1, 0)
        value_sum[rows, cols] += contract(narrow(weights), out_grad, 1, 0)

    @pl.when(block == pl.num_programs(1) - 1)
    def finish():
        key_grads[...] = narrow(key_sum[...])
        value_grads[...] = narrow(value_sum[...])


def attend_sizes(queries, keys, span, query_rows):
    rows, cols = queries.shape
    extent = keys.shape[0]
    group_cols = 128 if cols % 128 == 0 else cols
    groups = cols // group_cols
    heads = group_cols // HD
    low_spec = pl.BlockSpec((1, query_rows), lambda g, b: (0, b))
    row_spec = pl.BlockSpec((query_rows, group_cols), lambda g, b: (b, g))
    all_spec = pl.BlockSpec((extent, group_cols), lambda g, b: (0, g))
    log_spec = pl.BlockSpec((1, heads, query_rows), lambda g, b: (g, 0, b))
    args = (heads, query_rows, span, extent - rows)
    log_shape = jax.ShapeDtypeStruct((groups, heads, rows), WIDE_TYPE)
    grid = (groups, rows // query_rows)
    flops = 2 * rows * span * cols
    return args, grid, low_spec, row_spec, all_spec, log_spec, log_shape, group_cols, flops


def attend_forward(low, queries, keys, values, span, query_rows, upright):
    args, grid, low_spec, row_spec, all_spec, log_spec, log_shape, unused, flops = attend_sizes(
        queries, keys, span, query_rows
    )
    mixed_spec, mixed_shape = row_spec, queries.shape
    if upright:
        group_cols = args[0] * HD
        mixed_spec = pl.BlockSpec((group_cols, query_rows), lambda g, b: (g, b))
        mixed_shape = queries.shape[::-1]
    return pl.pallas_call(
        functools.partial(forward_body, *args, upright),
        grid=grid,
        in_specs=[low_spec, row_spec, all_spec, all_spec],
        out_specs=[mixed_spec, log_spec],
        out_shape=[jax.ShapeDtypeStruct(mixed_shape, NARROW_TYPE), log_shape],
        compiler_params=pltpu.CompilerParams(vmem_limit_bytes=VMEM_BYTES),
        cost_estimate=pl.CostEstimate(
            flops=16 * flops, transcendentals=flops // 128, bytes_accessed=1 << 20
        ),
        name="attend_forward",
    )(low, queries, keys, values)


def attend_backward(low, log_total, queries, out_grads, keys, values, span, query_rows):
    args, grid, low_spec, row_spec, all_spec, log_spec, unused, group_cols, flops = attend_sizes(
        queries, keys, span, query_rows
    )
    key_shape = jax.ShapeDtypeStruct(keys.shape, NARROW_TYPE)
    return pl.pallas_call(
        functools.partial(backward_body, *args),
        grid=grid,
        in_specs=[low_spec, log_spec, row_spec, row_spec, all_spec, all_spec],
        out_specs=[row_spec, all_spec, all_spec],
        out_shape=[jax.ShapeDtypeStruct(queries.shape, NARROW_TYPE), key_shape, key_shape],
        scratch_shapes=[pltpu.VMEM((keys.shape[0], group_cols), WIDE_TYPE)] * 2,
        compiler_params=pltpu.CompilerParams(vmem_limit_bytes=VMEM_BYTES),
        cost_estimate=pl.CostEstimate(
            flops=20 * flops, transcendentals=flops // 128, bytes_accessed=1 << 20
        ),
        name="attend_backward",
    )(low, log_total, queries, out_grads, keys, values)


def in_blocks(function, rows, block_rows):
    if rows <= block_rows:
        return function(0)
    starts = jnp.arange(rows // block_rows, dtype=jnp.int32) * block_rows
    return lax.map(function, starts).reshape(rows, -1)


def on_device(
    stream,
    cotangent,
    boundary,
    counts,
    attend_gain,
    attend_input,
    attend_output,
    byte_gain,
    byte_up,
    byte_down,
    patch_gain,
    patch_input,
    patch_output,
    dense_gain,
    dense_up,
    dense_down,
):
    tok_rows, width = stream.shape
    head_cols = attend_input.shape[2]
    big_width = patch_input.shape[0]
    patch_cols = patch_input.shape[2]
    item_count = counts.shape[0]
    seq_devices = lax.axis_size("seq")
    device = lax.axis_index("seq")
    capacity = tok_rows // 4
    total_rows = seq_devices * capacity // 2
    owned_rows = total_rows // seq_devices
    item_cap = DEV_ITEM * capacity
    query_rows = min(256, tok_rows)

    per_device = counts.reshape(-1)
    ends = jnp.cumsum(per_device)
    offsets = ends - per_device
    item_begin = offsets.reshape(item_count, DEV_ITEM)[:, 0]
    my_first = offsets[device]
    rank_local = jnp.cumsum(boundary) - 1
    target = jnp.where(boundary == 1, rank_local, -1)
    send_map = narrow(jnp.arange(capacity)[:, None] == target[None, :])
    rank = jnp.arange(total_rows, dtype=jnp.int32)
    rank_device = jnp.sum(rank[:, None] >= ends[None, :], axis=1)
    rank_start = jnp.sum(
        jnp.where(rank_device[:, None] == jnp.arange(seq_devices)[None, :], offsets[None, :], 0),
        axis=1,
    )
    rank_slot = rank_device * capacity + rank - rank_start
    rank_low = jnp.max(
        jnp.where(rank[:, None] >= item_begin[None, :], item_begin[None, :], 0), axis=1
    )
    rank_low = rank_low[None, :].astype(jnp.int32)
    slot_rows = seq_devices * capacity

    def compact(slots):
        block_rows = min(1024, total_rows)

        def one_block(first_row):
            places = lax.dynamic_slice_in_dim(rank_slot, first_row, block_rows, 0)
            take_map = narrow(places[:, None] == jnp.arange(slot_rows)[None, :])
            return narrow(product(take_map, slots))

        return in_blocks(one_block, total_rows, block_rows)

    def my_slots(table):
        padded = jnp.pad(table, ((0, capacity), (0, 0)))
        return lax.dynamic_slice_in_dim(padded, my_first, capacity, 0)

    def my_block(table):
        return lax.dynamic_slice_in_dim(table, device * owned_rows, owned_rows, 0)

    with jax.named_scope("byte_attend"):
        stream_value = wide(stream)
        normed = narrow(rms_scale(stream_value, attend_gain))
        in_matrix = attend_input.reshape(width, 3 * head_cols)
        projected = narrow(product(normed, in_matrix))
        queries = projected[:, :head_cols]
        key_value = projected[:, head_cols:]
        need_list = []
        while sum(need_list) < WIN:
            need_list.append(min(tok_rows, WIN - sum(need_list)))
        arrived_list = []
        for step, need_rows in enumerate(need_list):
            arrived_list.append(from_behind(key_value[tok_rows - need_rows :], "seq", step + 1))
        extended = jnp.concatenate(arrived_list[::-1] + [key_value], axis=0)
        delta_slots = narrow(product(send_map, cotangent))
        extended, delta_slots = lax.optimization_barrier((extended, delta_slots))
        keys = extended[:, :head_cols]
        values = extended[:, head_cols:]
        window_low = jnp.maximum(
            jnp.arange(tok_rows, dtype=jnp.int32) + 1, WIN - device * tok_rows
        )[None, :]
        window_span = WIN + query_rows
        mixed_heads, window_log = attend_forward(
            window_low, queries, keys, values, window_span, query_rows, True
        )
        all_mixed = tensor_gather(mixed_heads, 0, 2)
        all_output = lax.all_gather(attend_output, "tensor", axis=0, tiled=True)
        after_attend = stream_value + transposed_times(all_mixed, all_output)

    with jax.named_scope("byte_feed"):
        normed_two = narrow(rms_scale(after_attend, byte_gain))
        gate_pre = product(normed_two, byte_up)
        activated = narrow(gelu_tanh(gate_pre))
        feed_part = narrow(product(activated, byte_down))

    with jax.named_scope("patch_rows"):
        attend_high = narrow(after_attend)
        attend_rest = narrow(after_attend - wide(attend_high))
        rows_sum = wide(tensor_sum(narrow(product(send_map, feed_part)), 1, 2))
        rows_here = narrow(
            product(send_map, attend_high) + product(send_map, attend_rest) + rows_sum
        )
        byte_rows = compact(seq_gather(rows_here, 2))

    with jax.named_scope("cotangent_rows"):
        delta_grad = compact(lax.all_gather(delta_slots, "seq", axis=0, tiled=True))
        delta_own = my_block(delta_grad)

    wide_pad = ((0, 0), (0, big_width - width))
    with jax.named_scope("patch_attend"):
        normed_three = narrow(rms_scale(wide(jnp.pad(byte_rows, wide_pad)), patch_gain))
        patch_matrix = patch_input.reshape(big_width, 3 * patch_cols)
        patch_projected = narrow(product(normed_three, patch_matrix))
        patch_queries = patch_projected[:, :patch_cols]
        patch_keys = patch_projected[:, patch_cols : 2 * patch_cols]
        patch_values = patch_projected[:, 2 * patch_cols :]
        patch_query_rows = min(256, total_rows)
        patch_span = min(total_rows, item_cap + patch_query_rows)
        mixed_patch, patch_log = attend_forward(
            rank_low, patch_queries, patch_keys, patch_values, patch_span, patch_query_rows, False
        )
        branch_own = wide(tensor_sum(narrow(product(my_block(mixed_patch), patch_output)), 3, 2))

    with jax.named_scope("patch_dense"):
        own_rows = wide(jnp.pad(my_block(byte_rows), wide_pad))
        after_patch = own_rows + branch_own
        normed_four = narrow(rms_scale(after_patch, dense_gain))
        dense_pre = product(normed_four, dense_up)
        dense_pre_grad = narrow(gelu_back(dense_pre, times_transposed(delta_own, dense_down)))
        normed_four_grad = wide(tensor_sum(narrow(times_transposed(dense_pre_grad, dense_up)), 4, 2))
        after_patch_grad, densegain_grad = norm_back(after_patch, dense_gain, normed_four_grad)
        branch_grad_own = narrow(after_patch_grad + wide(jnp.pad(delta_own, wide_pad)))
        branch_grad = seq_gather(branch_grad_own, 5)
        branch_grad, normed_later = lax.optimization_barrier((branch_grad, normed_four))
        all_normed = lax.all_gather(normed_later, "seq", axis=0, tiled=True)

    with jax.named_scope("dense_weights"):
        block_rows = min(1024, total_rows)

        def dense_block(first_row):
            some_normed = lax.dynamic_slice_in_dim(all_normed, first_row, block_rows, 0)
            some_delta = lax.dynamic_slice_in_dim(delta_grad, first_row, block_rows, 0)
            some_pre = product(some_normed, dense_up)
            some_act = narrow(gelu_tanh(some_pre))
            some_grad = narrow(gelu_back(some_pre, times_transposed(some_delta, dense_down)))
            return (
                some_act,
                transposed_times(some_act, some_delta),
                transposed_times(some_normed, some_grad),
            )

        if total_rows == block_rows:
            dense_act, densedown_grad, denseup_grad = dense_block(0)
        else:

            def dense_step(sums, first_row):
                some_act, down_part, up_part = dense_block(first_row)
                return (sums[0] + down_part, sums[1] + up_part), some_act

            starts = jnp.arange(total_rows // block_rows, dtype=jnp.int32) * block_rows
            initial = (jnp.zeros(dense_down.shape), jnp.zeros(dense_up.shape))
            (densedown_grad, denseup_grad), dense_act = lax.scan(dense_step, initial, starts)
            dense_act = dense_act.reshape(total_rows, -1)

    with jax.named_scope("result"):
        delta_part = product(my_slots(mixed_patch), patch_output[:, :width])
        delta_part = narrow(delta_part + product(my_slots(dense_act), dense_down))
        result_part = wide(feed_part) + transposed_times(send_map, delta_part)
        result = narrow(after_attend + wide(lax.psum(narrow(result_part), "tensor")))

    with jax.named_scope("patch_attend_back"):
        patchoutput_grad = transposed_times(mixed_patch, branch_grad)
        mixed_patch_grad = narrow(times_transposed(branch_grad, patch_output))
        patch_projected_grad = jnp.concatenate(
            attend_backward(
                rank_low,
                patch_log,
                patch_queries,
                mixed_patch_grad,
                patch_keys,
                patch_values,
                patch_span,
                patch_query_rows,
            ),
            axis=1,
        )
        patchinput_grad = transposed_times(normed_three, patch_projected_grad)
        patchinput_grad = patchinput_grad.reshape(big_width, 3, patch_cols)
        normed_three_grad = times_transposed(my_slots(patch_projected_grad), patch_matrix)
        normed_three_grad = wide(tensor_sum(narrow(normed_three_grad), 6, 2))
        patch_norm_grad, patchgain_grad = norm_back(
            wide(jnp.pad(rows_here, wide_pad)), patch_gain, normed_three_grad
        )
        rows_grad = narrow(wide(my_slots(branch_grad[:, :width])) + patch_norm_grad[:, :width])

    with jax.named_scope("byte_feed_back"):
        feed_grad = narrow(
            jnp.where(
                boundary[:, None] == 1,
                transposed_times(send_map, rows_grad),
                wide(cotangent),
            )
        )
        activated_grad = times_transposed(feed_grad, byte_down)
        gate_grad = narrow(gelu_back(gate_pre, activated_grad))
        bytedown_grad = transposed_times(activated, feed_grad)
        byteup_grad = transposed_times(normed_two, gate_grad)
        feed_pack = narrow(jnp.concatenate([byteup_grad, bytedown_grad], axis=1))
        normed_two_part = narrow(times_transposed(gate_grad, byte_up))
        feed_pack, normed_two_part = lax.optimization_barrier((feed_pack, normed_two_part))
        normed_two_grad = wide(tensor_sum(normed_two_part, 7, 2))
        feed_norm_grad, bytegain_grad = norm_back(after_attend, byte_gain, normed_two_grad)
        after_attend_grad = wide(feed_grad) + feed_norm_grad

    with jax.named_scope("byte_attend_back"):
        attend_branch_grad = narrow(after_attend_grad)
        attendoutput_grad = product(mixed_heads, attend_branch_grad)
        mixed_heads_grad = narrow(times_transposed(attend_branch_grad, attend_output))
        query_grad, key_grad, value_grad = attend_backward(
            window_low, window_log, queries, mixed_heads_grad, keys, values, window_span, query_rows
        )
        pair_grad = jnp.concatenate([key_grad, value_grad], axis=1)
        own_grad = wide(pair_grad[WIN:])
        begin_row = WIN
        for step, need_rows in enumerate(need_list):
            begin_row = begin_row - need_rows
            returned = from_behind(pair_grad[begin_row : begin_row + need_rows], "seq", -step - 1)
            own_grad = own_grad.at[tok_rows - need_rows :].add(wide(returned))
        projected_grad = jnp.concatenate([query_grad, narrow(own_grad)], axis=1)
        attendinput_grad = transposed_times(normed, projected_grad)
        normed_grad = wide(tensor_sum(narrow(times_transposed(projected_grad, in_matrix)), 8, 2))
        stream_norm_grad, attendgain_grad = norm_back(stream_value, attend_gain, normed_grad)
        inflow = narrow(after_attend_grad + stream_norm_grad)

    with jax.named_scope("weight_sums"):

        def seq_sum(pieces):
            part = lax.psum_scatter(pieces, "seq", scatter_dimension=0, tiled=True)
            return wide(lax.all_gather(part, "seq", axis=0, tiled=True))

        feed_sum = seq_sum(feed_pack)
        hidden = byte_up.shape[1]
        byteup_grad = feed_sum[:, :hidden]
        bytedown_grad = feed_sum[:, hidden:]
        gains = jnp.concatenate([attendgain_grad, bytegain_grad, patchgain_grad, densegain_grad])
        gain_cols = gains.shape[0] // width
        gains = jnp.pad(gains.reshape(gain_cols, width).T, ((0, 0), (0, 128 - gain_cols)))
        attend_sum = seq_sum(
            narrow(jnp.concatenate([attendinput_grad, attendoutput_grad.T, gains], axis=1))
        )
        attendinput_grad = attend_sum[:, : 3 * head_cols].reshape(width, 3, head_cols)
        attendoutput_grad = attend_sum[:, 3 * head_cols : 4 * head_cols].T
        gains = attend_sum[:, 4 * head_cols : 4 * head_cols + gain_cols].T.reshape(-1)
        attendgain_grad = gains[:width]
        bytegain_grad = gains[width : 2 * width]
        patchgain_grad = gains[2 * width : 2 * width + big_width]
        densegain_grad = gains[2 * width + big_width :]

    return (
        result,
        inflow,
        attendgain_grad,
        attendinput_grad,
        attendoutput_grad,
        bytegain_grad,
        byteup_grad,
        bytedown_grad,
        patchgain_grad,
        patchinput_grad,
        patchoutput_grad,
        densegain_grad,
        denseup_grad,
        densedown_grad,
    )


def solution(mesh):
    in_specs = (
        P("seq", None),
        P("seq", None),
        P("seq"),
        P(),
        P(),
        P(None, None, "tensor"),
        P("tensor", None),
        P(),
        P(None, "tensor"),
        P("tensor", None),
        P(),
        P(None, None, "tensor"),
        P("tensor", None),
        P(),
        P(None, "tensor"),
        P("tensor", None),
    )
    out_specs = (
        P("seq", None),
        P("seq", None),
        P(),
        P(None, None, "tensor"),
        P("tensor", None),
        P(),
        P(None, "tensor"),
        P("tensor", None),
        P(),
        P(None, None, "tensor"),
        P("tensor", None),
        P(),
        P(None, "tensor"),
        P("tensor", None),
    )
    return jax.shard_map(
        on_device, mesh=mesh, in_specs=in_specs, out_specs=out_specs, check_vma=False
    )
```

```python
import functools

import jax
import jax.numpy as jnp
from jax import lax
from jax.experimental import pallas as pl
from jax.experimental.pallas import tpu as pltpu
from jax.sharding import PartitionSpec as P

HD = 64
WIN = 1536
DEV_ITEM = 4

EPSILON = 1e-06
NEGATIVE = -1e30
SCORE_SCALE = HD ** (-0.5)
WIDE_TYPE = jnp.float32
NARROW_TYPE = jnp.bfloat16
VMEM_BYTES = 48 << 20
MESH = pl.DeviceIdType.MESH


def from_behind(value, axis, steps):
    count = lax.axis_size(axis)
    initial, last = (max(0, -steps), min(count, count - steps))
    return lax.ppermute(value, axis, [(source, source + steps) for source in range(initial, last)])


def rms_scale(values, scaling):
    return values * lax.rsqrt(jnp.mean(values * values, axis=-1, keepdims=True) + EPSILON) * scaling


def gelu_tanh(values):
    return jax.nn.gelu(values, approximate=True)


def norm_back(values, scaling, upstream):
    unused, pullback = jax.vjp(rms_scale, values, scaling)
    return pullback(upstream)


def gelu_back(values, upstream):
    unused, pullback = jax.vjp(gelu_tanh, values)
    return pullback(upstream)[0]


def contract(left_side, right_side, left_axis, right_axis):
    return lax.dot_general(
        left_side,
        right_side,
        (((left_axis,), (right_axis,)), ((), ())),
        preferred_element_type=WIDE_TYPE,
    )


def product(left_side, right_side):
    return contract(left_side, right_side, 1, 0)


def times_transposed(left_side, right_side):
    return contract(left_side, right_side, 1, 1)


def transposed_times(left_side, right_side):
    return contract(left_side, right_side, 0, 0)


def wide(values):
    return values.astype(WIDE_TYPE)


def narrow(values):
    return values.astype(NARROW_TYPE)


def meet(peers):
    barrier = pltpu.get_barrier_semaphore()
    for peer in peers:
        pl.semaphore_signal(barrier, inc=1, device_id=peer, device_id_type=MESH)
    pl.semaphore_wait(barrier, len(peers))


def tensor_peers():
    place = lax.axis_index("tensor")
    pair = place + 1 - 2 * (place % 2)
    across = (place + 2) % 4
    return place, pair, across


def remote(source, target, send_sem, recv_sem, peer):
    return pltpu.make_async_remote_copy(
        src_ref=source,
        dst_ref=target,
        send_sem=send_sem,
        recv_sem=recv_sem,
        device_id=peer,
        device_id_type=MESH,
    )


def tensor_sum_body(chunks, part, total, pair_got, mine, across_got, send_sem, recv_sem):
    place, pair, across = tensor_peers()
    pair_id = {"tensor": pair}
    across_id = {"tensor": across}
    meet((pair_id, across_id))
    rows = part.shape[0] // 2
    step = rows // chunks
    core = place % 2

    def piece(half, chunk):
        return pl.ds(pl.multiple_of(half * rows + chunk * step, 16), step)

    given = []
    for chunk in range(chunks):
        copy = remote(
            part.at[piece(1 - core, chunk)],
            pair_got.at[pl.ds(chunk * step, step)],
            send_sem.at[0, chunk],
            recv_sem.at[0, chunk],
            pair_id,
        )
        copy.start()
        given.append(copy)
    far = []
    for chunk in range(chunks):
        given[chunk].wait_recv()
        here = pl.ds(chunk * step, step)
        mine[here] = narrow(wide(part[piece(core, chunk)]) + wide(pair_got[here]))
        copy = remote(
            mine.at[here],
            across_got.at[here],
            send_sem.at[1, chunk],
            recv_sem.at[1, chunk],
            across_id,
        )
        copy.start()
        far.append(copy)
    back = []
    for chunk in range(chunks):
        far[chunk].wait_recv()
        here = pl.ds(chunk * step, step)
        own = piece(core, chunk)
        total[own] = narrow(wide(mine[here]) + wide(across_got[here]))
        copy = remote(
            total.at[own],
            total.at[own],
            send_sem.at[2, chunk],
            recv_sem.at[2, chunk],
            pair_id,
        )
        copy.start()
        back.append(copy)
    for copy in back:
        copy.wait_recv()
    for copy in given + far + back:
        copy.wait_send()


def tensor_sum(part, collective_id, chunks):
    rows, cols = part.shape
    half = rows // 2
    dma = pltpu.SemaphoreType.DMA
    return pl.pallas_call(
        functools.partial(tensor_sum_body, chunks),
        in_specs=[pl.BlockSpec(memory_space=pltpu.VMEM)],
        out_specs=pl.BlockSpec(memory_space=pltpu.VMEM),
        out_shape=jax.ShapeDtypeStruct((rows, cols), NARROW_TYPE),
        scratch_shapes=[
            pltpu.VMEM((half, cols), NARROW_TYPE),
            pltpu.VMEM((half, cols), NARROW_TYPE),
            pltpu.VMEM((half, cols), NARROW_TYPE),
            dma((3, chunks)), dma((3, chunks)),
        ],
        compiler_params=pltpu.CompilerParams(
            collective_id=collective_id, has_side_effects=True, vmem_limit_bytes=VMEM_BYTES
        ),
        name="tensor_sum",
    )(part)


def tensor_gather_body(chunks, block, out, local_sem, send_sem, recv_sem):
    place, pair, across = tensor_peers()
    pair_id = {"tensor": pair}
    across_id = {"tensor": across}
    meet((pair_id, across_id))
    rows = block.shape[0]
    step = rows // chunks

    def piece(owner, chunk):
        return pl.ds(pl.multiple_of(owner * rows + chunk * step, 16), step)

    copies = []
    for kind, peer in ((0, across_id), (1, pair_id)):
        for chunk in range(chunks):
            copy = remote(
                block.at[pl.ds(chunk * step, step)],
                out.at[piece(place, chunk)],
                send_sem.at[kind, chunk],
                recv_sem.at[kind, chunk],
                peer,
            )
            copy.start()
            copies.append(copy)
    local = pltpu.make_async_copy(block, out.at[pl.ds(pl.multiple_of(place * rows, 16), rows)], local_sem)
    local.start()
    passed = []
    for chunk in range(chunks):
        copies[chunk].wait_recv()
        copy = remote(
            out.at[piece(across, chunk)],
            out.at[piece(across, chunk)],
            send_sem.at[2, chunk],
            recv_sem.at[2, chunk],
            pair_id,
        )
        copy.start()
        passed.append(copy)
    local.wait()
    for chunk in range(chunks):
        copies[chunks + chunk].wait_recv()
        passed[chunk].wait_recv()
    for copy in copies + passed:
        copy.wait_send()


def tensor_gather(block, collective_id, chunks):
    rows, cols = block.shape
    dma = pltpu.SemaphoreType.DMA
    return pl.pallas_call(
        functools.partial(tensor_gather_body, chunks),
        in_specs=[pl.BlockSpec(memory_space=pltpu.VMEM)],
        out_specs=pl.BlockSpec(memory_space=pltpu.VMEM),
        out_shape=jax.ShapeDtypeStruct((4*rows, cols), NARROW_TYPE),
        scratch_shapes=[dma(()), dma((3, chunks)), dma((3, chunks))],
        compiler_params=pltpu.CompilerParams(
            collective_id=collective_id, has_side_effects=True, vmem_limit_bytes=VMEM_BYTES
        ),
        name="tensor_gather",
    )(block)


def ring_at(spot, count):
    half = spot // (count // 2)
    return (1 - half) * 2 * spot + half * (2 * (count - 1 - spot) + 1)


def ring_spot(device, count):
    return device // 2 + (device % 2) * (count - 1 - 2 * (device // 2))


def seq_gather_body(count, block, out, local_sem, ring_send, ring_recv, pair_send, pair_recv):
    device = lax.axis_index("seq")
    place, pair, across = tensor_peers()
    spot = ring_spot(device, count)
    ahead = {"seq": ring_at((spot + 1) % count, count)}
    behind = {"seq": ring_at((spot + count - 1) % count, count)}
    pair_id = {"tensor": pair}
    meet((ahead, behind, pair_id))
    rows = block.shape[0]
    step = rows // 4
    core = place % 2

    def piece(owner, sub):
        return pl.ds(pl.multiple_of(owner * rows + core * 2 * step + sub * step, 16), step)

    hops = count // 2
    sends = []
    moves = {}

    def launch(way, hop, sub):
        distance = hop - 1
        if way == 0:
            owner = ring_at((spot + count - distance) % count, count)
        else:
            owner = ring_at((spot + distance) % count, count)
        if hop == 1:
            source = block.at[pl.ds(pl.multiple_of(core * 2 * step + sub * step, 16), step)]
        else:
            source = out.at[piece(owner, sub)]
        copy = remote(
            source,
            out.at[piece(owner, sub)],
            ring_send.at[way, hop - 1, sub],
            ring_recv.at[way, hop - 1, sub],
            (ahead, behind)[way],
        )
        copy.start()
        moves[way, hop, sub] = copy
        sends.append(copy)

    order = ((0, 0), (1, 1), (0, 1), (1, 0))
    for way, sub in order:
        launch(way, 1, sub)
    local = pltpu.make_async_copy(
        block, out.at[pl.ds(pl.multiple_of(device * rows, 16), rows)], local_sem
    )
    local.start()
    pairs = []
    for hop in range(1, hops + 1):
        for way, sub in order:
            if hop == hops and way != sub:
                continue
            moves[way, hop, sub].wait_recv()
            if hop + 1 < hops or (hop + 1 == hops and way == sub):
                launch(way, hop + 1, sub)
            if way == 0:
                owner = ring_at((spot + count - hop) % count, count)
            else:
                owner = ring_at((spot + hop) % count, count)
            copy = remote(
                out.at[piece(owner, sub)],
                out.at[piece(owner, sub)],
                pair_send.at[way, hop - 1, sub],
                pair_recv.at[way, hop - 1, sub],
                pair_id,
            )
            copy.start()
            pairs.append(copy)
    local.wait()
    for copy in pairs:
        copy.wait_recv()
    for copy in sends + pairs:
        copy.wait_send()


def seq_gather(block, collective_id):
    rows, cols = block.shape
    count = lax.axis_size("seq")
    dma = pltpu.SemaphoreType.DMA
    sems = dma((2, count // 2, 2))
    return pl.pallas_call(
        functools.partial(seq_gather_body, count),
        in_specs=[pl.BlockSpec(memory_space=pltpu.VMEM)],
        out_specs=pl.BlockSpec(memory_space=pltpu.VMEM),
        out_shape=jax.ShapeDtypeStruct((count*rows, cols), NARROW_TYPE),
        scratch_shapes=[dma(()), sems, sems, sems, sems],
        compiler_params=pltpu.CompilerParams(
            collective_id=collective_id, has_side_effects=True, vmem_limit_bytes=VMEM_BYTES
        ),
        name="seq_gather",
    )(block)


def allowed_pairs(low_row, first_key, span, first_query, query_rows):
    key_pos = first_key + lax.broadcasted_iota(jnp.int32, (span, query_rows), 0)
    query_pos = first_query + lax.broadcasted_iota(jnp.int32, (span, query_rows), 1)
    return (key_pos >= low_row) & (key_pos <= query_pos)


def choose_span(counts, spans, query_rows, block, run):
    if len(spans) == 1:
        run(spans[0])
    else:
        count = counts[block]
        for span in spans:
            pl.when(count == span // query_rows)(functools.partial(run, span))


def forward_body(
    heads, query_rows, spans, offset, upright, counts, low, queries, keys, values, mixed, log_total
):
    block = pl.program_id(1)

    def run(span):
        start = pl.multiple_of(block * query_rows + query_rows + offset - span, 128)
        allowed = allowed_pairs(low[...], start, span, block * query_rows + offset, query_rows)
        rows = pl.ds(start, span)
        for head in range(heads):
            cols = slice(head * HD, (head + 1) * HD)
            scores = contract(keys[rows, cols], queries[:, cols] * SCORE_SCALE, 1, 1)
            scores = jnp.where(allowed, scores, NEGATIVE)
            top = jnp.max(scores, axis=0, keepdims=True)
            raised = jnp.exp(scores - top)
            total = jnp.sum(raised, axis=0, keepdims=True)
            mixed_head = contract(values[rows, cols], narrow(raised), 0, 0) * (1.0 / total)
            if upright:
                mixed[cols, :] = narrow(mixed_head)
            else:
                mixed[:, cols] = narrow(mixed_head.T)
            log_total[0, head : head + 1, :] = top + jnp.log(total)

    choose_span(counts, spans, query_rows, block, run)


def backward_body(
    heads,
    query_rows,
    spans,
    offset,
    upright,
    counts,
    low,
    log_total,
    queries,
    mixed,
    out_grads,
    keys,
    values,
    query_grads,
    key_grads,
    value_grads,
    key_sum,
    value_sum,
):
    block = pl.program_id(1)

    @pl.when(block == 0)
    def clear():
        key_sum[...] = jnp.zeros_like(key_sum)
        value_sum[...] = jnp.zeros_like(value_sum)

    def run(span):
        start = pl.multiple_of(block * query_rows + query_rows + offset - span, 128)
        allowed = allowed_pairs(low[...], start, span, block * query_rows + offset, query_rows)
        rows = pl.ds(start, span)
        for head in range(heads):
            cols = slice(head * HD, (head + 1) * HD)
            query = queries[:, cols] * SCORE_SCALE
            out_grad = out_grads[:, cols]
            if upright:
                overlap = wide(mixed[cols, :]) * wide(out_grad).T
            else:
                overlap = (wide(mixed[:, cols]) * wide(out_grad)).T
            inner = jnp.sum(overlap, axis=0, keepdims=True)
            key = keys[rows, cols]
            scores = contract(key, query, 1, 1)
            weights = jnp.where(allowed, jnp.exp(scores - log_total[0, head : head + 1, :]), 0.0)
            weight_grad = contract(values[rows, cols], out_grad, 1, 1)
            score_grad = narrow(weights * (weight_grad - inner))
            query_grads[:, cols] = narrow(contract(key, score_grad, 0, 0).T * SCORE_SCALE)
            key_sum[rows, cols] += contract(score_grad, query, 1, 0)
            value_sum[rows, cols] += contract(narrow(weights), out_grad, 1, 0)

    choose_span(counts, spans, query_rows, block, run)

    @pl.when(block == pl.num_programs(1) - 1)
    def finish():
        key_grads[...] = narrow(key_sum[...])
        value_grads[...] = narrow(value_sum[...])


def attend_sizes(queries, keys, spans, query_rows):
    rows, cols = queries.shape
    extent = keys.shape[0]
    group_cols = 128 if cols % 128 == 0 else cols
    groups = cols // group_cols
    heads = group_cols // HD
    count_spec = pl.BlockSpec(memory_space=pltpu.SMEM)
    low_spec = pl.BlockSpec((1, query_rows), lambda g, b: (0, b))
    row_spec = pl.BlockSpec((query_rows, group_cols), lambda g, b: (b, g))
    flat_spec = pl.BlockSpec((group_cols, query_rows), lambda g, b: (g, b))
    all_spec = pl.BlockSpec((extent, group_cols), lambda g, b: (0, g))
    log_spec = pl.BlockSpec((1, heads, query_rows), lambda g, b: (g, 0, b))
    args = (heads, query_rows, spans, extent - rows)
    log_shape = jax.ShapeDtypeStruct((groups, heads, rows), WIDE_TYPE)
    grid = (groups, rows // query_rows)
    flops = 2 * rows * spans[-1] * cols
    specs = (count_spec, low_spec, row_spec, flat_spec, all_spec, log_spec)
    return args, grid, specs, log_shape, group_cols, flops


def attend_forward(counts, low, queries, keys, values, spans, query_rows, upright):
    args, grid, specs, log_shape, unused, flops = attend_sizes(queries, keys, spans, query_rows)
    count_spec, low_spec, row_spec, flat_spec, all_spec, log_spec = specs
    mixed_shape = queries.shape[::-1] if upright else queries.shape
    return pl.pallas_call(
        functools.partial(forward_body, *args, upright),
        grid=grid,
        in_specs=[count_spec, low_spec, row_spec, all_spec, all_spec],
        out_specs=[flat_spec if upright else row_spec, log_spec],
        out_shape=[jax.ShapeDtypeStruct(mixed_shape, NARROW_TYPE), log_shape],
        compiler_params=pltpu.CompilerParams(vmem_limit_bytes=VMEM_BYTES),
        cost_estimate=pl.CostEstimate(
            flops=16 * flops, transcendentals=flops // 128, bytes_accessed=1 << 20
        ),
        name="attend_forward",
    )(counts, low, queries, keys, values)


def attend_backward(
    counts, low, log_total, queries, mixed, out_grads, keys, values, spans, query_rows, upright
):
    args, grid, specs, unused, group_cols, flops = attend_sizes(queries, keys, spans, query_rows)
    count_spec, low_spec, row_spec, flat_spec, all_spec, log_spec = specs
    mixed_spec = flat_spec if upright else row_spec
    key_shape = jax.ShapeDtypeStruct(keys.shape, NARROW_TYPE)
    return pl.pallas_call(
        functools.partial(backward_body, *args, upright),
        grid=grid,
        in_specs=[
            count_spec, low_spec, log_spec, row_spec, mixed_spec, row_spec, all_spec, all_spec
        ],
        out_specs=[row_spec, all_spec, all_spec],
        out_shape=[jax.ShapeDtypeStruct(queries.shape, NARROW_TYPE), key_shape, key_shape],
        scratch_shapes=[pltpu.VMEM((keys.shape[0], group_cols), WIDE_TYPE)] * 2,
        compiler_params=pltpu.CompilerParams(vmem_limit_bytes=VMEM_BYTES),
        cost_estimate=pl.CostEstimate(
            flops=20 * flops, transcendentals=flops // 128, bytes_accessed=1 << 20
        ),
        name="attend_backward",
    )(counts, low, log_total, queries, mixed, out_grads, keys, values)


def together(*values):
    return lax.optimization_barrier(values)


def in_blocks(function, rows, block_rows):
    if rows <= block_rows:
        return function(0)
    starts = jnp.arange(rows // block_rows, dtype=jnp.int32) * block_rows
    return lax.map(function, starts).reshape(rows, -1)


def on_device(
    stream,
    cotangent,
    boundary,
    counts,
    attend_gain,
    attend_input,
    attend_output,
    byte_gain,
    byte_up,
    byte_down,
    patch_gain,
    patch_input,
    patch_output,
    dense_gain,
    dense_up,
    dense_down,
):
    tok_rows, width = stream.shape
    head_cols = attend_input.shape[2]
    big_width = patch_input.shape[0]
    patch_cols = patch_input.shape[2]
    item_count = counts.shape[0]
    seq_devices = lax.axis_size("seq")
    device = lax.axis_index("seq")
    capacity = tok_rows // 4
    total_rows = seq_devices * capacity // 2
    owned_rows = total_rows // seq_devices
    item_cap = DEV_ITEM * capacity
    query_rows = min(256, tok_rows)

    per_device = counts.reshape(-1)
    ends = jnp.cumsum(per_device)
    offsets = ends - per_device
    item_begin = offsets.reshape(item_count, DEV_ITEM)[:, 0]
    my_first = offsets[device]
    rank_local = jnp.cumsum(boundary) - 1
    target = jnp.where(boundary == 1, rank_local, -1)
    send_map = narrow(jnp.arange(capacity)[:, None] == target[None, :])
    rank = jnp.arange(total_rows, dtype=jnp.int32)
    rank_device = jnp.sum(rank[:, None] >= ends[None, :], axis=1)
    rank_start = jnp.sum(
        jnp.where(rank_device[:, None] == jnp.arange(seq_devices)[None, :], offsets[None, :], 0),
        axis=1,
    )
    rank_slot = rank_device * capacity + rank - rank_start
    rank_low = jnp.max(
        jnp.where(rank[:, None] >= item_begin[None, :], item_begin[None, :], 0), axis=1
    )
    rank_low = rank_low[None, :].astype(jnp.int32)
    slot_rows = seq_devices * capacity

    def compact_rows(slots, first_row, block_rows):
        places = lax.dynamic_slice_in_dim(rank_slot, first_row, block_rows, 0)
        take_map = narrow(places[:, None] == jnp.arange(slot_rows)[None, :])
        return narrow(product(take_map, slots))

    def compact(slots):
        block_rows = min(1024, total_rows)
        return in_blocks(
            lambda first_row: compact_rows(slots, first_row, block_rows), total_rows, block_rows
        )

    def my_slots(table):
        padded = jnp.pad(table, ((0, capacity), (0, 0)))
        return lax.dynamic_slice_in_dim(padded, my_first, capacity, 0)

    def my_block(table):
        return lax.dynamic_slice_in_dim(table, device * owned_rows, owned_rows, 0)

    with jax.named_scope("byte_attend"):
        stream_value = wide(stream)
        normed = narrow(rms_scale(stream_value, attend_gain))
        in_matrix = attend_input.reshape(width, 3 * head_cols)
        projected = narrow(product(normed, in_matrix))
        queries = projected[:, :head_cols]
        key_value = projected[:, head_cols:]
        need_list = []
        while sum(need_list) < WIN:
            need_list.append(min(tok_rows, WIN - sum(need_list)))
        arrived_list = []
        for step, need_rows in enumerate(need_list):
            arrived_list.append(from_behind(key_value[tok_rows - need_rows :], "seq", step + 1))
        extended = jnp.concatenate(arrived_list[::-1] + [key_value], axis=0)
        delta_slots = narrow(product(send_map, cotangent))
        extended, first_half = together(extended, delta_slots[:, : width // 2])
        slot_halves = [lax.all_gather(first_half, "seq", axis=0, tiled=True)]
        keys = extended[:, :head_cols]
        values = extended[:, head_cols:]
        window_low = jnp.maximum(
            jnp.arange(tok_rows, dtype=jnp.int32) + 1, WIN - device * tok_rows
        )[None, :]
        window_spans = (WIN + query_rows,)
        window_counts = jnp.zeros((tok_rows // query_rows,), jnp.int32)
        mixed_heads, window_log = attend_forward(
            window_counts, window_low, queries, keys, values, window_spans, query_rows, True
        )
        all_mixed = tensor_gather(mixed_heads, 0, 2)
        all_output = lax.all_gather(attend_output, "tensor", axis=0, tiled=True)
        after_attend = stream_value + transposed_times(all_mixed, all_output)

    with jax.named_scope("byte_feed"):
        normed_two = narrow(rms_scale(after_attend, byte_gain))
        gate_pre = product(normed_two, byte_up)
        activated = narrow(gelu_tanh(gate_pre))
        feed_part = narrow(product(activated, byte_down))

    with jax.named_scope("patch_rows"):
        attend_high = narrow(after_attend)
        attend_rest = narrow(after_attend - wide(attend_high))
        rows_sum = wide(tensor_sum(narrow(product(send_map, feed_part)), 1, 2))
        rows_here = narrow(
            product(send_map, attend_high) + product(send_map, attend_rest) + rows_sum
        )
        gathered_rows, second_half = together(
            seq_gather(rows_here, 2), delta_slots[:, width // 2 :]
        )
        byte_rows = compact(gathered_rows)

    with jax.named_scope("cotangent_rows"):
        slot_halves.append(lax.all_gather(second_half, "seq", axis=0, tiled=True))
        delta_own = jnp.concatenate(
            [compact_rows(half, device * owned_rows, owned_rows) for half in slot_halves], axis=1
        )

    wide_pad = ((0, 0), (0, big_width - width))
    with jax.named_scope("patch_attend"):
        normed_three = narrow(rms_scale(wide(jnp.pad(byte_rows, wide_pad)), patch_gain))
        patch_matrix = patch_input.reshape(big_width, 3 * patch_cols)
        patch_projected = narrow(product(normed_three, patch_matrix))
        patch_queries = patch_projected[:, :patch_cols]
        patch_keys = patch_projected[:, patch_cols : 2 * patch_cols]
        patch_values = patch_projected[:, 2 * patch_cols :]
        patch_query_rows = min(256, total_rows)
        most_blocks = min(total_rows, item_cap + patch_query_rows) // patch_query_rows
        patch_spans = tuple(patch_query_rows * (blocks + 1) for blocks in range(most_blocks))
        patch_counts = (
            jnp.arange(total_rows // patch_query_rows, dtype=jnp.int32)
            + 1
            - rank_low[0, ::patch_query_rows] // patch_query_rows
        )
        mixed_patch, patch_log = attend_forward(
            patch_counts,
            rank_low,
            patch_queries,
            patch_keys,
            patch_values,
            patch_spans,
            patch_query_rows,
            False,
        )
        branch_own = wide(tensor_sum(narrow(product(my_block(mixed_patch), patch_output)), 3, 2))

    with jax.named_scope("patch_dense"):
        own_rows = wide(jnp.pad(my_block(byte_rows), wide_pad))
        after_patch = own_rows + branch_own
        normed_four = narrow(rms_scale(after_patch, dense_gain))
        dense_pre = product(normed_four, dense_up)
        dense_pre_grad = narrow(gelu_back(dense_pre, times_transposed(delta_own, dense_down)))
        normed_four_grad = wide(tensor_sum(narrow(times_transposed(dense_pre_grad, dense_up)), 4, 2))
        after_patch_grad, densegain_grad = norm_back(after_patch, dense_gain, normed_four_grad)
        branch_grad_own = narrow(after_patch_grad + wide(jnp.pad(delta_own, wide_pad)))
        branch_grad, normed_later = together(seq_gather(branch_grad_own, 5), normed_four)
        all_normed = lax.all_gather(normed_later, "seq", axis=0, tiled=True)

    with jax.named_scope("patch_attend_back"):
        patchoutput_grad = transposed_times(mixed_patch, branch_grad)
        mixed_patch_grad = narrow(times_transposed(branch_grad, patch_output))
        patch_projected_grad = jnp.concatenate(
            attend_backward(
                patch_counts,
                rank_low,
                patch_log,
                patch_queries,
                mixed_patch,
                mixed_patch_grad,
                patch_keys,
                patch_values,
                patch_spans,
                patch_query_rows,
                False,
            ),
            axis=1,
        )
        patchinput_grad = transposed_times(normed_three, patch_projected_grad)
        patchinput_grad = patchinput_grad.reshape(big_width, 3, patch_cols)
        normed_three_grad = times_transposed(my_slots(patch_projected_grad), patch_matrix)
        normed_three_grad = wide(tensor_sum(narrow(normed_three_grad), 6, 2))
        patch_norm_grad, patchgain_grad = norm_back(
            wide(jnp.pad(rows_here, wide_pad)), patch_gain, normed_three_grad
        )
        rows_grad = narrow(wide(my_slots(branch_grad[:, :width])) + patch_norm_grad[:, :width])

    with jax.named_scope("byte_feed_back"):
        feed_grad = narrow(
            jnp.where(
                boundary[:, None] == 1,
                transposed_times(send_map, rows_grad),
                wide(cotangent),
            )
        )
        activated_grad = times_transposed(feed_grad, byte_down)
        gate_grad = narrow(gelu_back(gate_pre, activated_grad))
        bytedown_grad = transposed_times(activated, feed_grad)
        byteup_grad = transposed_times(normed_two, gate_grad)
        feed_pack = narrow(jnp.concatenate([byteup_grad, bytedown_grad], axis=1))
        normed_two_part = narrow(times_transposed(gate_grad, byte_up))
        feed_pack, normed_two_part, all_normed = together(feed_pack, normed_two_part, all_normed)
        feed_part_sum = lax.psum_scatter(feed_pack, "seq", scatter_dimension=0, tiled=True)
        normed_two_grad = wide(tensor_sum(normed_two_part, 7, 4))
        feed_norm_grad, bytegain_grad = norm_back(after_attend, byte_gain, normed_two_grad)
        after_attend_grad = wide(feed_grad) + feed_norm_grad

    with jax.named_scope("byte_attend_back"):
        attend_branch_grad = narrow(after_attend_grad)
        attendoutput_grad = product(mixed_heads, attend_branch_grad)
        mixed_heads_grad = narrow(times_transposed(attend_branch_grad, attend_output))
        query_grad, key_grad, value_grad = attend_backward(
            window_counts,
            window_low,
            window_log,
            queries,
            mixed_heads,
            mixed_heads_grad,
            keys,
            values,
            window_spans,
            query_rows,
            True,
        )
        pair_grad = jnp.concatenate([key_grad, value_grad], axis=1)
        pair_grad, all_normed, delta_halves = together(pair_grad, all_normed, tuple(slot_halves))
        own_grad = wide(pair_grad[WIN:])
        begin_row = WIN
        for step, need_rows in enumerate(need_list):
            begin_row = begin_row - need_rows
            returned = from_behind(pair_grad[begin_row : begin_row + need_rows], "seq", -step - 1)
            own_grad = own_grad.at[tok_rows - need_rows :].add(wide(returned))
        own_grad, feed_part_sum = together(own_grad, feed_part_sum)
        projected_grad = jnp.concatenate([query_grad, narrow(own_grad)], axis=1)
        attendinput_grad = transposed_times(normed, projected_grad)
        attend_pack = narrow(jnp.concatenate([attendinput_grad, attendoutput_grad.T], axis=1))
        normed_part = narrow(times_transposed(projected_grad, in_matrix))
        attend_pack, normed_part = together(attend_pack, normed_part)
        normed_grad = wide(tensor_sum(normed_part, 8, 4))
        stream_norm_grad, attendgain_grad = norm_back(stream_value, attend_gain, normed_grad)
        inflow = narrow(after_attend_grad + stream_norm_grad)

    with jax.named_scope("dense_weights"):
        block_rows = min(1024, total_rows)

        delta_grad = jnp.concatenate([compact(half) for half in delta_halves], axis=1)

        def dense_block(first_row):
            some_normed = lax.dynamic_slice_in_dim(all_normed, first_row, block_rows, 0)
            some_delta = lax.dynamic_slice_in_dim(delta_grad, first_row, block_rows, 0)
            some_pre = product(some_normed, dense_up)
            some_act = narrow(gelu_tanh(some_pre))
            some_grad = narrow(gelu_back(some_pre, times_transposed(some_delta, dense_down)))
            return (
                some_act,
                transposed_times(some_act, some_delta),
                transposed_times(some_normed, some_grad),
            )

        if total_rows == block_rows:
            dense_act, densedown_grad, denseup_grad = dense_block(0)
        else:

            def dense_step(sums, first_row):
                some_act, down_part, up_part = dense_block(first_row)
                return (sums[0] + down_part, sums[1] + up_part), some_act

            starts = jnp.arange(total_rows // block_rows, dtype=jnp.int32) * block_rows
            initial = (jnp.zeros(dense_down.shape), jnp.zeros(dense_up.shape))
            (densedown_grad, denseup_grad), dense_act = lax.scan(dense_step, initial, starts)
            dense_act = dense_act.reshape(total_rows, -1)

    with jax.named_scope("result"):
        delta_part = product(my_slots(mixed_patch), patch_output[:, :width])
        delta_part = narrow(delta_part + product(my_slots(dense_act), dense_down))
        result_part = wide(feed_part) + transposed_times(send_map, delta_part)
        result = narrow(after_attend + wide(tensor_sum(narrow(result_part), 9, 4)))

    with jax.named_scope("weight_sums"):
        feed_sum = lax.all_gather(feed_part_sum, "seq", axis=0, tiled=True)
        attend_part = lax.psum_scatter(attend_pack, "seq", scatter_dimension=0, tiled=True)
        feed_sum, attend_part = together(feed_sum, attend_part)
        feed_sum = wide(feed_sum)
        hidden = byte_up.shape[1]
        byteup_grad = feed_sum[:, :hidden]
        bytedown_grad = feed_sum[:, hidden:]
        gains = jnp.concatenate([attendgain_grad, bytegain_grad, patchgain_grad, densegain_grad])
        gains = gains.reshape(-1, width)
        gain_rows = gains.shape[0]
        gains = narrow(jnp.pad(gains, ((0, 16 - gain_rows), (0, 0))))
        attend_sum = lax.all_gather(
            jnp.concatenate([attend_part, gains], axis=0), "seq", axis=0, tiled=True
        )
        attend_sum = wide(attend_sum).reshape(seq_devices, -1, width)
        part_rows = attend_part.shape[0]
        gains = jnp.sum(attend_sum[:, part_rows : part_rows + gain_rows], axis=0).reshape(-1)
        attend_sum = attend_sum[:, :part_rows].reshape(width, width)
        attendinput_grad = attend_sum[:, : 3 * head_cols].reshape(width, 3, head_cols)
        attendoutput_grad = attend_sum[:, 3 * head_cols :].T
        attendgain_grad = gains[:width]
        bytegain_grad = gains[width : 2 * width]
        patchgain_grad = gains[2 * width : 2 * width + big_width]
        densegain_grad = gains[2 * width + big_width :]

    return (
        result,
        inflow,
        attendgain_grad,
        attendinput_grad,
        attendoutput_grad,
        bytegain_grad,
        byteup_grad,
        bytedown_grad,
        patchgain_grad,
        patchinput_grad,
        patchoutput_grad,
        densegain_grad,
        denseup_grad,
        densedown_grad,
    )


def solution(mesh):
    in_specs = (
        P("seq", None),
        P("seq", None),
        P("seq"),
        P(),
        P(),
        P(None, None, "tensor"),
        P("tensor", None),
        P(),
        P(None, "tensor"),
        P("tensor", None),
        P(),
        P(None, None, "tensor"),
        P("tensor", None),
        P(),
        P(None, "tensor"),
        P("tensor", None),
    )
    out_specs = (
        P("seq", None),
        P("seq", None),
        P(),
        P(None, None, "tensor"),
        P("tensor", None),
        P(),
        P(None, "tensor"),
        P("tensor", None),
        P(),
        P(None, None, "tensor"),
        P("tensor", None),
        P(),
        P(None, "tensor"),
        P("tensor", None),
    )
    return jax.shard_map(
        on_device, mesh=mesh, in_specs=in_specs, out_specs=out_specs, check_vma=False
    )
```

```python
import functools

import jax
import jax.numpy as jnp
from jax import lax
from jax.experimental import pallas as pl
from jax.experimental.pallas import tpu as pltpu
from jax.sharding import PartitionSpec as P

HD = 64
WIN = 1536
DEV_ITEM = 4

EPSILON = 1e-06
NEGATIVE = -1e30
SCORE_SCALE = HD ** (-0.5)
WIDE_TYPE = jnp.float32
NARROW_TYPE = jnp.bfloat16
VMEM_BYTES = 48 << 20
MESH = pl.DeviceIdType.MESH


def from_behind(value, axis, steps):
    count = lax.axis_size(axis)
    initial, last = (max(0, -steps), min(count, count - steps))
    return lax.ppermute(value, axis, [(source, source + steps) for source in range(initial, last)])


def rms_scale(values, scaling):
    return values * lax.rsqrt(jnp.mean(values * values, axis=-1, keepdims=True) + EPSILON) * scaling


def gelu_tanh(values):
    return jax.nn.gelu(values, approximate=True)


def norm_back(values, scaling, upstream):
    unused, pullback = jax.vjp(rms_scale, values, scaling)
    return pullback(upstream)


def gelu_back(values, upstream):
    unused, pullback = jax.vjp(gelu_tanh, values)
    return pullback(upstream)[0]


def contract(left_side, right_side, left_axis, right_axis):
    return lax.dot_general(
        left_side,
        right_side,
        (((left_axis,), (right_axis,)), ((), ())),
        preferred_element_type=WIDE_TYPE,
    )


def product(left_side, right_side):
    return contract(left_side, right_side, 1, 0)


def times_transposed(left_side, right_side):
    return contract(left_side, right_side, 1, 1)


def transposed_times(left_side, right_side):
    return contract(left_side, right_side, 0, 0)


def wide(values):
    return values.astype(WIDE_TYPE)


def narrow(values):
    return values.astype(NARROW_TYPE)


def meet(peers):
    barrier = pltpu.get_barrier_semaphore()
    for peer in peers:
        pl.semaphore_signal(barrier, inc=1, device_id=peer, device_id_type=MESH)
    pl.semaphore_wait(barrier, len(peers))


def tensor_peers():
    place = lax.axis_index("tensor")
    pair = place + 1 - 2 * (place % 2)
    across = (place + 2) % 4
    return place, pair, across


def remote(source, target, send_sem, recv_sem, peer):
    return pltpu.make_async_remote_copy(
        src_ref=source,
        dst_ref=target,
        send_sem=send_sem,
        recv_sem=recv_sem,
        device_id=peer,
        device_id_type=MESH,
    )


def seq_peers(count):
    device = lax.axis_index("seq")
    spot = ring_spot(device, count)
    ahead = {"seq": ring_at((spot + 1) % count, count)}
    behind = {"seq": ring_at((spot + count - 1) % count, count)}
    return device, spot, ahead, behind


def ring_at(spot, count):
    half = spot // (count // 2)
    return (1 - half) * 2 * spot + half * (2 * (count - 1 - spot) + 1)


def ring_spot(device, count):
    return device // 2 + (device % 2) * (count - 1 - 2 * (device // 2))


def run_stages(transfers, pattern):
    for index in pattern:
        next(transfers[index], None)
    for transfer in transfers:
        for unused in transfer:
            pass


def tensor_sum_stages(chunks, part, total, pair_got, mine, across_got, send_sem, recv_sem):
    place, pair, across = tensor_peers()
    pair_id = {"tensor": pair}
    across_id = {"tensor": across}
    rows = part.shape[0] // 2
    step = rows // chunks
    core = place % 2

    def piece(half, chunk):
        return pl.ds(pl.multiple_of(half * rows + chunk * step, 16), step)

    given = []
    for chunk in range(chunks):
        copy = remote(
            part.at[piece(1 - core, chunk)],
            pair_got.at[pl.ds(chunk * step, step)],
            send_sem.at[0, chunk],
            recv_sem.at[0, chunk],
            pair_id,
        )
        copy.start()
        given.append(copy)
    yield
    far = []
    for chunk in range(chunks):
        given[chunk].wait_recv()
        here = pl.ds(chunk * step, step)
        mine[here] = narrow(wide(part[piece(core, chunk)]) + wide(pair_got[here]))
        copy = remote(
            mine.at[here],
            across_got.at[here],
            send_sem.at[1, chunk],
            recv_sem.at[1, chunk],
            across_id,
        )
        copy.start()
        far.append(copy)
    yield
    back = []
    for chunk in range(chunks):
        far[chunk].wait_recv()
        here = pl.ds(chunk * step, step)
        own = piece(core, chunk)
        total[own] = narrow(wide(mine[here]) + wide(across_got[here]))
        copy = remote(
            total.at[own],
            total.at[own],
            send_sem.at[2, chunk],
            recv_sem.at[2, chunk],
            pair_id,
        )
        copy.start()
        back.append(copy)
        yield
    for copy in back:
        copy.wait_recv()
    for copy in given + far + back:
        copy.wait_send()


def tensor_gather_stages(chunks, block, out, local_sem, send_sem, recv_sem):
    place, pair, across = tensor_peers()
    pair_id = {"tensor": pair}
    across_id = {"tensor": across}
    rows = block.shape[0]
    step = rows // chunks

    def piece(owner, chunk):
        return pl.ds(pl.multiple_of(owner * rows + chunk * step, 16), step)

    copies = []
    for kind, peer in ((0, across_id), (1, pair_id)):
        for chunk in range(chunks):
            copy = remote(
                block.at[pl.ds(chunk * step, step)],
                out.at[piece(place, chunk)],
                send_sem.at[kind, chunk],
                recv_sem.at[kind, chunk],
                peer,
            )
            copy.start()
            copies.append(copy)
    local = pltpu.make_async_copy(block, out.at[pl.ds(pl.multiple_of(place * rows, 16), rows)], local_sem)
    local.start()
    yield
    passed = []
    for chunk in range(chunks):
        copies[chunk].wait_recv()
        copy = remote(
            out.at[piece(across, chunk)],
            out.at[piece(across, chunk)],
            send_sem.at[2, chunk],
            recv_sem.at[2, chunk],
            pair_id,
        )
        copy.start()
        passed.append(copy)
        yield
    local.wait()
    for chunk in range(chunks):
        copies[chunks + chunk].wait_recv()
        passed[chunk].wait_recv()
    for copy in copies + passed:
        copy.wait_send()


def ring_gather_stages(
    count, shared, block, out, local_sem, ring_send, ring_recv, pair_send, pair_recv
):
    device, spot, ahead, behind = seq_peers(count)
    place, pair, across = tensor_peers()
    pair_id = {"tensor": pair}
    rows = block.shape[0]
    step = rows // (4 if shared else 2)
    first = (place % 2) * 2 * step if shared else 0

    def piece(owner, sub):
        return pl.ds(pl.multiple_of(owner * rows + first + sub * step, 16), step)

    hops = count // 2
    sends = []
    moves = {}

    def owner_at(way, distance):
        if way == 0:
            return ring_at((spot + count - distance) % count, count)
        return ring_at((spot + distance) % count, count)

    def launch(way, hop, sub):
        owner = owner_at(way, hop - 1)
        if hop == 1:
            source = block.at[pl.ds(pl.multiple_of(first + sub * step, 16), step)]
        else:
            source = out.at[piece(owner, sub)]
        copy = remote(
            source,
            out.at[piece(owner, sub)],
            ring_send.at[way, hop - 1, sub],
            ring_recv.at[way, hop - 1, sub],
            (ahead, behind)[way],
        )
        copy.start()
        moves[way, hop, sub] = copy
        sends.append(copy)

    order = ((0, 0), (1, 1), (0, 1), (1, 0))
    for way, sub in order:
        launch(way, 1, sub)
    local = pltpu.make_async_copy(
        block, out.at[pl.ds(pl.multiple_of(device * rows, 16), rows)], local_sem
    )
    local.start()
    yield
    pairs = []
    for hop in range(1, hops + 1):
        for way, sub in order:
            if hop == hops and way != sub:
                continue
            moves[way, hop, sub].wait_recv()
            if hop + 1 < hops or (hop + 1 == hops and way == sub):
                launch(way, hop + 1, sub)
            if shared:
                owner = owner_at(way, hop)
                copy = remote(
                    out.at[piece(owner, sub)],
                    out.at[piece(owner, sub)],
                    pair_send.at[way, hop - 1, sub],
                    pair_recv.at[way, hop - 1, sub],
                    pair_id,
                )
                copy.start()
                pairs.append(copy)
        yield
    local.wait()
    for copy in pairs:
        copy.wait_recv()
    for copy in sends + pairs:
        copy.wait_send()


def ring_sum_stages(count, part, shard, arrived, send_sem, recv_sem):
    device, spot, ahead, behind = seq_peers(count)
    rows = part.shape[0] // count
    half = rows // 2
    moves = {}

    def piece(distance, way):
        owner = ring_at((spot + count - distance if way == 0 else spot + distance) % count, count)
        return pl.ds(pl.multiple_of(owner * rows + way * half, 16), half)

    def launch(way, step, source):
        copy = remote(
            source,
            arrived.at[way, step],
            send_sem.at[way, step],
            recv_sem.at[way, step],
            (ahead, behind)[way],
        )
        copy.start()
        moves[way, step] = copy

    for way in range(2):
        launch(way, 0, part.at[piece(1, way)])
    yield
    for step in range(count - 1):
        for way in range(2):
            moves[way, step].wait_recv()
            summed = wide(part[piece(step + 2, way)]) + wide(arrived[way, step])
            if step < count - 2:
                arrived[way, step] = narrow(summed)
                launch(way, step + 1, arrived.at[way, step])
            else:
                shard[pl.ds(way * half, half)] = narrow(summed)
        yield
    for copy in moves.values():
        copy.wait_send()


def meet_tensor(count):
    place, pair, across = tensor_peers()
    peers = [{"tensor": pair}, {"tensor": across}]
    if count:
        peers += seq_peers(count)[2:]
    meet(peers)


def tensor_sum_body(chunks, *refs):
    meet_tensor(0)
    run_stages([tensor_sum_stages(chunks, *refs)], ())


def seq_gather_body(count, *refs):
    device, spot, ahead, behind = seq_peers(count)
    place, pair, across = tensor_peers()
    meet((ahead, behind, {"tensor": pair}))
    run_stages([ring_gather_stages(count, True, *refs)], ())


def two_gathers_body(count, chunks, block, rows, out, all_rows, *refs):
    meet_tensor(count)
    run_stages(
        [
            ring_gather_stages(count, True, rows, all_rows, *refs[3:]),
            tensor_gather_stages(chunks, block, out, *refs[:3]),
        ],
        (0, 1, 0, 1, 1, 0),
    )


def two_sums_body(count, chunks, part, pack, total, shard, *refs):
    meet_tensor(count)
    run_stages(
        [
            tensor_sum_stages(chunks, part, total, *refs[:5]),
            ring_sum_stages(count, pack, shard, *refs[5:]),
        ],
        (0, 1, 0, 1, 1, 0, 1, 0, 1, 1, 0, 1, 0, 1),
    )


def sum_and_gather_body(count, chunks, part, block, total, out, *refs):
    meet_tensor(count)
    run_stages(
        [
            tensor_sum_stages(chunks, part, total, *refs[:5]),
            ring_gather_stages(count, False, block, out, *refs[5:], None, None),
        ],
        (0, 1, 0, 1, 0, 1, 0, 1, 0, 1, 0),
    )


DMA = pltpu.SemaphoreType.DMA


def sum_scratch(part, chunks):
    rows, cols = part.shape
    half = pltpu.VMEM((rows // 2, cols), NARROW_TYPE)
    return [half, half, half, DMA((3, chunks)), DMA((3, chunks))]


def ring_sems(count, sets):
    return [DMA(())] + [DMA((2, count // 2, 2))] * (2 * sets)


def exchange(body, name, collective_id, shapes, scratch, args):
    results = pl.pallas_call(
        body,
        in_specs=[pl.BlockSpec(memory_space=pltpu.VMEM)] * len(args),
        out_specs=[pl.BlockSpec(memory_space=pltpu.VMEM)] * len(shapes),
        out_shape=[jax.ShapeDtypeStruct(shape, NARROW_TYPE) for shape in shapes],
        scratch_shapes=scratch,
        compiler_params=pltpu.CompilerParams(
            collective_id=collective_id, has_side_effects=True, vmem_limit_bytes=VMEM_BYTES
        ),
        name=name,
    )(*args)
    return results[0] if len(shapes) == 1 else results


def tensor_sum(part, collective_id, chunks):
    body = functools.partial(tensor_sum_body, chunks)
    scratch = sum_scratch(part, chunks)
    return exchange(body, "tensor_sum", collective_id, [part.shape], scratch, [part])


def seq_gather(block, collective_id):
    rows, cols = block.shape
    count = lax.axis_size("seq")
    body = functools.partial(seq_gather_body, count)
    scratch = ring_sems(count, 2)
    return exchange(body, "seq_gather", collective_id, [(count * rows, cols)], scratch, [block])


def two_gathers(block, rows, collective_id, chunks):
    count = lax.axis_size("seq")
    shapes = [(4 * block.shape[0], block.shape[1]), (count * rows.shape[0], rows.shape[1])]
    scratch = [DMA(()), DMA((3, chunks)), DMA((3, chunks))] + ring_sems(count, 2)
    body = functools.partial(two_gathers_body, count, chunks)
    return exchange(body, "two_gathers", collective_id, shapes, scratch, [block, rows])


def two_sums(part, pack, collective_id, chunks):
    count = lax.axis_size("seq")
    rows, cols = pack.shape
    moves = count - 1
    scratch = sum_scratch(part, chunks) + [
        pltpu.VMEM((2, moves, rows // count // 2, cols), NARROW_TYPE),
        DMA((2, moves)),
        DMA((2, moves)),
    ]
    body = functools.partial(two_sums_body, count, chunks)
    shapes = [part.shape, (rows // count, cols)]
    return exchange(body, "two_sums", collective_id, shapes, scratch, [part, pack])


def sum_and_gather(part, block, collective_id, chunks):
    count = lax.axis_size("seq")
    shapes = [part.shape, (count * block.shape[0], block.shape[1])]
    scratch = sum_scratch(part, chunks) + ring_sems(count, 1)
    body = functools.partial(sum_and_gather_body, count, chunks)
    return exchange(body, "sum_and_gather", collective_id, shapes, scratch, [part, block])


def allowed_pairs(low_row, first_key, span, first_query, query_rows):
    key_pos = first_key + lax.broadcasted_iota(jnp.int32, (span, query_rows), 0)
    query_pos = first_query + lax.broadcasted_iota(jnp.int32, (span, query_rows), 1)
    return (key_pos >= low_row) & (key_pos <= query_pos)


def choose_span(counts, spans, query_rows, block, run):
    if len(spans) == 1:
        run(spans[0])
    else:
        count = counts[block]
        for span in spans:
            pl.when(count == span // query_rows)(functools.partial(run, span))


def forward_body(
    heads, query_rows, spans, offset, upright, counts, low, queries, keys, values, mixed, log_total
):
    block = pl.program_id(1)

    def run(span):
        start = pl.multiple_of(block * query_rows + query_rows + offset - span, 128)
        allowed = allowed_pairs(low[...], start, span, block * query_rows + offset, query_rows)
        rows = pl.ds(start, span)
        for head in range(heads):
            cols = slice(head * HD, (head + 1) * HD)
            scores = contract(keys[rows, cols], queries[:, cols] * SCORE_SCALE, 1, 1)
            scores = jnp.where(allowed, scores, NEGATIVE)
            top = jnp.max(scores, axis=0, keepdims=True)
            raised = jnp.exp(scores - top)
            total = jnp.sum(raised, axis=0, keepdims=True)
            mixed_head = contract(values[rows, cols], narrow(raised), 0, 0) * (1.0 / total)
            if upright:
                mixed[cols, :] = narrow(mixed_head)
            else:
                mixed[:, cols] = narrow(mixed_head.T)
            log_total[0, head : head + 1, :] = top + jnp.log(total)

    choose_span(counts, spans, query_rows, block, run)


def backward_body(
    heads,
    query_rows,
    spans,
    offset,
    upright,
    counts,
    low,
    log_total,
    queries,
    mixed,
    out_grads,
    keys,
    values,
    query_grads,
    key_grads,
    value_grads,
    key_sum,
    value_sum,
):
    block = pl.program_id(1)

    @pl.when(block == 0)
    def clear():
        key_sum[...] = jnp.zeros_like(key_sum)
        value_sum[...] = jnp.zeros_like(value_sum)

    def run(span):
        start = pl.multiple_of(block * query_rows + query_rows + offset - span, 128)
        allowed = allowed_pairs(low[...], start, span, block * query_rows + offset, query_rows)
        rows = pl.ds(start, span)
        for head in range(heads):
            cols = slice(head * HD, (head + 1) * HD)
            query = queries[:, cols] * SCORE_SCALE
            out_grad = out_grads[:, cols]
            if upright:
                overlap = wide(mixed[cols, :]) * wide(out_grad).T
            else:
                overlap = (wide(mixed[:, cols]) * wide(out_grad)).T
            inner = jnp.sum(overlap, axis=0, keepdims=True)
            key = keys[rows, cols]
            scores = contract(key, query, 1, 1)
            weights = jnp.where(allowed, jnp.exp(scores - log_total[0, head : head + 1, :]), 0.0)
            weight_grad = contract(values[rows, cols], out_grad, 1, 1)
            score_grad = narrow(weights * (weight_grad - inner))
            query_grads[:, cols] = narrow(contract(key, score_grad, 0, 0).T * SCORE_SCALE)
            key_sum[rows, cols] += contract(score_grad, query, 1, 0)
            value_sum[rows, cols] += contract(narrow(weights), out_grad, 1, 0)

    choose_span(counts, spans, query_rows, block, run)

    @pl.when(block == pl.num_programs(1) - 1)
    def finish():
        key_grads[...] = narrow(key_sum[...])
        value_grads[...] = narrow(value_sum[...])


def attend_sizes(queries, keys, spans, query_rows):
    rows, cols = queries.shape
    extent = keys.shape[0]
    group_cols = 128 if cols % 128 == 0 else cols
    groups = cols // group_cols
    heads = group_cols // HD
    count_spec = pl.BlockSpec(memory_space=pltpu.SMEM)
    low_spec = pl.BlockSpec((1, query_rows), lambda g, b: (0, b))
    row_spec = pl.BlockSpec((query_rows, group_cols), lambda g, b: (b, g))
    flat_spec = pl.BlockSpec((group_cols, query_rows), lambda g, b: (g, b))
    all_spec = pl.BlockSpec((extent, group_cols), lambda g, b: (0, g))
    log_spec = pl.BlockSpec((1, heads, query_rows), lambda g, b: (g, 0, b))
    args = (heads, query_rows, spans, extent - rows)
    log_shape = jax.ShapeDtypeStruct((groups, heads, rows), WIDE_TYPE)
    grid = (groups, rows // query_rows)
    flops = 2 * rows * spans[-1] * cols
    specs = (count_spec, low_spec, row_spec, flat_spec, all_spec, log_spec)
    return args, grid, specs, log_shape, group_cols, flops


def attend_forward(counts, low, queries, keys, values, spans, query_rows, upright):
    args, grid, specs, log_shape, unused, flops = attend_sizes(queries, keys, spans, query_rows)
    count_spec, low_spec, row_spec, flat_spec, all_spec, log_spec = specs
    mixed_shape = queries.shape[::-1] if upright else queries.shape
    return pl.pallas_call(
        functools.partial(forward_body, *args, upright),
        grid=grid,
        in_specs=[count_spec, low_spec, row_spec, all_spec, all_spec],
        out_specs=[flat_spec if upright else row_spec, log_spec],
        out_shape=[jax.ShapeDtypeStruct(mixed_shape, NARROW_TYPE), log_shape],
        compiler_params=pltpu.CompilerParams(vmem_limit_bytes=VMEM_BYTES),
        cost_estimate=pl.CostEstimate(
            flops=16 * flops, transcendentals=flops // 128, bytes_accessed=1 << 20
        ),
        name="attend_forward",
    )(counts, low, queries, keys, values)


def attend_backward(
    counts, low, log_total, queries, mixed, out_grads, keys, values, spans, query_rows, upright
):
    args, grid, specs, unused, group_cols, flops = attend_sizes(queries, keys, spans, query_rows)
    count_spec, low_spec, row_spec, flat_spec, all_spec, log_spec = specs
    mixed_spec = flat_spec if upright else row_spec
    key_shape = jax.ShapeDtypeStruct(keys.shape, NARROW_TYPE)
    return pl.pallas_call(
        functools.partial(backward_body, *args, upright),
        grid=grid,
        in_specs=[
            count_spec, low_spec, log_spec, row_spec, mixed_spec, row_spec, all_spec, all_spec
        ],
        out_specs=[row_spec, all_spec, all_spec],
        out_shape=[jax.ShapeDtypeStruct(queries.shape, NARROW_TYPE), key_shape, key_shape],
        scratch_shapes=[pltpu.VMEM((keys.shape[0], group_cols), WIDE_TYPE)] * 2,
        compiler_params=pltpu.CompilerParams(vmem_limit_bytes=VMEM_BYTES),
        cost_estimate=pl.CostEstimate(
            flops=(1 if upright else 20) * flops,
            transcendentals=0 if upright else flops // 128,
            bytes_accessed=1 << 10 if upright else 1 << 20,
        ),
        name="attend_backward",
    )(counts, low, log_total, queries, mixed, out_grads, keys, values)


def together(*values):
    return lax.optimization_barrier(values)


def in_blocks(function, rows, block_rows):
    if rows <= block_rows:
        return function(0)
    starts = jnp.arange(rows // block_rows, dtype=jnp.int32) * block_rows
    return lax.map(function, starts).reshape(rows, -1)


def on_device(
    stream,
    cotangent,
    boundary,
    counts,
    attend_gain,
    attend_input,
    attend_output,
    byte_gain,
    byte_up,
    byte_down,
    patch_gain,
    patch_input,
    patch_output,
    dense_gain,
    dense_up,
    dense_down,
):
    tok_rows, width = stream.shape
    head_cols = attend_input.shape[2]
    big_width = patch_input.shape[0]
    patch_cols = patch_input.shape[2]
    item_count = counts.shape[0]
    seq_devices = lax.axis_size("seq")
    device = lax.axis_index("seq")
    capacity = tok_rows // 4
    total_rows = seq_devices * capacity // 2
    owned_rows = total_rows // seq_devices
    item_cap = DEV_ITEM * capacity
    query_rows = min(256, tok_rows)

    per_device = counts.reshape(-1)
    ends = jnp.cumsum(per_device)
    offsets = ends - per_device
    item_begin = offsets.reshape(item_count, DEV_ITEM)[:, 0]
    my_first = offsets[device]
    rank_local = jnp.cumsum(boundary) - 1
    target = jnp.where(boundary == 1, rank_local, -1)
    send_map = narrow(jnp.arange(capacity)[:, None] == target[None, :])
    rank = jnp.arange(total_rows, dtype=jnp.int32)
    rank_device = jnp.sum(rank[:, None] >= ends[None, :], axis=1)
    rank_start = jnp.sum(
        jnp.where(rank_device[:, None] == jnp.arange(seq_devices)[None, :], offsets[None, :], 0),
        axis=1,
    )
    rank_slot = rank_device * capacity + rank - rank_start
    rank_low = jnp.max(
        jnp.where(rank[:, None] >= item_begin[None, :], item_begin[None, :], 0), axis=1
    )
    rank_low = rank_low[None, :].astype(jnp.int32)
    slot_rows = seq_devices * capacity

    def compact_rows(slots, first_row, block_rows):
        places = lax.dynamic_slice_in_dim(rank_slot, first_row, block_rows, 0)
        take_map = narrow(places[:, None] == jnp.arange(slot_rows)[None, :])
        return narrow(product(take_map, slots))

    def compact(slots):
        block_rows = min(1024, total_rows)
        return in_blocks(
            lambda first_row: compact_rows(slots, first_row, block_rows), total_rows, block_rows
        )

    def my_slots(table):
        padded = jnp.pad(table, ((0, capacity), (0, 0)))
        return lax.dynamic_slice_in_dim(padded, my_first, capacity, 0)

    def my_block(table):
        return lax.dynamic_slice_in_dim(table, device * owned_rows, owned_rows, 0)

    with jax.named_scope("byte_attend"):
        stream_value = wide(stream)
        normed = narrow(rms_scale(stream_value, attend_gain))
        in_matrix = attend_input.reshape(width, 3 * head_cols)
        projected = narrow(product(normed, in_matrix))
        queries = projected[:, :head_cols]
        key_value = projected[:, head_cols:]
        need_list = []
        while sum(need_list) < WIN:
            need_list.append(min(tok_rows, WIN - sum(need_list)))
        arrived_list = []
        for step, need_rows in enumerate(need_list):
            arrived_list.append(from_behind(key_value[tok_rows - need_rows :], "seq", step + 1))
        extended = jnp.concatenate(arrived_list[::-1] + [key_value], axis=0)
        delta_slots = narrow(product(send_map, cotangent))
        keys = extended[:, :head_cols]
        values = extended[:, head_cols:]
        window_low = jnp.maximum(
            jnp.arange(tok_rows, dtype=jnp.int32) + 1, WIN - device * tok_rows
        )[None, :]
        window_spans = (WIN + query_rows,)
        window_counts = jnp.zeros((tok_rows // query_rows,), jnp.int32)
        mixed_heads, window_log = attend_forward(
            window_counts, window_low, queries, keys, values, window_spans, query_rows, True
        )
        all_mixed, all_slots = two_gathers(mixed_heads, delta_slots, 0, 2)
        all_output = lax.all_gather(attend_output, "tensor", axis=0, tiled=True)
        after_attend = stream_value + transposed_times(all_mixed, all_output)

    with jax.named_scope("byte_feed"):
        normed_two = narrow(rms_scale(after_attend, byte_gain))
        gate_pre = product(normed_two, byte_up)
        activated = narrow(gelu_tanh(gate_pre))
        feed_part = narrow(product(activated, byte_down))

    with jax.named_scope("patch_rows"):
        attend_high = narrow(after_attend)
        attend_rest = narrow(after_attend - wide(attend_high))
        rows_sum = wide(tensor_sum(narrow(product(send_map, feed_part)), 1, 4))
        rows_here = narrow(
            product(send_map, attend_high) + product(send_map, attend_rest) + rows_sum
        )
        byte_rows = compact(seq_gather(rows_here, 2))

    with jax.named_scope("cotangent_rows"):
        delta_own = compact_rows(all_slots, device * owned_rows, owned_rows)

    wide_pad = ((0, 0), (0, big_width - width))
    with jax.named_scope("patch_attend"):
        normed_three = narrow(rms_scale(wide(jnp.pad(byte_rows, wide_pad)), patch_gain))
        patch_matrix = patch_input.reshape(big_width, 3 * patch_cols)
        patch_projected = narrow(product(normed_three, patch_matrix))
        patch_queries = patch_projected[:, :patch_cols]
        patch_keys = patch_projected[:, patch_cols : 2 * patch_cols]
        patch_values = patch_projected[:, 2 * patch_cols :]
        patch_query_rows = min(256, total_rows)
        most_blocks = min(total_rows, item_cap + patch_query_rows) // patch_query_rows
        patch_spans = tuple(patch_query_rows * (blocks + 1) for blocks in range(most_blocks))
        patch_counts = (
            jnp.arange(total_rows // patch_query_rows, dtype=jnp.int32)
            + 1
            - rank_low[0, ::patch_query_rows] // patch_query_rows
        )
        mixed_patch, patch_log = attend_forward(
            patch_counts,
            rank_low,
            patch_queries,
            patch_keys,
            patch_values,
            patch_spans,
            patch_query_rows,
            False,
        )
        branch_own = wide(tensor_sum(narrow(product(my_block(mixed_patch), patch_output)), 3, 4))

    with jax.named_scope("patch_dense"):
        own_rows = wide(jnp.pad(my_block(byte_rows), wide_pad))
        after_patch = own_rows + branch_own
        normed_four = narrow(rms_scale(after_patch, dense_gain))
        dense_pre = product(normed_four, dense_up)
        dense_pre_grad = narrow(gelu_back(dense_pre, times_transposed(delta_own, dense_down)))
        normed_four_grad = wide(tensor_sum(narrow(times_transposed(dense_pre_grad, dense_up)), 4, 4))
        after_patch_grad, densegain_grad = norm_back(after_patch, dense_gain, normed_four_grad)
        branch_grad_own = narrow(after_patch_grad + wide(jnp.pad(delta_own, wide_pad)))
        branch_grad, normed_later = together(seq_gather(branch_grad_own, 5), normed_four)
        all_normed = lax.all_gather(normed_later, "seq", axis=0, tiled=True)

    with jax.named_scope("patch_attend_back"):
        mixed_patch_grad = narrow(times_transposed(branch_grad, patch_output))
        patch_projected_grad = jnp.concatenate(
            attend_backward(
                patch_counts,
                rank_low,
                patch_log,
                patch_queries,
                mixed_patch,
                mixed_patch_grad,
                patch_keys,
                patch_values,
                patch_spans,
                patch_query_rows,
                False,
            ),
            axis=1,
        )
        normed_three_grad = times_transposed(my_slots(patch_projected_grad), patch_matrix)
        normed_three_grad = wide(tensor_sum(narrow(normed_three_grad), 6, 4))
        patch_norm_grad, patchgain_grad = norm_back(
            wide(jnp.pad(rows_here, wide_pad)), patch_gain, normed_three_grad
        )
        rows_grad = narrow(wide(my_slots(branch_grad[:, :width])) + patch_norm_grad[:, :width])

    with jax.named_scope("byte_feed_back"):
        feed_grad = narrow(
            jnp.where(
                boundary[:, None] == 1,
                transposed_times(send_map, rows_grad),
                wide(cotangent),
            )
        )
        activated_grad = times_transposed(feed_grad, byte_down)
        gate_grad = narrow(gelu_back(gate_pre, activated_grad))
        bytedown_grad = transposed_times(activated, feed_grad)
        byteup_grad = transposed_times(normed_two, gate_grad)
        feed_pack = narrow(jnp.concatenate([byteup_grad, bytedown_grad], axis=1))
        normed_two_part = narrow(times_transposed(gate_grad, byte_up))
        feed_pack, normed_two_part, all_normed = together(feed_pack, normed_two_part, all_normed)
        feed_part_sum = lax.psum_scatter(feed_pack, "seq", scatter_dimension=0, tiled=True)
        normed_two_grad = wide(tensor_sum(normed_two_part, 7, 4))
        feed_norm_grad, bytegain_grad = norm_back(after_attend, byte_gain, normed_two_grad)
        after_attend_grad = wide(feed_grad) + feed_norm_grad

    with jax.named_scope("byte_attend_back"):
        attend_branch_grad = narrow(after_attend_grad)
        attendoutput_grad = product(mixed_heads, attend_branch_grad)
        mixed_heads_grad = narrow(times_transposed(attend_branch_grad, attend_output))
        query_grad, key_grad, value_grad = attend_backward(
            window_counts,
            window_low,
            window_log,
            queries,
            mixed_heads,
            mixed_heads_grad,
            keys,
            values,
            window_spans,
            query_rows,
            True,
        )
        pair_grad = jnp.concatenate([key_grad, value_grad], axis=1)
        pair_grad, all_normed, later_slots, later_branch, later_projected = together(
            pair_grad, all_normed, all_slots, branch_grad, patch_projected_grad
        )
        patchoutput_grad = transposed_times(mixed_patch, later_branch)
        patchinput_grad = transposed_times(normed_three, later_projected)
        patchinput_grad = patchinput_grad.reshape(big_width, 3, patch_cols)
        begin_row = WIN
        returned_list = []
        for step, need_rows in enumerate(need_list):
            begin_row = begin_row - need_rows
            returned_list.append(
                from_behind(pair_grad[begin_row : begin_row + need_rows], "seq", -step - 1)
            )

    with jax.named_scope("dense_weights"):
        block_rows = min(1024, total_rows)

        delta_grad = compact(later_slots)
        delta_grad, patchoutput_grad, patchinput_grad, feed_part_sum = together(
            delta_grad, patchoutput_grad, patchinput_grad, feed_part_sum
        )

        def dense_parts(first_row):
            some_normed = lax.dynamic_slice_in_dim(all_normed, first_row, block_rows, 0)
            some_delta = lax.dynamic_slice_in_dim(delta_grad, first_row, block_rows, 0)
            some_pre = product(some_normed, dense_up)
            some_act = narrow(gelu_tanh(some_pre))
            some_grad = narrow(gelu_back(some_pre, times_transposed(some_delta, dense_down)))
            return some_normed, some_delta, some_act, some_grad

        if total_rows == block_rows:
            some_normed, some_delta, dense_act, dense_grad = dense_parts(0)
            densedown_grad = transposed_times(dense_act, some_delta)
            denseup_grad = transposed_times(some_normed, dense_grad)
        else:

            def dense_step(sums, first_row):
                some_normed, some_delta, some_act, some_grad = dense_parts(first_row)
                down_sum = sums[0] + transposed_times(some_act, some_delta)
                up_sum = sums[1] + transposed_times(some_normed, some_grad)
                return (down_sum, up_sum), some_act

            starts = jnp.arange(total_rows // block_rows, dtype=jnp.int32) * block_rows
            initial = (jnp.zeros(dense_down.shape), jnp.zeros(dense_up.shape))
            (densedown_grad, denseup_grad), dense_act = lax.scan(dense_step, initial, starts)
            dense_act = dense_act.reshape(total_rows, -1)

        returned_list, dense_act, densedown_grad, denseup_grad = together(
            returned_list, dense_act, densedown_grad, denseup_grad
        )

    with jax.named_scope("byte_attend_sum"):
        own_grad = wide(pair_grad[WIN:])
        for need_rows, returned in zip(need_list, returned_list):
            own_grad = own_grad.at[tok_rows - need_rows :].add(wide(returned))
        projected_grad = jnp.concatenate([query_grad, narrow(own_grad)], axis=1)
        attendinput_grad = transposed_times(normed, projected_grad)
        attend_pack = narrow(jnp.concatenate([attendinput_grad, attendoutput_grad.T], axis=1))
        normed_part = narrow(times_transposed(projected_grad, in_matrix))
        attend_pack, normed_part = together(attend_pack, normed_part)
        pack_rows = width // seq_devices
        ring_fits = pack_rows % 32 == 0
        if ring_fits:
            normed_grad, attend_part = two_sums(normed_part, attend_pack, 8, 4)
        else:
            normed_grad = tensor_sum(normed_part, 8, 4)
            attend_part = lax.psum_scatter(attend_pack, "seq", scatter_dimension=0, tiled=True)
        normed_grad = wide(normed_grad)
        stream_norm_grad, attendgain_grad = norm_back(stream_value, attend_gain, normed_grad)
        inflow = narrow(after_attend_grad + stream_norm_grad)

    with jax.named_scope("result"):
        delta_part = product(my_slots(mixed_patch), patch_output[:, :width])
        delta_part = narrow(delta_part + product(my_slots(dense_act), dense_down))
        result_part = wide(feed_part) + transposed_times(send_map, delta_part)
        gains = jnp.concatenate([attendgain_grad, bytegain_grad, patchgain_grad, densegain_grad])
        gains = gains.reshape(-1, width)
        gain_rows = gains.shape[0]
        gains = narrow(jnp.pad(gains, ((0, 32 - gain_rows), (0, 0))))
        attend_block = jnp.concatenate([attend_part, gains], axis=0)
        result_part, feed_sum = together(
            narrow(result_part), lax.all_gather(feed_part_sum, "seq", axis=0, tiled=True)
        )
        if ring_fits:
            result_sum, attend_sum = sum_and_gather(result_part, attend_block, 9, 4)
        else:
            result_sum = tensor_sum(result_part, 9, 4)
            attend_sum = lax.all_gather(attend_block, "seq", axis=0, tiled=True)
        result = narrow(after_attend + wide(result_sum))

    with jax.named_scope("weight_sums"):
        feed_sum = wide(feed_sum)
        hidden = byte_up.shape[1]
        byteup_grad = feed_sum[:, :hidden]
        bytedown_grad = feed_sum[:, hidden:]
        attend_sum = wide(attend_sum).reshape(seq_devices, -1, width)
        gains = jnp.sum(attend_sum[:, pack_rows : pack_rows + gain_rows], axis=0).reshape(-1)
        attend_sum = attend_sum[:, :pack_rows].reshape(width, width)
        attendinput_grad = attend_sum[:, : 3 * head_cols].reshape(width, 3, head_cols)
        attendoutput_grad = attend_sum[:, 3 * head_cols :].T
        attendgain_grad = gains[:width]
        bytegain_grad = gains[width : 2 * width]
        patchgain_grad = gains[2 * width : 2 * width + big_width]
        densegain_grad = gains[2 * width + big_width :]

    return (
        result,
        inflow,
        attendgain_grad,
        attendinput_grad,
        attendoutput_grad,
        bytegain_grad,
        byteup_grad,
        bytedown_grad,
        patchgain_grad,
        patchinput_grad,
        patchoutput_grad,
        densegain_grad,
        denseup_grad,
        densedown_grad,
    )


def solution(mesh):
    in_specs = (
        P("seq", None),
        P("seq", None),
        P("seq"),
        P(),
        P(),
        P(None, None, "tensor"),
        P("tensor", None),
        P(),
        P(None, "tensor"),
        P("tensor", None),
        P(),
        P(None, None, "tensor"),
        P("tensor", None),
        P(),
        P(None, "tensor"),
        P("tensor", None),
    )
    out_specs = (
        P("seq", None),
        P("seq", None),
        P(),
        P(None, None, "tensor"),
        P("tensor", None),
        P(),
        P(None, "tensor"),
        P("tensor", None),
        P(),
        P(None, None, "tensor"),
        P("tensor", None),
        P(),
        P(None, "tensor"),
        P("tensor", None),
    )
    return jax.shard_map(
        on_device, mesh=mesh, in_specs=in_specs, out_specs=out_specs, check_vma=False
    )
```

```python
import functools

import jax
import jax.numpy as jnp
from jax import lax
from jax.experimental import pallas as pl
from jax.experimental.pallas import tpu as pltpu
from jax.sharding import PartitionSpec as P

HD = 64
WIN = 1536
DEV_ITEM = 4

EPSILON = 1e-06
NEGATIVE = -1e30
SCORE_SCALE = HD ** (-0.5)
WIDE_TYPE = jnp.float32
NARROW_TYPE = jnp.bfloat16
VMEM_BYTES = 48 << 20
MESH = pl.DeviceIdType.MESH


def from_behind(value, axis, steps):
    count = lax.axis_size(axis)
    initial, last = (max(0, -steps), min(count, count - steps))
    return lax.ppermute(value, axis, [(source, source + steps) for source in range(initial, last)])


def rms_scale(values, scaling):
    return values * lax.rsqrt(jnp.mean(values * values, axis=-1, keepdims=True) + EPSILON) * scaling


def gelu_tanh(values):
    return jax.nn.gelu(values, approximate=True)


def norm_back(values, scaling, upstream):
    unused, pullback = jax.vjp(rms_scale, values, scaling)
    return pullback(upstream)


def gelu_back(values, upstream):
    unused, pullback = jax.vjp(gelu_tanh, values)
    return pullback(upstream)[0]


def contract(left_side, right_side, left_axis, right_axis):
    return lax.dot_general(
        left_side,
        right_side,
        (((left_axis,), (right_axis,)), ((), ())),
        preferred_element_type=WIDE_TYPE,
    )


def product(left_side, right_side):
    return contract(left_side, right_side, 1, 0)


def times_transposed(left_side, right_side):
    return contract(left_side, right_side, 1, 1)


def transposed_times(left_side, right_side):
    return contract(left_side, right_side, 0, 0)


def wide(values):
    return values.astype(WIDE_TYPE)


def narrow(values):
    return values.astype(NARROW_TYPE)


def meet(peers):
    barrier = pltpu.get_barrier_semaphore()
    for peer in peers:
        pl.semaphore_signal(barrier, inc=1, device_id=peer, device_id_type=MESH)
    pl.semaphore_wait(barrier, len(peers))


def tensor_peers():
    place = lax.axis_index("tensor")
    pair = place + 1 - 2 * (place % 2)
    across = (place + 2) % 4
    return place, pair, across


def remote(source, target, send_sem, recv_sem, peer):
    return pltpu.make_async_remote_copy(
        src_ref=source,
        dst_ref=target,
        send_sem=send_sem,
        recv_sem=recv_sem,
        device_id=peer,
        device_id_type=MESH,
    )


def seq_peers(count):
    device = lax.axis_index("seq")
    spot = ring_spot(device, count)
    ahead = {"seq": ring_at((spot + 1) % count, count)}
    behind = {"seq": ring_at((spot + count - 1) % count, count)}
    return device, spot, ahead, behind


def ring_at(spot, count):
    half = spot // (count // 2)
    return (1 - half) * 2 * spot + half * (2 * (count - 1 - spot) + 1)


def ring_spot(device, count):
    return device // 2 + (device % 2) * (count - 1 - 2 * (device // 2))


def run_stages(transfers, pattern):
    for index in pattern:
        next(transfers[index], None)
    for transfer in transfers:
        for unused in transfer:
            pass


def tensor_sum_stages(chunks, part, total, pair_got, mine, across_got, send_sem, recv_sem):
    place, pair, across = tensor_peers()
    pair_id = {"tensor": pair}
    across_id = {"tensor": across}
    rows = part.shape[0] // 2
    step = rows // chunks
    core = place % 2

    def piece(half, chunk):
        return pl.ds(pl.multiple_of(half * rows + chunk * step, 16), step)

    given = []
    for chunk in range(chunks):
        copy = remote(
            part.at[piece(1 - core, chunk)],
            pair_got.at[pl.ds(chunk * step, step)],
            send_sem.at[0, chunk],
            recv_sem.at[0, chunk],
            pair_id,
        )
        copy.start()
        given.append(copy)
    yield
    far = []
    for chunk in range(chunks):
        given[chunk].wait_recv()
        here = pl.ds(chunk * step, step)
        mine[here] = narrow(wide(part[piece(core, chunk)]) + wide(pair_got[here]))
        copy = remote(
            mine.at[here],
            across_got.at[here],
            send_sem.at[1, chunk],
            recv_sem.at[1, chunk],
            across_id,
        )
        copy.start()
        far.append(copy)
    yield
    back = []
    for chunk in range(chunks):
        far[chunk].wait_recv()
        here = pl.ds(chunk * step, step)
        own = piece(core, chunk)
        total[own] = narrow(wide(mine[here]) + wide(across_got[here]))
        copy = remote(
            total.at[own],
            total.at[own],
            send_sem.at[2, chunk],
            recv_sem.at[2, chunk],
            pair_id,
        )
        copy.start()
        back.append(copy)
        yield
    for copy in back:
        copy.wait_recv()
    for copy in given + far + back:
        copy.wait_send()


def tensor_gather_stages(chunks, block, out, local_sem, send_sem, recv_sem):
    place, pair, across = tensor_peers()
    pair_id = {"tensor": pair}
    across_id = {"tensor": across}
    rows = block.shape[0]
    step = rows // chunks

    def piece(owner, chunk):
        return pl.ds(pl.multiple_of(owner * rows + chunk * step, 16), step)

    copies = []
    for kind, peer in ((0, across_id), (1, pair_id)):
        for chunk in range(chunks):
            copy = remote(
                block.at[pl.ds(chunk * step, step)],
                out.at[piece(place, chunk)],
                send_sem.at[kind, chunk],
                recv_sem.at[kind, chunk],
                peer,
            )
            copy.start()
            copies.append(copy)
    local = pltpu.make_async_copy(block, out.at[pl.ds(pl.multiple_of(place * rows, 16), rows)], local_sem)
    local.start()
    yield
    passed = []
    for chunk in range(chunks):
        copies[chunk].wait_recv()
        copy = remote(
            out.at[piece(across, chunk)],
            out.at[piece(across, chunk)],
            send_sem.at[2, chunk],
            recv_sem.at[2, chunk],
            pair_id,
        )
        copy.start()
        passed.append(copy)
        yield
    local.wait()
    for chunk in range(chunks):
        copies[chunks + chunk].wait_recv()
        passed[chunk].wait_recv()
    for copy in copies + passed:
        copy.wait_send()


def ring_gather_stages(
    count, shared, block, out, local_sem, ring_send, ring_recv, pair_send, pair_recv
):
    device, spot, ahead, behind = seq_peers(count)
    place, pair, across = tensor_peers()
    pair_id = {"tensor": pair}
    rows = block.shape[0]
    step = rows // (4 if shared else 2)
    first = (place % 2) * 2 * step if shared else 0

    def piece(owner, sub):
        return pl.ds(pl.multiple_of(owner * rows + first + sub * step, 16), step)

    hops = count // 2
    sends = []
    moves = {}

    def owner_at(way, distance):
        if way == 0:
            return ring_at((spot + count - distance) % count, count)
        return ring_at((spot + distance) % count, count)

    def launch(way, hop, sub):
        owner = owner_at(way, hop - 1)
        if hop == 1:
            source = block.at[pl.ds(pl.multiple_of(first + sub * step, 16), step)]
        else:
            source = out.at[piece(owner, sub)]
        copy = remote(
            source,
            out.at[piece(owner, sub)],
            ring_send.at[way, hop - 1, sub],
            ring_recv.at[way, hop - 1, sub],
            (ahead, behind)[way],
        )
        copy.start()
        moves[way, hop, sub] = copy
        sends.append(copy)

    order = ((0, 0), (1, 1), (0, 1), (1, 0))
    for way, sub in order:
        launch(way, 1, sub)
    local = pltpu.make_async_copy(
        block, out.at[pl.ds(pl.multiple_of(device * rows, 16), rows)], local_sem
    )
    local.start()
    yield
    pairs = []
    for hop in range(1, hops + 1):
        for way, sub in order:
            if hop == hops and way != sub:
                continue
            moves[way, hop, sub].wait_recv()
            if hop + 1 < hops or (hop + 1 == hops and way == sub):
                launch(way, hop + 1, sub)
            if shared:
                owner = owner_at(way, hop)
                copy = remote(
                    out.at[piece(owner, sub)],
                    out.at[piece(owner, sub)],
                    pair_send.at[way, hop - 1, sub],
                    pair_recv.at[way, hop - 1, sub],
                    pair_id,
                )
                copy.start()
                pairs.append(copy)
        yield
    local.wait()
    for copy in pairs:
        copy.wait_recv()
    for copy in sends + pairs:
        copy.wait_send()


def ring_sum_stages(count, part, shard, arrived, send_sem, recv_sem):
    device, spot, ahead, behind = seq_peers(count)
    rows = part.shape[0] // count
    half = rows // 2
    moves = {}

    def piece(distance, way):
        owner = ring_at((spot + count - distance if way == 0 else spot + distance) % count, count)
        return pl.ds(pl.multiple_of(owner * rows + way * half, 16), half)

    def launch(way, step, source):
        copy = remote(
            source,
            arrived.at[way, step],
            send_sem.at[way, step],
            recv_sem.at[way, step],
            (ahead, behind)[way],
        )
        copy.start()
        moves[way, step] = copy

    for way in range(2):
        launch(way, 0, part.at[piece(1, way)])
    yield
    for step in range(count - 1):
        for way in range(2):
            moves[way, step].wait_recv()
            summed = wide(part[piece(step + 2, way)]) + wide(arrived[way, step])
            if step < count - 2:
                arrived[way, step] = narrow(summed)
                launch(way, step + 1, arrived.at[way, step])
            else:
                shard[pl.ds(way * half, half)] = narrow(summed)
        yield
    for copy in moves.values():
        copy.wait_send()


def meet_tensor(count):
    place, pair, across = tensor_peers()
    peers = [{"tensor": pair}, {"tensor": across}]
    if count:
        peers += seq_peers(count)[2:]
    meet(peers)


def tensor_sum_body(chunks, *refs):
    meet_tensor(0)
    run_stages([tensor_sum_stages(chunks, *refs)], ())


def seq_gather_body(count, *refs):
    device, spot, ahead, behind = seq_peers(count)
    place, pair, across = tensor_peers()
    meet((ahead, behind, {"tensor": pair}))
    run_stages([ring_gather_stages(count, True, *refs)], ())


def two_gathers_body(count, chunks, block, rows, out, all_rows, *refs):
    meet_tensor(count)
    run_stages(
        [
            ring_gather_stages(count, True, rows, all_rows, *refs[3:]),
            tensor_gather_stages(chunks, block, out, *refs[:3]),
        ],
        (0, 1, 0, 1, 1, 0),
    )


def two_sums_body(count, chunks, part, pack, total, shard, *refs):
    meet_tensor(count)
    run_stages(
        [
            tensor_sum_stages(chunks, part, total, *refs[:5]),
            ring_sum_stages(count, pack, shard, *refs[5:]),
        ],
        (0, 1, 0, 1, 1, 0, 1, 0, 1, 1, 0, 1, 0, 1),
    )


def sum_and_gather_body(count, chunks, part, block, total, out, *refs):
    meet_tensor(count)
    run_stages(
        [
            tensor_sum_stages(chunks, part, total, *refs[:5]),
            ring_gather_stages(count, False, block, out, *refs[5:], None, None),
        ],
        (0, 1, 0, 1, 0, 1, 0, 1, 0, 1, 0),
    )


DMA = pltpu.SemaphoreType.DMA


def sum_scratch(part, chunks):
    rows, cols = part.shape
    half = pltpu.VMEM((rows // 2, cols), NARROW_TYPE)
    return [half, half, half, DMA((3, chunks)), DMA((3, chunks))]


def ring_sems(count, sets):
    return [DMA(())] + [DMA((2, count // 2, 2))] * (2 * sets)


def exchange(body, name, collective_id, shapes, scratch, args):
    results = pl.pallas_call(
        body,
        in_specs=[pl.BlockSpec(memory_space=pltpu.VMEM)] * len(args),
        out_specs=[pl.BlockSpec(memory_space=pltpu.VMEM)] * len(shapes),
        out_shape=[jax.ShapeDtypeStruct(shape, NARROW_TYPE) for shape in shapes],
        scratch_shapes=scratch,
        compiler_params=pltpu.CompilerParams(
            collective_id=collective_id, has_side_effects=True, vmem_limit_bytes=VMEM_BYTES
        ),
        name=name,
    )(*args)
    return results[0] if len(shapes) == 1 else results


def tensor_sum(part, collective_id, chunks):
    body = functools.partial(tensor_sum_body, chunks)
    scratch = sum_scratch(part, chunks)
    return exchange(body, "tensor_sum", collective_id, [part.shape], scratch, [part])


def seq_gather(block, collective_id):
    rows, cols = block.shape
    count = lax.axis_size("seq")
    body = functools.partial(seq_gather_body, count)
    scratch = ring_sems(count, 2)
    return exchange(body, "seq_gather", collective_id, [(count * rows, cols)], scratch, [block])


def two_gathers(block, rows, collective_id, chunks):
    count = lax.axis_size("seq")
    shapes = [(4 * block.shape[0], block.shape[1]), (count * rows.shape[0], rows.shape[1])]
    scratch = [DMA(()), DMA((3, chunks)), DMA((3, chunks))] + ring_sems(count, 2)
    body = functools.partial(two_gathers_body, count, chunks)
    return exchange(body, "two_gathers", collective_id, shapes, scratch, [block, rows])


def two_sums(part, pack, collective_id, chunks):
    count = lax.axis_size("seq")
    rows, cols = pack.shape
    moves = count - 1
    scratch = sum_scratch(part, chunks) + [
        pltpu.VMEM((2, moves, rows // count // 2, cols), NARROW_TYPE),
        DMA((2, moves)),
        DMA((2, moves)),
    ]
    body = functools.partial(two_sums_body, count, chunks)
    shapes = [part.shape, (rows // count, cols)]
    return exchange(body, "two_sums", collective_id, shapes, scratch, [part, pack])


def sum_and_gather(part, block, collective_id, chunks):
    count = lax.axis_size("seq")
    shapes = [part.shape, (count * block.shape[0], block.shape[1])]
    scratch = sum_scratch(part, chunks) + ring_sems(count, 1)
    body = functools.partial(sum_and_gather_body, count, chunks)
    return exchange(body, "sum_and_gather", collective_id, shapes, scratch, [part, block])


def allowed_pairs(low_row, first_key, span, first_query, query_rows):
    key_pos = first_key + lax.broadcasted_iota(jnp.int32, (span, query_rows), 0)
    query_pos = first_query + lax.broadcasted_iota(jnp.int32, (span, query_rows), 1)
    return (key_pos >= low_row) & (key_pos <= query_pos)


def choose_span(counts, spans, query_rows, block, run):
    if len(spans) == 1:
        run(spans[0])
    else:
        count = counts[block]
        for span in spans:
            pl.when(count == span // query_rows)(functools.partial(run, span))


def forward_body(
    heads, query_rows, spans, offset, upright, counts, low, queries, keys, values, mixed, log_total
):
    block = pl.program_id(1)

    def run(span):
        start = pl.multiple_of(block * query_rows + query_rows + offset - span, 128)
        allowed = allowed_pairs(low[...], start, span, block * query_rows + offset, query_rows)
        rows = pl.ds(start, span)
        for head in range(heads):
            cols = slice(head * HD, (head + 1) * HD)
            scores = contract(keys[rows, cols], queries[:, cols] * SCORE_SCALE, 1, 1)
            scores = jnp.where(allowed, scores, NEGATIVE)
            top = jnp.max(scores, axis=0, keepdims=True)
            raised = jnp.exp(scores - top)
            total = jnp.sum(raised, axis=0, keepdims=True)
            mixed_head = contract(values[rows, cols], narrow(raised), 0, 0) * (1.0 / total)
            if upright:
                mixed[cols, :] = narrow(mixed_head)
            else:
                mixed[:, cols] = narrow(mixed_head.T)
            log_total[0, head : head + 1, :] = top + jnp.log(total)

    choose_span(counts, spans, query_rows, block, run)


def backward_body(
    heads,
    query_rows,
    spans,
    offset,
    upright,
    counts,
    low,
    log_total,
    queries,
    mixed,
    out_grads,
    keys,
    values,
    query_grads,
    key_grads,
    value_grads,
    key_sum,
    value_sum,
):
    block = pl.program_id(1)

    @pl.when(block == 0)
    def clear():
        key_sum[...] = jnp.zeros_like(key_sum)
        value_sum[...] = jnp.zeros_like(value_sum)

    def run(span):
        start = pl.multiple_of(block * query_rows + query_rows + offset - span, 128)
        allowed = allowed_pairs(low[...], start, span, block * query_rows + offset, query_rows)
        rows = pl.ds(start, span)
        for head in range(heads):
            cols = slice(head * HD, (head + 1) * HD)
            query = queries[:, cols] * SCORE_SCALE
            out_grad = out_grads[:, cols]
            if upright:
                overlap = wide(mixed[cols, :]) * wide(out_grad).T
            else:
                overlap = (wide(mixed[:, cols]) * wide(out_grad)).T
            inner = jnp.sum(overlap, axis=0, keepdims=True)
            key = keys[rows, cols]
            scores = contract(key, query, 1, 1)
            weights = jnp.where(allowed, jnp.exp(scores - log_total[0, head : head + 1, :]), 0.0)
            weight_grad = contract(values[rows, cols], out_grad, 1, 1)
            score_grad = narrow(weights * (weight_grad - inner))
            query_grads[:, cols] = narrow(contract(key, score_grad, 0, 0).T * SCORE_SCALE)
            key_sum[rows, cols] += contract(score_grad, query, 1, 0)
            value_sum[rows, cols] += contract(narrow(weights), out_grad, 1, 0)

    choose_span(counts, spans, query_rows, block, run)

    @pl.when(block == pl.num_programs(1) - 1)
    def finish():
        key_grads[...] = narrow(key_sum[...])
        value_grads[...] = narrow(value_sum[...])


def attend_sizes(queries, keys, spans, query_rows):
    rows, cols = queries.shape
    extent = keys.shape[0]
    group_cols = 128 if cols % 128 == 0 else cols
    groups = cols // group_cols
    heads = group_cols // HD
    count_spec = pl.BlockSpec(memory_space=pltpu.SMEM)
    low_spec = pl.BlockSpec((1, query_rows), lambda g, b: (0, b))
    row_spec = pl.BlockSpec((query_rows, group_cols), lambda g, b: (b, g))
    flat_spec = pl.BlockSpec((group_cols, query_rows), lambda g, b: (g, b))
    all_spec = pl.BlockSpec((extent, group_cols), lambda g, b: (0, g))
    log_spec = pl.BlockSpec((1, heads, query_rows), lambda g, b: (g, 0, b))
    args = (heads, query_rows, spans, extent - rows)
    log_shape = jax.ShapeDtypeStruct((groups, heads, rows), WIDE_TYPE)
    grid = (groups, rows // query_rows)
    flops = 2 * rows * spans[-1] * cols
    specs = (count_spec, low_spec, row_spec, flat_spec, all_spec, log_spec)
    return args, grid, specs, log_shape, group_cols, flops


def attend_forward(counts, low, queries, keys, values, spans, query_rows, upright):
    args, grid, specs, log_shape, unused, flops = attend_sizes(queries, keys, spans, query_rows)
    count_spec, low_spec, row_spec, flat_spec, all_spec, log_spec = specs
    mixed_shape = queries.shape[::-1] if upright else queries.shape
    return pl.pallas_call(
        functools.partial(forward_body, *args, upright),
        grid=grid,
        in_specs=[count_spec, low_spec, row_spec, all_spec, all_spec],
        out_specs=[flat_spec if upright else row_spec, log_spec],
        out_shape=[jax.ShapeDtypeStruct(mixed_shape, NARROW_TYPE), log_shape],
        compiler_params=pltpu.CompilerParams(vmem_limit_bytes=VMEM_BYTES),
        cost_estimate=pl.CostEstimate(
            flops=16 * flops, transcendentals=flops // 128, bytes_accessed=1 << 20
        ),
        name="attend_forward",
    )(counts, low, queries, keys, values)


def attend_backward(
    counts, low, log_total, queries, mixed, out_grads, keys, values, spans, query_rows, upright
):
    args, grid, specs, unused, group_cols, flops = attend_sizes(queries, keys, spans, query_rows)
    count_spec, low_spec, row_spec, flat_spec, all_spec, log_spec = specs
    mixed_spec = flat_spec if upright else row_spec
    key_shape = jax.ShapeDtypeStruct(keys.shape, NARROW_TYPE)
    return pl.pallas_call(
        functools.partial(backward_body, *args, upright),
        grid=grid,
        in_specs=[
            count_spec, low_spec, log_spec, row_spec, mixed_spec, row_spec, all_spec, all_spec
        ],
        out_specs=[row_spec, all_spec, all_spec],
        out_shape=[jax.ShapeDtypeStruct(queries.shape, NARROW_TYPE), key_shape, key_shape],
        scratch_shapes=[pltpu.VMEM((keys.shape[0], group_cols), WIDE_TYPE)] * 2,
        compiler_params=pltpu.CompilerParams(vmem_limit_bytes=VMEM_BYTES),
        cost_estimate=pl.CostEstimate(
            flops=(1 if upright else 20) * flops,
            transcendentals=0 if upright else flops // 128,
            bytes_accessed=1 << 10 if upright else 1 << 20,
        ),
        name="attend_backward",
    )(counts, low, log_total, queries, mixed, out_grads, keys, values)


def stacked_body(parts, left, right, out):
    stacked = contract(left[...], right[...], 0, 0)
    cols = stacked.shape[1] // parts
    for part in range(parts):
        out[part] = stacked[:, part * cols : (part + 1) * cols]


def stacked_product(left, right, parts):
    rows, left_cols = left.shape
    right_cols = right.shape[1]
    block_cols = 256
    if rows > 1024:
        return transposed_times(left, right).reshape(left_cols, parts, right_cols // parts)
    return pl.pallas_call(
        functools.partial(stacked_body, parts),
        grid=(left_cols // block_cols,),
        in_specs=[
            pl.BlockSpec((rows, block_cols), lambda g: (0, g)),
            pl.BlockSpec((rows, right_cols), lambda g: (0, 0)),
        ],
        out_specs=pl.BlockSpec((parts, block_cols, right_cols // parts), lambda g: (0, g, 0)),
        out_shape=jax.ShapeDtypeStruct((parts, left_cols, right_cols // parts), WIDE_TYPE),
        compiler_params=pltpu.CompilerParams(vmem_limit_bytes=VMEM_BYTES),
        name="stacked_product",
    )(left, right).transpose(1, 0, 2)


def together(*values):
    return lax.optimization_barrier(values)


def in_blocks(function, rows, block_rows):
    if rows <= block_rows:
        return function(0)
    starts = jnp.arange(rows // block_rows, dtype=jnp.int32) * block_rows
    return lax.map(function, starts).reshape(rows, -1)


def on_device(
    stream,
    cotangent,
    boundary,
    counts,
    attend_gain,
    attend_input,
    attend_output,
    byte_gain,
    byte_up,
    byte_down,
    patch_gain,
    patch_input,
    patch_output,
    dense_gain,
    dense_up,
    dense_down,
):
    tok_rows, width = stream.shape
    head_cols = attend_input.shape[2]
    big_width = patch_input.shape[0]
    patch_cols = patch_input.shape[2]
    item_count = counts.shape[0]
    seq_devices = lax.axis_size("seq")
    device = lax.axis_index("seq")
    capacity = tok_rows // 4
    total_rows = seq_devices * capacity // 2
    owned_rows = total_rows // seq_devices
    item_cap = DEV_ITEM * capacity
    query_rows = min(256, tok_rows)

    per_device = counts.reshape(-1)
    ends = jnp.cumsum(per_device)
    offsets = ends - per_device
    item_begin = offsets.reshape(item_count, DEV_ITEM)[:, 0]
    my_first = offsets[device]
    rank_local = jnp.cumsum(boundary) - 1
    target = jnp.where(boundary == 1, rank_local, -1)
    send_map = narrow(jnp.arange(capacity)[:, None] == target[None, :])
    rank = jnp.arange(total_rows, dtype=jnp.int32)
    rank_device = jnp.sum(rank[:, None] >= ends[None, :], axis=1)
    rank_start = jnp.sum(
        jnp.where(rank_device[:, None] == jnp.arange(seq_devices)[None, :], offsets[None, :], 0),
        axis=1,
    )
    rank_slot = rank_device * capacity + rank - rank_start
    rank_low = jnp.max(
        jnp.where(rank[:, None] >= item_begin[None, :], item_begin[None, :], 0), axis=1
    )
    rank_low = rank_low[None, :].astype(jnp.int32)
    slot_rows = seq_devices * capacity

    def compact_rows(slots, first_row, block_rows):
        places = lax.dynamic_slice_in_dim(rank_slot, first_row, block_rows, 0)
        take_map = narrow(places[:, None] == jnp.arange(slot_rows)[None, :])
        return narrow(product(take_map, slots))

    def compact(slots):
        block_rows = min(1024, total_rows)
        return in_blocks(
            lambda first_row: compact_rows(slots, first_row, block_rows), total_rows, block_rows
        )

    def my_slots(table):
        padded = jnp.pad(table, ((0, capacity), (0, 0)))
        return lax.dynamic_slice_in_dim(padded, my_first, capacity, 0)

    def my_block(table):
        return lax.dynamic_slice_in_dim(table, device * owned_rows, owned_rows, 0)

    with jax.named_scope("byte_attend"):
        stream_value = wide(stream)
        normed = narrow(rms_scale(stream_value, attend_gain))
        in_matrix = attend_input.reshape(width, 3 * head_cols)
        projected = narrow(product(normed, in_matrix))
        queries = projected[:, :head_cols]
        key_value = projected[:, head_cols:]
        need_list = []
        while sum(need_list) < WIN:
            need_list.append(min(tok_rows, WIN - sum(need_list)))
        arrived_list = []
        for step, need_rows in enumerate(need_list):
            arrived_list.append(from_behind(key_value[tok_rows - need_rows :], "seq", step + 1))
        extended = jnp.concatenate(arrived_list[::-1] + [key_value], axis=0)
        delta_slots = narrow(product(send_map, cotangent))
        keys = extended[:, :head_cols]
        values = extended[:, head_cols:]
        window_low = jnp.maximum(
            jnp.arange(tok_rows, dtype=jnp.int32) + 1, WIN - device * tok_rows
        )[None, :]
        window_spans = (WIN + query_rows,)
        window_counts = jnp.zeros((tok_rows // query_rows,), jnp.int32)
        mixed_heads, window_log = attend_forward(
            window_counts, window_low, queries, keys, values, window_spans, query_rows, True
        )
        all_mixed, all_slots = two_gathers(mixed_heads, delta_slots, 0, 2)
        all_output = lax.all_gather(attend_output, "tensor", axis=0, tiled=True)
        after_attend = stream_value + transposed_times(all_mixed, all_output)

    with jax.named_scope("byte_feed"):
        normed_two = narrow(rms_scale(after_attend, byte_gain))
        gate_pre = product(normed_two, byte_up)
        activated = narrow(gelu_tanh(gate_pre))
        feed_part = narrow(product(activated, byte_down))

    with jax.named_scope("patch_rows"):
        attend_high = narrow(after_attend)
        attend_rest = narrow(after_attend - wide(attend_high))
        rows_sum = wide(tensor_sum(narrow(product(send_map, feed_part)), 1, 4))
        rows_here = narrow(
            product(send_map, attend_high) + product(send_map, attend_rest) + rows_sum
        )
        byte_rows = compact(seq_gather(rows_here, 2))

    with jax.named_scope("cotangent_rows"):
        delta_own = compact_rows(all_slots, device * owned_rows, owned_rows)

    wide_pad = ((0, 0), (0, big_width - width))
    with jax.named_scope("patch_attend"):
        normed_three = narrow(rms_scale(wide(jnp.pad(byte_rows, wide_pad)), patch_gain))
        patch_matrix = patch_input.reshape(big_width, 3 * patch_cols)
        patch_projected = narrow(product(normed_three, patch_matrix))
        patch_queries = patch_projected[:, :patch_cols]
        patch_keys = patch_projected[:, patch_cols : 2 * patch_cols]
        patch_values = patch_projected[:, 2 * patch_cols :]
        patch_query_rows = min(256, total_rows)
        most_blocks = min(total_rows, item_cap + patch_query_rows) // patch_query_rows
        patch_spans = tuple(patch_query_rows * (blocks + 1) for blocks in range(most_blocks))
        patch_counts = (
            jnp.arange(total_rows // patch_query_rows, dtype=jnp.int32)
            + 1
            - rank_low[0, ::patch_query_rows] // patch_query_rows
        )
        mixed_patch, patch_log = attend_forward(
            patch_counts,
            rank_low,
            patch_queries,
            patch_keys,
            patch_values,
            patch_spans,
            patch_query_rows,
            False,
        )
        branch_own = wide(tensor_sum(narrow(product(my_block(mixed_patch), patch_output)), 3, 4))

    with jax.named_scope("patch_dense"):
        own_rows = wide(jnp.pad(my_block(byte_rows), wide_pad))
        after_patch = own_rows + branch_own
        normed_four = narrow(rms_scale(after_patch, dense_gain))
        dense_pre = product(normed_four, dense_up)
        dense_pre_grad = narrow(gelu_back(dense_pre, times_transposed(delta_own, dense_down)))
        normed_four_grad = wide(tensor_sum(narrow(times_transposed(dense_pre_grad, dense_up)), 4, 4))
        after_patch_grad, densegain_grad = norm_back(after_patch, dense_gain, normed_four_grad)
        branch_grad_own = narrow(after_patch_grad + wide(jnp.pad(delta_own, wide_pad)))
        branch_grad, normed_later = together(seq_gather(branch_grad_own, 5), normed_four)
        all_normed = lax.all_gather(normed_later, "seq", axis=0, tiled=True)

    with jax.named_scope("patch_attend_back"):
        mixed_patch_grad = narrow(times_transposed(branch_grad, patch_output))
        patch_projected_grad = jnp.concatenate(
            attend_backward(
                patch_counts,
                rank_low,
                patch_log,
                patch_queries,
                mixed_patch,
                mixed_patch_grad,
                patch_keys,
                patch_values,
                patch_spans,
                patch_query_rows,
                False,
            ),
            axis=1,
        )
        normed_three_grad = times_transposed(my_slots(patch_projected_grad), patch_matrix)
        normed_three_grad = wide(tensor_sum(narrow(normed_three_grad), 6, 4))
        patch_norm_grad, patchgain_grad = norm_back(
            wide(jnp.pad(rows_here, wide_pad)), patch_gain, normed_three_grad
        )
        rows_grad = narrow(wide(my_slots(branch_grad[:, :width])) + patch_norm_grad[:, :width])

    with jax.named_scope("byte_feed_back"):
        feed_grad = narrow(
            jnp.where(
                boundary[:, None] == 1,
                transposed_times(send_map, rows_grad),
                wide(cotangent),
            )
        )
        activated_grad = times_transposed(feed_grad, byte_down)
        gate_grad = narrow(gelu_back(gate_pre, activated_grad))
        bytedown_grad = transposed_times(activated, feed_grad)
        byteup_grad = transposed_times(normed_two, gate_grad)
        feed_pack = narrow(jnp.concatenate([byteup_grad, bytedown_grad], axis=0))
        normed_two_part = narrow(times_transposed(gate_grad, byte_up))
        feed_pack, normed_two_part, all_normed = together(feed_pack, normed_two_part, all_normed)
        feed_part_sum = lax.psum_scatter(feed_pack, "seq", scatter_dimension=0, tiled=True)
        normed_two_grad = wide(tensor_sum(normed_two_part, 7, 4))
        feed_norm_grad, bytegain_grad = norm_back(after_attend, byte_gain, normed_two_grad)
        after_attend_grad = wide(feed_grad) + feed_norm_grad

    with jax.named_scope("byte_attend_back"):
        attend_branch_grad = narrow(after_attend_grad)
        attendoutput_grad = product(mixed_heads, attend_branch_grad)
        mixed_heads_grad = narrow(times_transposed(attend_branch_grad, attend_output))
        mixed_heads_grad, later_projected = together(mixed_heads_grad, patch_projected_grad)
        patchinput_grad = stacked_product(normed_three, later_projected, 3)
        query_grad, key_grad, value_grad = attend_backward(
            window_counts,
            window_low,
            window_log,
            queries,
            mixed_heads,
            mixed_heads_grad,
            keys,
            values,
            window_spans,
            query_rows,
            True,
        )
        pair_grad = jnp.concatenate([key_grad, value_grad], axis=1)
        pair_grad, patchinput_grad = together(pair_grad, patchinput_grad)
        query_grad, all_normed, later_slots, later_branch, feed_part_sum = together(
            query_grad, all_normed, all_slots, branch_grad, feed_part_sum
        )
        patchoutput_grad = transposed_times(mixed_patch, later_branch)
        begin_row = WIN
        returned_list = []
        for step, need_rows in enumerate(need_list):
            begin_row = begin_row - need_rows
            returned_list.append(
                from_behind(pair_grad[begin_row : begin_row + need_rows], "seq", -step - 1)
            )

    with jax.named_scope("dense_weights"):
        block_rows = min(1024, total_rows)

        delta_grad = compact(later_slots)

        def dense_parts(first_row):
            some_normed = lax.dynamic_slice_in_dim(all_normed, first_row, block_rows, 0)
            some_delta = lax.dynamic_slice_in_dim(delta_grad, first_row, block_rows, 0)
            some_pre = product(some_normed, dense_up)
            some_act = narrow(gelu_tanh(some_pre))
            some_grad = narrow(gelu_back(some_pre, times_transposed(some_delta, dense_down)))
            return some_normed, some_delta, some_act, some_grad

        if total_rows == block_rows:
            some_normed, some_delta, dense_act, dense_grad = dense_parts(0)
            densedown_grad = transposed_times(dense_act, some_delta)
            denseup_grad = transposed_times(some_normed, dense_grad)
        else:

            def dense_step(sums, first_row):
                some_normed, some_delta, some_act, some_grad = dense_parts(first_row)
                down_sum = sums[0] + transposed_times(some_act, some_delta)
                up_sum = sums[1] + transposed_times(some_normed, some_grad)
                return (down_sum, up_sum), some_act

            starts = jnp.arange(total_rows // block_rows, dtype=jnp.int32) * block_rows
            initial = (jnp.zeros(dense_down.shape), jnp.zeros(dense_up.shape))
            (densedown_grad, denseup_grad), dense_act = lax.scan(dense_step, initial, starts)
            dense_act = dense_act.reshape(total_rows, -1)

        returned_list, dense_act, densedown_grad, denseup_grad, patchoutput_grad = together(
            returned_list, dense_act, densedown_grad, denseup_grad, patchoutput_grad
        )

    with jax.named_scope("byte_attend_sum"):
        own_grad = wide(pair_grad[WIN:])
        for need_rows, returned in zip(need_list, returned_list):
            own_grad = own_grad.at[tok_rows - need_rows :].add(wide(returned))
        projected_grad = jnp.concatenate([query_grad, narrow(own_grad)], axis=1)
        attend_pack = narrow(
            jnp.concatenate([transposed_times(projected_grad, normed), attendoutput_grad], axis=0)
        )
        normed_part = narrow(times_transposed(projected_grad, in_matrix))
        attend_pack, normed_part = together(attend_pack, normed_part)
        pack_rows = width // seq_devices
        ring_fits = pack_rows % 32 == 0
        if ring_fits:
            normed_grad, attend_part = two_sums(normed_part, attend_pack, 8, 4)
        else:
            normed_grad = tensor_sum(normed_part, 8, 4)
            attend_part = lax.psum_scatter(attend_pack, "seq", scatter_dimension=0, tiled=True)
        normed_grad = wide(normed_grad)
        stream_norm_grad, attendgain_grad = norm_back(stream_value, attend_gain, normed_grad)
        inflow = narrow(after_attend_grad + stream_norm_grad)

    with jax.named_scope("result"):
        delta_part = product(my_slots(mixed_patch), patch_output[:, :width])
        delta_part = narrow(delta_part + product(my_slots(dense_act), dense_down))
        result_part = wide(feed_part) + transposed_times(send_map, delta_part)
        gains = jnp.concatenate([attendgain_grad, bytegain_grad, patchgain_grad, densegain_grad])
        gains = gains.reshape(-1, width)
        gain_rows = gains.shape[0]
        gains = narrow(jnp.pad(gains, ((0, 32 - gain_rows), (0, 0))))
        attend_block = jnp.concatenate([attend_part, gains], axis=0)
        result_part, feed_sum = together(
            narrow(result_part), lax.all_gather(feed_part_sum, "seq", axis=0, tiled=True)
        )
        if ring_fits:
            result_sum, attend_sum = sum_and_gather(result_part, attend_block, 9, 4)
        else:
            result_sum = tensor_sum(result_part, 9, 4)
            attend_sum = lax.all_gather(attend_block, "seq", axis=0, tiled=True)
        result = narrow(after_attend + wide(result_sum))

    with jax.named_scope("weight_sums"):
        feed_sum = wide(feed_sum)
        byteup_grad = feed_sum[:width]
        bytedown_grad = feed_sum[width:]
        attend_sum = wide(attend_sum).reshape(seq_devices, -1, width)
        gains = jnp.sum(attend_sum[:, pack_rows : pack_rows + gain_rows], axis=0).reshape(-1)
        attend_sum = attend_sum[:, :pack_rows].reshape(width, width)
        attendinput_grad = attend_sum[: 3 * head_cols].reshape(3, head_cols, width)
        attendinput_grad = attendinput_grad.transpose(2, 0, 1)
        attendoutput_grad = attend_sum[3 * head_cols :]
        attendgain_grad = gains[:width]
        bytegain_grad = gains[width : 2 * width]
        patchgain_grad = gains[2 * width : 2 * width + big_width]
        densegain_grad = gains[2 * width + big_width :]

    return (
        result,
        inflow,
        attendgain_grad,
        attendinput_grad,
        attendoutput_grad,
        bytegain_grad,
        byteup_grad,
        bytedown_grad,
        patchgain_grad,
        patchinput_grad,
        patchoutput_grad,
        densegain_grad,
        denseup_grad,
        densedown_grad,
    )


def solution(mesh):
    in_specs = (
        P("seq", None),
        P("seq", None),
        P("seq"),
        P(),
        P(),
        P(None, None, "tensor"),
        P("tensor", None),
        P(),
        P(None, "tensor"),
        P("tensor", None),
        P(),
        P(None, None, "tensor"),
        P("tensor", None),
        P(),
        P(None, "tensor"),
        P("tensor", None),
    )
    out_specs = (
        P("seq", None),
        P("seq", None),
        P(),
        P(None, None, "tensor"),
        P("tensor", None),
        P(),
        P(None, "tensor"),
        P("tensor", None),
        P(),
        P(None, None, "tensor"),
        P("tensor", None),
        P(),
        P(None, "tensor"),
        P("tensor", None),
    )
    return jax.shard_map(
        on_device, mesh=mesh, in_specs=in_specs, out_specs=out_specs, check_vma=False
    )
```

```python
import functools

import jax
import jax.numpy as jnp
from jax import lax
from jax.experimental import pallas as pl
from jax.experimental.pallas import tpu as pltpu
from jax.sharding import PartitionSpec as P

HD = 64
WIN = 1536
DEV_ITEM = 4

EPSILON = 1e-06
NEGATIVE = -1e30
SCORE_SCALE = HD ** (-0.5)
WIDE_TYPE = jnp.float32
NARROW_TYPE = jnp.bfloat16
VMEM_BYTES = 48 << 20
MESH = pl.DeviceIdType.MESH


def from_behind(value, axis, steps):
    count = lax.axis_size(axis)
    initial, last = (max(0, -steps), min(count, count - steps))
    return lax.ppermute(value, axis, [(source, source + steps) for source in range(initial, last)])


def rms_scale(values, scaling):
    return values * lax.rsqrt(jnp.mean(values * values, axis=-1, keepdims=True) + EPSILON) * scaling


def gelu_tanh(values):
    return jax.nn.gelu(values, approximate=True)


def norm_back(values, scaling, upstream):
    unused, pullback = jax.vjp(rms_scale, values, scaling)
    return pullback(upstream)


def gelu_back(values, upstream):
    unused, pullback = jax.vjp(gelu_tanh, values)
    return pullback(upstream)[0]


def contract(left_side, right_side, left_axis, right_axis):
    return lax.dot_general(
        left_side,
        right_side,
        (((left_axis,), (right_axis,)), ((), ())),
        preferred_element_type=WIDE_TYPE,
    )


def product(left_side, right_side):
    return contract(left_side, right_side, 1, 0)


def times_transposed(left_side, right_side):
    return contract(left_side, right_side, 1, 1)


def transposed_times(left_side, right_side):
    return contract(left_side, right_side, 0, 0)


def wide(values):
    return values.astype(WIDE_TYPE)


def narrow(values):
    return values.astype(NARROW_TYPE)


def meet(peers):
    barrier = pltpu.get_barrier_semaphore()
    for peer in peers:
        pl.semaphore_signal(barrier, inc=1, device_id=peer, device_id_type=MESH)
    pl.semaphore_wait(barrier, len(peers))


def tensor_peers():
    place = lax.axis_index("tensor")
    pair = place + 1 - 2 * (place % 2)
    across = (place + 2) % 4
    return place, pair, across


def remote(source, target, send_sem, recv_sem, peer):
    return pltpu.make_async_remote_copy(
        src_ref=source,
        dst_ref=target,
        send_sem=send_sem,
        recv_sem=recv_sem,
        device_id=peer,
        device_id_type=MESH,
    )


def seq_peers(count):
    device = lax.axis_index("seq")
    spot = ring_spot(device, count)
    ahead = {"seq": ring_at((spot + 1) % count, count)}
    behind = {"seq": ring_at((spot + count - 1) % count, count)}
    return device, spot, ahead, behind


def ring_at(spot, count):
    half = spot // (count // 2)
    return (1 - half) * 2 * spot + half * (2 * (count - 1 - spot) + 1)


def ring_spot(device, count):
    return device // 2 + (device % 2) * (count - 1 - 2 * (device // 2))


def run_stages(transfers, pattern):
    for index in pattern:
        next(transfers[index], None)
    for transfer in transfers:
        for unused in transfer:
            pass


def tensor_sum_stages(chunks, part, total, pair_got, mine, across_got, send_sem, recv_sem):
    place, pair, across = tensor_peers()
    pair_id = {"tensor": pair}
    across_id = {"tensor": across}
    rows = part.shape[0] // 2
    step = rows // chunks
    core = place % 2

    def piece(half, chunk):
        return pl.ds(pl.multiple_of(half * rows + chunk * step, 16), step)

    given = []
    for chunk in range(chunks):
        copy = remote(
            part.at[piece(1 - core, chunk)],
            pair_got.at[pl.ds(chunk * step, step)],
            send_sem.at[0, chunk],
            recv_sem.at[0, chunk],
            pair_id,
        )
        copy.start()
        given.append(copy)
    yield
    far = []
    for chunk in range(chunks):
        given[chunk].wait_recv()
        here = pl.ds(chunk * step, step)
        mine[here] = narrow(wide(part[piece(core, chunk)]) + wide(pair_got[here]))
        copy = remote(
            mine.at[here],
            across_got.at[here],
            send_sem.at[1, chunk],
            recv_sem.at[1, chunk],
            across_id,
        )
        copy.start()
        far.append(copy)
    yield
    back = []
    for chunk in range(chunks):
        far[chunk].wait_recv()
        here = pl.ds(chunk * step, step)
        own = piece(core, chunk)
        total[own] = narrow(wide(mine[here]) + wide(across_got[here]))
        copy = remote(
            total.at[own],
            total.at[own],
            send_sem.at[2, chunk],
            recv_sem.at[2, chunk],
            pair_id,
        )
        copy.start()
        back.append(copy)
        yield
    for copy in back:
        copy.wait_recv()
    for copy in given + far + back:
        copy.wait_send()


def tensor_gather_stages(chunks, block, out, local_sem, send_sem, recv_sem):
    place, pair, across = tensor_peers()
    pair_id = {"tensor": pair}
    across_id = {"tensor": across}
    rows = block.shape[0]
    step = rows // chunks

    def piece(owner, chunk):
        return pl.ds(pl.multiple_of(owner * rows + chunk * step, 16), step)

    copies = []
    for kind, peer in ((0, across_id), (1, pair_id)):
        for chunk in range(chunks):
            copy = remote(
                block.at[pl.ds(chunk * step, step)],
                out.at[piece(place, chunk)],
                send_sem.at[kind, chunk],
                recv_sem.at[kind, chunk],
                peer,
            )
            copy.start()
            copies.append(copy)
    local = pltpu.make_async_copy(block, out.at[pl.ds(pl.multiple_of(place * rows, 16), rows)], local_sem)
    local.start()
    yield
    passed = []
    for chunk in range(chunks):
        copies[chunk].wait_recv()
        copy = remote(
            out.at[piece(across, chunk)],
            out.at[piece(across, chunk)],
            send_sem.at[2, chunk],
            recv_sem.at[2, chunk],
            pair_id,
        )
        copy.start()
        passed.append(copy)
        yield
    local.wait()
    for chunk in range(chunks):
        copies[chunks + chunk].wait_recv()
        passed[chunk].wait_recv()
    for copy in copies + passed:
        copy.wait_send()


def ring_gather_stages(
    count, shared, block, out, local_sem, ring_send, ring_recv, pair_send, pair_recv
):
    device, spot, ahead, behind = seq_peers(count)
    place, pair, across = tensor_peers()
    pair_id = {"tensor": pair}
    rows = block.shape[0]
    step = rows // (4 if shared else 2)
    first = (place % 2) * 2 * step if shared else 0

    def piece(owner, sub):
        return pl.ds(pl.multiple_of(owner * rows + first + sub * step, 16), step)

    hops = count // 2
    sends = []
    moves = {}

    def owner_at(way, distance):
        if way == 0:
            return ring_at((spot + count - distance) % count, count)
        return ring_at((spot + distance) % count, count)

    def launch(way, hop, sub):
        owner = owner_at(way, hop - 1)
        if hop == 1:
            source = block.at[pl.ds(pl.multiple_of(first + sub * step, 16), step)]
        else:
            source = out.at[piece(owner, sub)]
        copy = remote(
            source,
            out.at[piece(owner, sub)],
            ring_send.at[way, hop - 1, sub],
            ring_recv.at[way, hop - 1, sub],
            (ahead, behind)[way],
        )
        copy.start()
        moves[way, hop, sub] = copy
        sends.append(copy)

    order = ((0, 0), (1, 1), (0, 1), (1, 0))
    for way, sub in order:
        launch(way, 1, sub)
    local = pltpu.make_async_copy(
        block, out.at[pl.ds(pl.multiple_of(device * rows, 16), rows)], local_sem
    )
    local.start()
    yield
    pairs = []
    for hop in range(1, hops + 1):
        for way, sub in order:
            if hop == hops and way != sub:
                continue
            moves[way, hop, sub].wait_recv()
            if hop + 1 < hops or (hop + 1 == hops and way == sub):
                launch(way, hop + 1, sub)
            if shared:
                owner = owner_at(way, hop)
                copy = remote(
                    out.at[piece(owner, sub)],
                    out.at[piece(owner, sub)],
                    pair_send.at[way, hop - 1, sub],
                    pair_recv.at[way, hop - 1, sub],
                    pair_id,
                )
                copy.start()
                pairs.append(copy)
        yield
    local.wait()
    for copy in pairs:
        copy.wait_recv()
    for copy in sends + pairs:
        copy.wait_send()


def ring_sum_stages(count, part, shard, arrived, send_sem, recv_sem):
    device, spot, ahead, behind = seq_peers(count)
    rows = part.shape[0] // count
    half = rows // 2
    moves = {}

    def piece(distance, way):
        owner = ring_at((spot + count - distance if way == 0 else spot + distance) % count, count)
        return pl.ds(pl.multiple_of(owner * rows + way * half, 16), half)

    def launch(way, step, source):
        copy = remote(
            source,
            arrived.at[way, step],
            send_sem.at[way, step],
            recv_sem.at[way, step],
            (ahead, behind)[way],
        )
        copy.start()
        moves[way, step] = copy

    for way in range(2):
        launch(way, 0, part.at[piece(1, way)])
    yield
    for step in range(count - 1):
        for way in range(2):
            moves[way, step].wait_recv()
            summed = wide(part[piece(step + 2, way)]) + wide(arrived[way, step])
            if step < count - 2:
                arrived[way, step] = narrow(summed)
                launch(way, step + 1, arrived.at[way, step])
            else:
                shard[pl.ds(way * half, half)] = narrow(summed)
        yield
    for copy in moves.values():
        copy.wait_send()


def meet_tensor(count):
    place, pair, across = tensor_peers()
    peers = [{"tensor": pair}, {"tensor": across}]
    if count:
        peers += seq_peers(count)[2:]
    meet(peers)


def tensor_sum_body(chunks, *refs):
    meet_tensor(0)
    run_stages([tensor_sum_stages(chunks, *refs)], ())


def seq_gather_body(count, *refs):
    device, spot, ahead, behind = seq_peers(count)
    place, pair, across = tensor_peers()
    meet((ahead, behind, {"tensor": pair}))
    run_stages([ring_gather_stages(count, True, *refs)], ())


def two_gathers_body(count, chunks, block, rows, out, all_rows, *refs):
    meet_tensor(count)
    run_stages(
        [
            ring_gather_stages(count, True, rows, all_rows, *refs[3:]),
            tensor_gather_stages(chunks, block, out, *refs[:3]),
        ],
        (0, 1, 0, 1, 1, 0),
    )


def two_sums_body(count, chunks, part, pack, total, shard, *refs):
    meet_tensor(count)
    run_stages(
        [
            tensor_sum_stages(chunks, part, total, *refs[:5]),
            ring_sum_stages(count, pack, shard, *refs[5:]),
        ],
        (0, 1, 0, 1, 0, 1, 0, 0, 1, 0, 1, 0, 0, 1, 0, 1, 0, 0),
    )


def sum_and_gather_body(count, chunks, part, block, total, out, *refs):
    meet_tensor(count)
    run_stages(
        [
            tensor_sum_stages(chunks, part, total, *refs[:5]),
            ring_gather_stages(count, False, block, out, *refs[5:], None, None),
        ],
        (0, 1, 0, 0, 1, 0, 0, 1, 0, 0, 1, 0, 0, 1, 0),
    )


DMA = pltpu.SemaphoreType.DMA


def sum_scratch(part, chunks):
    rows, cols = part.shape
    half = pltpu.VMEM((rows // 2, cols), NARROW_TYPE)
    return [half, half, half, DMA((3, chunks)), DMA((3, chunks))]


def ring_sems(count, sets):
    return [DMA(())] + [DMA((2, count // 2, 2))] * (2 * sets)


def exchange(body, name, collective_id, shapes, scratch, args):
    results = pl.pallas_call(
        body,
        in_specs=[pl.BlockSpec(memory_space=pltpu.VMEM)] * len(args),
        out_specs=[pl.BlockSpec(memory_space=pltpu.VMEM)] * len(shapes),
        out_shape=[jax.ShapeDtypeStruct(shape, NARROW_TYPE) for shape in shapes],
        scratch_shapes=scratch,
        compiler_params=pltpu.CompilerParams(
            collective_id=collective_id, has_side_effects=True, vmem_limit_bytes=VMEM_BYTES
        ),
        name=name,
    )(*args)
    return results[0] if len(shapes) == 1 else results


def tensor_sum(part, collective_id, chunks):
    body = functools.partial(tensor_sum_body, chunks)
    scratch = sum_scratch(part, chunks)
    return exchange(body, "tensor_sum", collective_id, [part.shape], scratch, [part])


def seq_gather(block, collective_id):
    rows, cols = block.shape
    count = lax.axis_size("seq")
    body = functools.partial(seq_gather_body, count)
    scratch = ring_sems(count, 2)
    return exchange(body, "seq_gather", collective_id, [(count * rows, cols)], scratch, [block])


def two_gathers(block, rows, collective_id, chunks):
    count = lax.axis_size("seq")
    shapes = [(4 * block.shape[0], block.shape[1]), (count * rows.shape[0], rows.shape[1])]
    scratch = [DMA(()), DMA((3, chunks)), DMA((3, chunks))] + ring_sems(count, 2)
    body = functools.partial(two_gathers_body, count, chunks)
    return exchange(body, "two_gathers", collective_id, shapes, scratch, [block, rows])


def two_sums(part, pack, collective_id, chunks):
    count = lax.axis_size("seq")
    rows, cols = pack.shape
    moves = count - 1
    scratch = sum_scratch(part, chunks) + [
        pltpu.VMEM((2, moves, rows // count // 2, cols), NARROW_TYPE),
        DMA((2, moves)),
        DMA((2, moves)),
    ]
    body = functools.partial(two_sums_body, count, chunks)
    shapes = [part.shape, (rows // count, cols)]
    return exchange(body, "two_sums", collective_id, shapes, scratch, [part, pack])


def sum_and_gather(part, block, collective_id, chunks):
    count = lax.axis_size("seq")
    shapes = [part.shape, (count * block.shape[0], block.shape[1])]
    scratch = sum_scratch(part, chunks) + ring_sems(count, 1)
    body = functools.partial(sum_and_gather_body, count, chunks)
    return exchange(body, "sum_and_gather", collective_id, shapes, scratch, [part, block])


def allowed_pairs(low_row, first_key, span, first_query, query_rows):
    key_pos = first_key + lax.broadcasted_iota(jnp.int32, (span, query_rows), 0)
    query_pos = first_query + lax.broadcasted_iota(jnp.int32, (span, query_rows), 1)
    return (key_pos >= low_row) & (key_pos <= query_pos)


def choose_span(counts, spans, query_rows, block, run):
    if len(spans) == 1:
        run(spans[0])
    else:
        count = counts[block]
        for span in spans:
            pl.when(count == span // query_rows)(functools.partial(run, span))


def forward_body(
    heads, query_rows, spans, offset, upright, counts, low, queries, keys, values, mixed, log_total
):
    block = pl.program_id(1)

    def run(span):
        start = pl.multiple_of(block * query_rows + query_rows + offset - span, 128)
        allowed = allowed_pairs(low[...], start, span, block * query_rows + offset, query_rows)
        rows = pl.ds(start, span)
        for head in range(heads):
            cols = slice(head * HD, (head + 1) * HD)
            scores = contract(keys[rows, cols], queries[:, cols] * SCORE_SCALE, 1, 1)
            scores = jnp.where(allowed, scores, NEGATIVE)
            top = jnp.max(scores, axis=0, keepdims=True)
            raised = jnp.exp(scores - top)
            total = jnp.sum(raised, axis=0, keepdims=True)
            mixed_head = contract(values[rows, cols], narrow(raised), 0, 0) * (1.0 / total)
            if upright:
                mixed[cols, :] = narrow(mixed_head)
            else:
                mixed[:, cols] = narrow(mixed_head.T)
            log_total[0, head : head + 1, :] = top + jnp.log(total)

    choose_span(counts, spans, query_rows, block, run)


def backward_body(
    heads,
    query_rows,
    spans,
    offset,
    upright,
    counts,
    low,
    log_total,
    queries,
    mixed,
    out_grads,
    keys,
    values,
    query_grads,
    key_grads,
    value_grads,
    key_sum,
    value_sum,
):
    block = pl.program_id(1)

    @pl.when(block == 0)
    def clear():
        key_sum[...] = jnp.zeros_like(key_sum)
        value_sum[...] = jnp.zeros_like(value_sum)

    def run(span):
        start = pl.multiple_of(block * query_rows + query_rows + offset - span, 128)
        allowed = allowed_pairs(low[...], start, span, block * query_rows + offset, query_rows)
        rows = pl.ds(start, span)
        for head in range(heads):
            cols = slice(head * HD, (head + 1) * HD)
            query = queries[:, cols] * SCORE_SCALE
            out_grad = out_grads[:, cols]
            if upright:
                overlap = wide(mixed[cols, :]) * wide(out_grad).T
            else:
                overlap = (wide(mixed[:, cols]) * wide(out_grad)).T
            inner = jnp.sum(overlap, axis=0, keepdims=True)
            key = keys[rows, cols]
            scores = contract(key, query, 1, 1)
            weights = jnp.where(allowed, jnp.exp(scores - log_total[0, head : head + 1, :]), 0.0)
            weight_grad = contract(values[rows, cols], out_grad, 1, 1)
            score_grad = narrow(weights * (weight_grad - inner))
            query_grads[:, cols] = narrow(contract(key, score_grad, 0, 0).T * SCORE_SCALE)
            key_sum[rows, cols] += contract(score_grad, query, 1, 0)
            value_sum[rows, cols] += contract(narrow(weights), out_grad, 1, 0)

    choose_span(counts, spans, query_rows, block, run)

    @pl.when(block == pl.num_programs(1) - 1)
    def finish():
        key_grads[...] = narrow(key_sum[...])
        value_grads[...] = narrow(value_sum[...])


def attend_sizes(queries, keys, spans, query_rows):
    rows, cols = queries.shape
    extent = keys.shape[0]
    group_cols = 128 if cols % 128 == 0 else cols
    groups = cols // group_cols
    heads = group_cols // HD
    count_spec = pl.BlockSpec(memory_space=pltpu.SMEM)
    low_spec = pl.BlockSpec((1, query_rows), lambda g, b: (0, b))
    row_spec = pl.BlockSpec((query_rows, group_cols), lambda g, b: (b, g))
    flat_spec = pl.BlockSpec((group_cols, query_rows), lambda g, b: (g, b))
    all_spec = pl.BlockSpec((extent, group_cols), lambda g, b: (0, g))
    log_spec = pl.BlockSpec((1, heads, query_rows), lambda g, b: (g, 0, b))
    args = (heads, query_rows, spans, extent - rows)
    log_shape = jax.ShapeDtypeStruct((groups, heads, rows), WIDE_TYPE)
    grid = (groups, rows // query_rows)
    flops = 2 * rows * spans[-1] * cols
    specs = (count_spec, low_spec, row_spec, flat_spec, all_spec, log_spec)
    return args, grid, specs, log_shape, group_cols, flops


def attend_forward(counts, low, queries, keys, values, spans, query_rows, upright):
    args, grid, specs, log_shape, unused, flops = attend_sizes(queries, keys, spans, query_rows)
    count_spec, low_spec, row_spec, flat_spec, all_spec, log_spec = specs
    mixed_shape = queries.shape[::-1] if upright else queries.shape
    return pl.pallas_call(
        functools.partial(forward_body, *args, upright),
        grid=grid,
        in_specs=[count_spec, low_spec, row_spec, all_spec, all_spec],
        out_specs=[flat_spec if upright else row_spec, log_spec],
        out_shape=[jax.ShapeDtypeStruct(mixed_shape, NARROW_TYPE), log_shape],
        compiler_params=pltpu.CompilerParams(vmem_limit_bytes=VMEM_BYTES),
        cost_estimate=pl.CostEstimate(
            flops=16 * flops, transcendentals=flops // 128, bytes_accessed=1 << 20
        ),
        name="attend_forward",
    )(counts, low, queries, keys, values)


def attend_backward(
    counts, low, log_total, queries, mixed, out_grads, keys, values, spans, query_rows, upright
):
    args, grid, specs, unused, group_cols, flops = attend_sizes(queries, keys, spans, query_rows)
    count_spec, low_spec, row_spec, flat_spec, all_spec, log_spec = specs
    mixed_spec = flat_spec if upright else row_spec
    key_shape = jax.ShapeDtypeStruct(keys.shape, NARROW_TYPE)
    return pl.pallas_call(
        functools.partial(backward_body, *args, upright),
        grid=grid,
        in_specs=[
            count_spec, low_spec, log_spec, row_spec, mixed_spec, row_spec, all_spec, all_spec
        ],
        out_specs=[row_spec, all_spec, all_spec],
        out_shape=[jax.ShapeDtypeStruct(queries.shape, NARROW_TYPE), key_shape, key_shape],
        scratch_shapes=[pltpu.VMEM((keys.shape[0], group_cols), WIDE_TYPE)] * 2,
        compiler_params=pltpu.CompilerParams(vmem_limit_bytes=VMEM_BYTES),
        cost_estimate=pl.CostEstimate(
            flops=(1 if upright else 20) * flops,
            transcendentals=0 if upright else flops // 128,
            bytes_accessed=1 << 10 if upright else 1 << 20,
        ),
        name="attend_backward",
    )(counts, low, log_total, queries, mixed, out_grads, keys, values)


def stacked_body(parts, left, right, out):
    stacked = contract(left[...], right[...], 0, 0)
    cols = stacked.shape[1] // parts
    for part in range(parts):
        out[part] = stacked[:, part * cols : (part + 1) * cols]


def stacked_product(left, right, parts):
    rows, left_cols = left.shape
    right_cols = right.shape[1]
    block_cols = 256
    if rows > 1024:
        return transposed_times(left, right).reshape(left_cols, parts, right_cols // parts)
    return pl.pallas_call(
        functools.partial(stacked_body, parts),
        grid=(left_cols // block_cols,),
        in_specs=[
            pl.BlockSpec((rows, block_cols), lambda g: (0, g)),
            pl.BlockSpec((rows, right_cols), lambda g: (0, 0)),
        ],
        out_specs=pl.BlockSpec((parts, block_cols, right_cols // parts), lambda g: (0, g, 0)),
        out_shape=jax.ShapeDtypeStruct((parts, left_cols, right_cols // parts), WIDE_TYPE),
        compiler_params=pltpu.CompilerParams(vmem_limit_bytes=VMEM_BYTES),
        name="stacked_product",
    )(left, right).transpose(1, 0, 2)


def together(*values):
    return lax.optimization_barrier(values)


def in_blocks(function, rows, block_rows):
    if rows <= block_rows:
        return function(0)
    starts = jnp.arange(rows // block_rows, dtype=jnp.int32) * block_rows
    return lax.map(function, starts).reshape(rows, -1)


def on_device(
    stream,
    cotangent,
    boundary,
    counts,
    attend_gain,
    attend_input,
    attend_output,
    byte_gain,
    byte_up,
    byte_down,
    patch_gain,
    patch_input,
    patch_output,
    dense_gain,
    dense_up,
    dense_down,
):
    tok_rows, width = stream.shape
    head_cols = attend_input.shape[2]
    big_width = patch_input.shape[0]
    patch_cols = patch_input.shape[2]
    item_count = counts.shape[0]
    seq_devices = lax.axis_size("seq")
    device = lax.axis_index("seq")
    capacity = tok_rows // 4
    total_rows = seq_devices * capacity // 2
    owned_rows = total_rows // seq_devices
    item_cap = DEV_ITEM * capacity
    query_rows = min(256, tok_rows)

    per_device = counts.reshape(-1)
    ends = jnp.cumsum(per_device)
    offsets = ends - per_device
    item_begin = offsets.reshape(item_count, DEV_ITEM)[:, 0]
    my_first = offsets[device]
    rank_local = jnp.cumsum(boundary) - 1
    target = jnp.where(boundary == 1, rank_local, -1)
    send_map = narrow(jnp.arange(capacity)[:, None] == target[None, :])
    rank = jnp.arange(total_rows, dtype=jnp.int32)
    rank_device = jnp.sum(rank[:, None] >= ends[None, :], axis=1)
    rank_start = jnp.sum(
        jnp.where(rank_device[:, None] == jnp.arange(seq_devices)[None, :], offsets[None, :], 0),
        axis=1,
    )
    rank_slot = rank_device * capacity + rank - rank_start
    rank_low = jnp.max(
        jnp.where(rank[:, None] >= item_begin[None, :], item_begin[None, :], 0), axis=1
    )
    rank_low = rank_low[None, :].astype(jnp.int32)
    slot_rows = seq_devices * capacity

    def compact_rows(slots, first_row, block_rows):
        places = lax.dynamic_slice_in_dim(rank_slot, first_row, block_rows, 0)
        take_map = narrow(places[:, None] == jnp.arange(slot_rows)[None, :])
        return narrow(product(take_map, slots))

    def compact(slots):
        block_rows = min(1024, total_rows)
        return in_blocks(
            lambda first_row: compact_rows(slots, first_row, block_rows), total_rows, block_rows
        )

    def my_slots(table):
        padded = jnp.pad(table, ((0, capacity), (0, 0)))
        return lax.dynamic_slice_in_dim(padded, my_first, capacity, 0)

    def my_block(table):
        return lax.dynamic_slice_in_dim(table, device * owned_rows, owned_rows, 0)

    with jax.named_scope("byte_attend"):
        stream_value = wide(stream)
        normed = narrow(rms_scale(stream_value, attend_gain))
        in_matrix = attend_input.reshape(width, 3 * head_cols)
        key_value = narrow(product(normed, in_matrix[:, head_cols:]))
        queries = narrow(product(normed, in_matrix[:, :head_cols]))
        need_list = []
        while sum(need_list) < WIN:
            need_list.append(min(tok_rows, WIN - sum(need_list)))
        arrived_list = []
        for step, need_rows in enumerate(need_list):
            arrived_list.append(from_behind(key_value[tok_rows - need_rows :], "seq", step + 1))
        extended = jnp.concatenate(arrived_list[::-1] + [key_value], axis=0)
        delta_slots = narrow(product(send_map, cotangent))
        keys = extended[:, :head_cols]
        values = extended[:, head_cols:]
        window_low = jnp.maximum(
            jnp.arange(tok_rows, dtype=jnp.int32) + 1, WIN - device * tok_rows
        )[None, :]
        window_spans = (WIN + query_rows,)
        window_counts = jnp.zeros((tok_rows // query_rows,), jnp.int32)
        mixed_heads, window_log = attend_forward(
            window_counts, window_low, queries, keys, values, window_spans, query_rows, True
        )
        all_mixed, all_slots = two_gathers(mixed_heads, delta_slots, 0, 2)
        all_output = lax.all_gather(attend_output, "tensor", axis=0, tiled=True)
        after_attend = stream_value + transposed_times(all_mixed, all_output)

    with jax.named_scope("byte_feed"):
        normed_two = narrow(rms_scale(after_attend, byte_gain))
        gate_pre = product(normed_two, byte_up)
        activated = narrow(gelu_tanh(gate_pre))
        feed_part = narrow(product(activated, byte_down))

    with jax.named_scope("patch_rows"):
        attend_high = narrow(after_attend)
        attend_rest = narrow(after_attend - wide(attend_high))
        rows_sum = wide(tensor_sum(narrow(product(send_map, feed_part)), 1, 4))
        rows_here = narrow(
            product(send_map, attend_high) + product(send_map, attend_rest) + rows_sum
        )
        byte_rows = compact(seq_gather(rows_here, 2))

    with jax.named_scope("cotangent_rows"):
        delta_own = compact_rows(all_slots, device * owned_rows, owned_rows)

    wide_pad = ((0, 0), (0, big_width - width))
    with jax.named_scope("patch_attend"):
        normed_three = narrow(rms_scale(wide(jnp.pad(byte_rows, wide_pad)), patch_gain))
        patch_matrix = patch_input.reshape(big_width, 3 * patch_cols)
        patch_projected = narrow(product(normed_three, patch_matrix))
        patch_queries = patch_projected[:, :patch_cols]
        patch_keys = patch_projected[:, patch_cols : 2 * patch_cols]
        patch_values = patch_projected[:, 2 * patch_cols :]
        patch_query_rows = min(256, total_rows)
        most_blocks = min(total_rows, item_cap + patch_query_rows) // patch_query_rows
        patch_spans = tuple(patch_query_rows * (blocks + 1) for blocks in range(most_blocks))
        patch_counts = (
            jnp.arange(total_rows // patch_query_rows, dtype=jnp.int32)
            + 1
            - rank_low[0, ::patch_query_rows] // patch_query_rows
        )
        mixed_patch, patch_log = attend_forward(
            patch_counts,
            rank_low,
            patch_queries,
            patch_keys,
            patch_values,
            patch_spans,
            patch_query_rows,
            False,
        )
        branch_own = wide(tensor_sum(narrow(product(my_block(mixed_patch), patch_output)), 3, 4))

    with jax.named_scope("patch_dense"):
        own_rows = wide(jnp.pad(my_block(byte_rows), wide_pad))
        after_patch = own_rows + branch_own
        normed_four = narrow(rms_scale(after_patch, dense_gain))
        dense_pre = product(normed_four, dense_up)
        dense_pre_grad = narrow(gelu_back(dense_pre, times_transposed(delta_own, dense_down)))
        normed_four_grad = wide(tensor_sum(narrow(times_transposed(dense_pre_grad, dense_up)), 4, 4))
        after_patch_grad, densegain_grad = norm_back(after_patch, dense_gain, normed_four_grad)
        branch_grad_own = narrow(after_patch_grad + wide(jnp.pad(delta_own, wide_pad)))
        branch_grad, normed_later = together(seq_gather(branch_grad_own, 5), normed_four)
        all_normed = lax.all_gather(normed_later, "seq", axis=0, tiled=True)

    with jax.named_scope("patch_attend_back"):
        mixed_patch_grad = narrow(times_transposed(branch_grad, patch_output))
        patch_projected_grad = jnp.concatenate(
            attend_backward(
                patch_counts,
                rank_low,
                patch_log,
                patch_queries,
                mixed_patch,
                mixed_patch_grad,
                patch_keys,
                patch_values,
                patch_spans,
                patch_query_rows,
                False,
            ),
            axis=1,
        )
        normed_three_grad = times_transposed(my_slots(patch_projected_grad), patch_matrix)
        normed_three_grad = wide(tensor_sum(narrow(normed_three_grad), 6, 4))
        patch_norm_grad, patchgain_grad = norm_back(
            wide(jnp.pad(rows_here, wide_pad)), patch_gain, normed_three_grad
        )
        rows_grad = narrow(wide(my_slots(branch_grad[:, :width])) + patch_norm_grad[:, :width])

    with jax.named_scope("byte_feed_back"):
        feed_grad = narrow(
            jnp.where(
                boundary[:, None] == 1,
                transposed_times(send_map, rows_grad),
                wide(cotangent),
            )
        )
        activated_grad = times_transposed(feed_grad, byte_down)
        gate_grad = narrow(gelu_back(gate_pre, activated_grad))
        bytedown_grad = transposed_times(activated, feed_grad)
        byteup_grad = transposed_times(normed_two, gate_grad)
        feed_pack = narrow(jnp.concatenate([byteup_grad, bytedown_grad], axis=0))
        normed_two_part = narrow(times_transposed(gate_grad, byte_up))
        feed_pack, normed_two_part, all_normed = together(feed_pack, normed_two_part, all_normed)
        feed_part_sum = lax.psum_scatter(feed_pack, "seq", scatter_dimension=0, tiled=True)
        normed_two_grad = wide(tensor_sum(normed_two_part, 7, 8))
        feed_norm_grad, bytegain_grad = norm_back(after_attend, byte_gain, normed_two_grad)
        after_attend_grad = wide(feed_grad) + feed_norm_grad

    with jax.named_scope("byte_attend_back"):
        attend_branch_grad = narrow(after_attend_grad)
        attendoutput_grad = product(mixed_heads, attend_branch_grad)
        mixed_heads_grad = narrow(times_transposed(attend_branch_grad, attend_output))
        mixed_heads_grad, later_projected = together(mixed_heads_grad, patch_projected_grad)
        patchinput_grad = stacked_product(normed_three, later_projected, 3)
        query_grad, key_grad, value_grad = attend_backward(
            window_counts,
            window_low,
            window_log,
            queries,
            mixed_heads,
            mixed_heads_grad,
            keys,
            values,
            window_spans,
            query_rows,
            True,
        )
        pair_grad = jnp.concatenate([key_grad, value_grad], axis=1)
        pair_grad, patchinput_grad = together(pair_grad, patchinput_grad)
        query_grad, all_normed, later_slots, later_branch, feed_part_sum = together(
            query_grad, all_normed, all_slots, branch_grad, feed_part_sum
        )
        patchoutput_grad = transposed_times(mixed_patch, later_branch)
        begin_row = WIN
        returned_list = []
        for step, need_rows in enumerate(need_list):
            begin_row = begin_row - need_rows
            returned_list.append(
                from_behind(pair_grad[begin_row : begin_row + need_rows], "seq", -step - 1)
            )

    with jax.named_scope("dense_weights"):
        block_rows = min(1024, total_rows)

        delta_grad = compact(later_slots)

        def dense_parts(first_row):
            some_normed = lax.dynamic_slice_in_dim(all_normed, first_row, block_rows, 0)
            some_delta = lax.dynamic_slice_in_dim(delta_grad, first_row, block_rows, 0)
            some_pre = product(some_normed, dense_up)
            some_act = narrow(gelu_tanh(some_pre))
            some_grad = narrow(gelu_back(some_pre, times_transposed(some_delta, dense_down)))
            return some_normed, some_delta, some_act, some_grad

        if total_rows == block_rows:
            some_normed, some_delta, dense_act, dense_grad = dense_parts(0)
            densedown_grad = transposed_times(dense_act, some_delta)
            denseup_grad = transposed_times(some_normed, dense_grad)
        else:

            def dense_step(sums, first_row):
                some_normed, some_delta, some_act, some_grad = dense_parts(first_row)
                down_sum = sums[0] + transposed_times(some_act, some_delta)
                up_sum = sums[1] + transposed_times(some_normed, some_grad)
                return (down_sum, up_sum), some_act

            starts = jnp.arange(total_rows // block_rows, dtype=jnp.int32) * block_rows
            initial = (jnp.zeros(dense_down.shape), jnp.zeros(dense_up.shape))
            (densedown_grad, denseup_grad), dense_act = lax.scan(dense_step, initial, starts)
            dense_act = dense_act.reshape(total_rows, -1)

        returned_list, dense_act, densedown_grad, denseup_grad, patchoutput_grad = together(
            returned_list, dense_act, densedown_grad, denseup_grad, patchoutput_grad
        )

    with jax.named_scope("byte_attend_sum"):
        own_grad = wide(pair_grad[WIN:])
        for need_rows, returned in zip(need_list, returned_list):
            own_grad = own_grad.at[tok_rows - need_rows :].add(wide(returned))
        projected_grad = jnp.concatenate([query_grad, narrow(own_grad)], axis=1)
        attend_pack = narrow(
            jnp.concatenate([transposed_times(projected_grad, normed), attendoutput_grad], axis=0)
        )
        normed_part = narrow(times_transposed(projected_grad, in_matrix))
        attend_pack, normed_part = together(attend_pack, normed_part)
        pack_rows = width // seq_devices
        ring_fits = pack_rows % 32 == 0
        if ring_fits:
            normed_grad, attend_part = two_sums(normed_part, attend_pack, 8, 8)
        else:
            normed_grad = tensor_sum(normed_part, 8, 4)
            attend_part = lax.psum_scatter(attend_pack, "seq", scatter_dimension=0, tiled=True)
        normed_grad = wide(normed_grad)
        stream_norm_grad, attendgain_grad = norm_back(stream_value, attend_gain, normed_grad)
        inflow = narrow(after_attend_grad + stream_norm_grad)

    with jax.named_scope("result"):
        delta_part = product(my_slots(mixed_patch), patch_output[:, :width])
        delta_part = narrow(delta_part + product(my_slots(dense_act), dense_down))
        result_part = wide(feed_part) + transposed_times(send_map, delta_part)
        gains = jnp.concatenate([attendgain_grad, bytegain_grad, patchgain_grad, densegain_grad])
        gains = gains.reshape(-1, width)
        gain_rows = gains.shape[0]
        gains = narrow(jnp.pad(gains, ((0, 32 - gain_rows), (0, 0))))
        attend_block = jnp.concatenate([attend_part, gains], axis=0)
        result_part, feed_sum = together(
            narrow(result_part), lax.all_gather(feed_part_sum, "seq", axis=0, tiled=True)
        )
        if ring_fits:
            result_sum, attend_sum = sum_and_gather(result_part, attend_block, 9, 8)
        else:
            result_sum = tensor_sum(result_part, 9, 4)
            attend_sum = lax.all_gather(attend_block, "seq", axis=0, tiled=True)
        result = narrow(after_attend + wide(result_sum))

    with jax.named_scope("weight_sums"):
        feed_sum = wide(feed_sum)
        byteup_grad = feed_sum[:width]
        bytedown_grad = feed_sum[width:]
        attend_sum = wide(attend_sum).reshape(seq_devices, -1, width)
        gains = jnp.sum(attend_sum[:, pack_rows : pack_rows + gain_rows], axis=0).reshape(-1)
        attend_sum = attend_sum[:, :pack_rows].reshape(width, width)
        attendinput_grad = attend_sum[: 3 * head_cols].reshape(3, head_cols, width)
        attendinput_grad = attendinput_grad.transpose(2, 0, 1)
        attendoutput_grad = attend_sum[3 * head_cols :]
        attendgain_grad = gains[:width]
        bytegain_grad = gains[width : 2 * width]
        patchgain_grad = gains[2 * width : 2 * width + big_width]
        densegain_grad = gains[2 * width + big_width :]

    return (
        result,
        inflow,
        attendgain_grad,
        attendinput_grad,
        attendoutput_grad,
        bytegain_grad,
        byteup_grad,
        bytedown_grad,
        patchgain_grad,
        patchinput_grad,
        patchoutput_grad,
        densegain_grad,
        denseup_grad,
        densedown_grad,
    )


def solution(mesh):
    in_specs = (
        P("seq", None),
        P("seq", None),
        P("seq"),
        P(),
        P(),
        P(None, None, "tensor"),
        P("tensor", None),
        P(),
        P(None, "tensor"),
        P("tensor", None),
        P(),
        P(None, None, "tensor"),
        P("tensor", None),
        P(),
        P(None, "tensor"),
        P("tensor", None),
    )
    out_specs = (
        P("seq", None),
        P("seq", None),
        P(),
        P(None, None, "tensor"),
        P("tensor", None),
        P(),
        P(None, "tensor"),
        P("tensor", None),
        P(),
        P(None, None, "tensor"),
        P("tensor", None),
        P(),
        P(None, "tensor"),
        P("tensor", None),
    )
    return jax.shard_map(
        on_device, mesh=mesh, in_specs=in_specs, out_specs=out_specs, check_vma=False
    )
```
